512 devices in a mesh: wave: 16 (over z_hi, y, core), tm: 32 (over z_lo, x).
Axes of the slice: x: 4, y: 4, z: 16 (z_hi: 2, z_lo: 8; z = z_hi * 8 + z_lo), core: 2. Of those that a mesh axis runs over, the one named last changes fastest.
Arguments:
- field: float32 [4, 128, 2, 2, 32768], P(None, 'wave', None, None, 'tm'), may hold values from -3 to 3
- lit_count: int32 [4], replicated, may hold values from 32 to 128
- route_fibre: int32 [4, 64], replicated, may hold values from 0 to 3, as said below
- route_slot: int32 [4, 64], replicated, may hold values from 0 to 63, as said below
- dispersion: float32 [2, 4], replicated, may hold values from 20 to 42
- nonlinearity: float32 [2, 4], replicated, may hold values from 0.25 to 2.5
Outputs:
- received: float32 [4, 128, 2, 2, 32768], P(None, 'wave', None, None, 'tm')
The draws below stay inside these ranges and needn't reach their ends.
Inputs may be any that keep to these rules, and one draw needn't show every extreme that they name: `route_fibre`: together with route_slot it names every block of every fibre exactly once. `route_slot`: blocks 4 g .. 4 g + 3 of all fibres form channel group g. Of the 16 blocks of one group, at most 2 land in any one group, and every draw has pairs of groups with exactly 2.
All inputs are finite; a program needn't handle non-finite values.
Results may differ from the reference program's by a relative error of at most 0.0003.
Values sent between devices are 32-bit elements; how exact they have to be, the bound alone decides.
A program may use at most 64 MiB of HBM per device.

```python
import math
import jax
import jax.numpy as jnp
from jax import lax

CH = 128
FIB = 4
BLK = 2
HALF = 2
NFFT = 2048
MARGIN = 512
VALID = 1024
TIME = 32768
NBLK = 64
WAVES = 16
GROUP_BLOCKS = 4
SENDS = 16
SLOTS = 2


def roadm_plan(key):
    base_key = jax.random.fold_in(key, 41)
    key_full, key_offset, key_order, key_place = jax.random.split(base_key, 4)
    half_slots = SLOTS // 2
    full_groups = jax.random.randint(key_full, (), 1, SENDS // SLOTS + 1)
    position = jnp.arange(SENDS)
    group_index = jnp.where(position < full_groups * SLOTS, position // SLOTS, full_groups + (position - full_groups * SLOTS) // half_slots)
    offsets = jax.random.permutation(key_offset, WAVES)
    target = (jnp.arange(WAVES)[:, None] + offsets[group_index][None, :]) % WAVES
    orders = jax.vmap(lambda subkey: jax.random.permutation(subkey, SENDS))(jax.random.split(key_order, WAVES))
    places = jax.vmap(lambda subkey: jax.random.permutation(subkey, SENDS))(jax.random.split(key_place, WAVES))
    target_flat = target.reshape(-1)
    serial = jnp.arange(WAVES * SENDS)
    earlier = (target_flat[None, :] == target_flat[:, None]) & (serial[None, :] < serial[:, None])
    arrival = jnp.sum(earlier.astype(jnp.int32), axis=1)
    landing = places[target_flat, arrival]
    source = orders.reshape(-1)
    source_group = serial // SENDS
    src_fibre = source // GROUP_BLOCKS
    src_block = source_group * GROUP_BLOCKS + source % GROUP_BLOCKS
    dst_fibre = (landing // GROUP_BLOCKS).astype(jnp.int32)
    dst_block = (target_flat * GROUP_BLOCKS + landing % GROUP_BLOCKS).astype(jnp.int32)
    fibre_map = jnp.zeros((FIB, NBLK), jnp.int32).at[src_fibre, src_block].set(dst_fibre)
    block_map = jnp.zeros((FIB, NBLK), jnp.int32).at[src_fibre, src_block].set(dst_block)
    return (fibre_map, block_map)


def draw_route_fibre(key, part):
    return roadm_plan(key)[0]


def draw_route_slot(key, part):
    return roadm_plan(key)[1]


def plant(entries, own_key, low, high):
    longest = entries.shape.index(max(entries.shape))
    spots = []
    for shift in (0, 1):
        where = [jax.random.randint(jax.random.fold_in(own_key, axis), (), 0, length) for axis, length in enumerate(entries.shape)]
        where[longest] = (where[longest] + shift) % entries.shape[longest]
        spots.append(tuple(where))
    return entries.at[spots[0]].set(low).at[spots[1]].set(high)


def levels(key, shape, cuts, least, top_value):
    loudness, own = 1.0, jax.random.fold_in(key, 6)
    for axis_at, blocks in cuts:
        steps = jnp.exp(jax.random.uniform(jax.random.fold_in(own, axis_at), (blocks,), jnp.float32, least / len(cuts), top_value / len(cuts)))
        loudness = loudness * jnp.repeat(steps, shape[axis_at] // blocks).reshape([-1 if axis == axis_at else 1 for axis in range(len(shape))])
    return loudness


def normal_values(stream_key, extent, scale, most, cuts=(), dtype=jnp.bfloat16):
    values = scale * jax.random.normal(stream_key, extent, jnp.float32)
    if cuts:
        values = values * levels(stream_key, extent, cuts, -0.22, 0.18)
    return jnp.clip(values, -most, most).astype(dtype)


def setup_inputs(seed: int = 0) -> dict:
    seeds = jax.random.split(jax.random.key(seed), 7)
    field = normal_values(seeds[0], (FIB, CH, 2, 2, TIME), 0.5, 3.0, ((1, 16), (4, 32)), jnp.float32)
    lit_count = plant(jax.random.randint(seeds[1], (FIB,), CH // 4, CH + 1), jax.random.fold_in(seeds[1], 1), CH // 4, CH).astype(jnp.int32)
    route_fibre = draw_route_fibre(jax.random.fold_in(seeds[6], 71), 0)
    route_slot = draw_route_slot(jax.random.fold_in(seeds[6], 71), 0)
    dispersion = jnp.clip(jax.random.uniform(seeds[4], (2, FIB), jnp.float32, 20.0, 42.0), 20.0, 42.0)
    nonlinearity = jnp.clip(jnp.exp(jax.random.uniform(seeds[5], (2, FIB), jnp.float32, math.log(0.25), math.log(2.5))), 0.25, 2.5)
    return dict(field=field, lit_count=lit_count, route_fibre=route_fibre, route_slot=route_slot, dispersion=dispersion, nonlinearity=nonlinearity)


def frequency_grid():
    index = jnp.arange(NFFT)
    signed = jnp.where(index < NFFT // 2, index, index - NFFT).astype(jnp.float32)
    return signed * (2.0 * jnp.pi / NFFT)


def fibre_step(arrays):
    waveform, spread, strength = arrays
    padded = jnp.concatenate([waveform[..., -MARGIN:], waveform, waveform[..., :MARGIN]], axis=-1)
    pieces = padded.reshape(CH, 2, 2, TIME // VALID + 1, VALID)
    blocks = jnp.concatenate([pieces[..., :-1, :], pieces[..., 1:, :]], axis=-1)
    complex_in = blocks[:, :, 0] + 1j * blocks[:, :, 1]
    spectrum = jnp.fft.fft(complex_in, axis=-1)
    omega = frequency_grid()
    channel = jnp.arange(CH).astype(jnp.float32)
    offsets = (jnp.pi / 2.0) * (2.0 * channel + 1.0 - CH) / CH
    theta = spread * (omega[None, :] ** 2 + 2.0 * omega[None, :] * offsets[:, None])
    spectrum = spectrum * jnp.exp(1j * theta)[:, None, None, :]
    inverse = jnp.fft.ifft(spectrum, axis=-1)[..., MARGIN:MARGIN + VALID].reshape(CH, 2, TIME)
    real_part = inverse.real
    imag_part = inverse.imag
    power = jnp.sum(real_part * real_part + imag_part * imag_part, axis=1)
    fibre_total = jnp.sum(power, axis=0)
    phase = strength * (2.0 * fibre_total[None, :] - power) / CH
    cosine = jnp.cos(phase)[:, None, :]
    sine = jnp.sin(phase)[:, None, :]
    return jnp.stack([real_part * cosine - imag_part * sine, real_part * sine + imag_part * cosine], axis=2)


def switch(waveform, route_fibre, route_slot):
    blocks = waveform.reshape(FIB * NBLK, BLK, 2, 2, TIME)
    target = (route_fibre * NBLK + route_slot).reshape(-1)
    moved = jnp.zeros_like(blocks).at[target].set(blocks)
    return moved.reshape(FIB, CH, 2, 2, TIME)


def reference(field, lit_count, route_fibre, route_slot, dispersion, nonlinearity):
    channel = jnp.arange(CH)
    lit_mask = channel[None, :] < lit_count[:, None]
    waveform = jnp.where(lit_mask[:, :, None, None, None], field, jnp.zeros_like(field))
    for span_index in range(2):
        if span_index == 1:
            waveform = switch(waveform, route_fibre, route_slot)
        for step_index in range(HALF):
            waveform = lax.map(fibre_step, (waveform, dispersion[span_index], nonlinearity[span_index]))
    return waveform
```

```python
import functools
import math

import jax
import jax.numpy as jnp
import numpy as np
from jax import lax
from jax.experimental import pallas as pl
from jax.experimental.pallas import tpu as pltpu
from jax.sharding import PartitionSpec as P

CH = 128
FIB = 4
LOC = 8
SEQ = 64
WAVE = 16
TM = 32
MESH = pl.DeviceIdType.MESH
F32 = jnp.float32
BF16 = jnp.bfloat16


def split_table(table):
    high = table.astype(jnp.bfloat16)
    low = (table - high.astype(np.float64)).astype(jnp.bfloat16)
    return high, low


def tables():
    eye = np.eye(8)
    r16 = np.arange(16)
    angle = 2.0 * np.pi * np.outer(r16, r16) / 16.0
    cos_a, sin_a = np.cos(angle), np.sin(angle)
    fwd = np.zeros((2, 16, 16, 2))
    fwd[0, :, :, 0], fwd[0, :, :, 1] = cos_a, sin_a
    fwd[1, :, :, 0], fwd[1, :, :, 1] = -sin_a, cos_a
    row_fwd = np.einsum("xrap,st->xsrtap", fwd, eye).reshape(256, 256)
    keep = np.zeros((8, 2, 2, 16))
    kc, ks = cos_a[4:12] / 2048.0, sin_a[4:12] / 2048.0
    keep[:, 0, 0], keep[:, 0, 1] = kc, -ks
    keep[:, 1, 0], keep[:, 1, 1] = ks, kc
    row_inv = np.einsum("apxr,st->sapxtr", keep, eye).reshape(128, 256)
    b = np.arange(128)
    angle = 2.0 * np.pi * (np.outer(b, b) % 128) / 128.0
    cos_b, sin_b = np.cos(angle), np.sin(angle)
    col_fwd = np.block([[cos_b, -sin_b], [sin_b, cos_b]])
    col_inv = np.block([[cos_b, sin_b], [-sin_b, cos_b]])
    twist = 2.0 * np.pi * np.outer(r16, b) / 2048.0
    out = []
    for table in (row_fwd, col_fwd, col_inv, row_inv):
        out.extend(split_table(table))
    out.append(np.cos(twist).astype(np.float32))
    out.append(np.sin(twist).astype(np.float32))
    return out


def fit(function, terms):
    nodes = np.cos(np.pi * (np.arange(400) + 0.5) / 400) * (np.pi * 1.02)
    square = nodes * nodes
    basis = np.stack([square**k for k in range(terms)], axis=1)
    return [float(v) for v in np.linalg.lstsq(basis, function(nodes), rcond=None)[0]]


SIN_POLY = fit(lambda x: np.sinc(x / np.pi), 8)
COS_POLY = fit(np.cos, 8)
TWO_PI = 2.0 * math.pi
PI_A = float(np.float32(6.28125))
PI_B = float(np.float32(np.round((TWO_PI - PI_A) * 2.0**24) / 2.0**24))
PI_B = float(np.floor((TWO_PI - PI_A) * 2.0**20) / 2.0**20)
PI_C = float(TWO_PI - PI_A - PI_B)


def sin_cos(angle):
    turns = jnp.floor(angle * (1.0 / TWO_PI) + 0.5)
    rest = ((angle - turns * PI_A) - turns * PI_B) - turns * PI_C
    square = rest * rest
    sine = jnp.full_like(square, SIN_POLY[-1])
    for value in SIN_POLY[-2::-1]:
        sine = sine * square + value
    cosine = jnp.full_like(square, COS_POLY[-1])
    for value in COS_POLY[-2::-1]:
        cosine = cosine * square + value
    return sine * rest, cosine


def split(x):
    high = x.astype(BF16)
    low = (x - high.astype(F32)).astype(BF16)
    return high, low


def dot(a, b):
    return jnp.dot(a, b, preferred_element_type=F32)


def left_product(table, data):
    high, low = split(data)
    return dot(table[0][...], high) + (dot(table[1][...], high) + dot(table[0][...], low))


def right_product(data, table):
    high, low = split(data)
    return dot(high, table[0][...]) + (dot(low, table[0][...]) + dot(high, table[1][...]))


def tiles(x):
    return x.reshape(-1, 8, 128)


def even_rows(shape):
    return lax.rem(lax.broadcasted_iota(jnp.int32, shape, len(shape) - 2), 2) == 0


def swap(x):
    t = tiles(x)
    even = even_rows(t.shape)
    return jnp.where(even, pltpu.roll(t, 7, 1), pltpu.roll(t, 1, 1)).reshape(x.shape)


def unpack_pair(x):
    t = tiles(x)
    even = even_rows(t.shape)
    first = jnp.where(even, t, pltpu.roll(t, 1, 1)).reshape(x.shape)
    second = jnp.where(even, pltpu.roll(t, 7, 1), t).reshape(x.shape)
    return first, second


def rotate(u, total, gain):
    square = u * u
    both = square[:, 0] + square[:, 1]
    power = both + swap(both)
    phase = gain * (2.0 * total[None] - power)
    sine, cosine = sin_cos(phase)
    signed = jnp.where(even_rows(sine.shape), -sine, sine)
    return u * cosine[:, None] + swap(u) * signed[:, None]


def disperse(u, t, filt_cos, filt_sin):
    rows = u.reshape(512, 128)
    x = jnp.concatenate([rows[:256], rows[256:]], axis=1)
    y = left_product(t["row_fwd"], x)
    tc = jnp.broadcast_to(t["twist_cos"][...][None], (8, 16, 128)).reshape(128, 128)
    ts = jnp.broadcast_to(t["twist_sin"][...][None], (8, 16, 128)).reshape(128, 128)
    halves = []
    for h in range(2):
        re = y[:128, h * 128 : (h + 1) * 128]
        im = y[128:, h * 128 : (h + 1) * 128]
        halves.append(jnp.concatenate([re * tc + im * ts, im * tc - re * ts], axis=1))
    spectrum = right_product(jnp.concatenate(halves, axis=0), t["col_fwd"])
    sr, si = spectrum[:, :128], spectrum[:, 128:]
    fc = jnp.broadcast_to(filt_cos[:, None], (8, 2, 16, 128)).reshape(256, 128)
    fs = jnp.broadcast_to(filt_sin[:, None], (8, 2, 16, 128)).reshape(256, 128)
    shaped = jnp.concatenate([sr * fc - si * fs, sr * fs + si * fc], axis=1)
    back = right_product(shaped, t["col_inv"])
    br, bi = back[:, :128], back[:, 128:]
    parts = []
    for h in range(2):
        re, im = br[h * 128 : (h + 1) * 128], bi[h * 128 : (h + 1) * 128]
        parts.append(jnp.concatenate([re * tc - im * ts, re * ts + im * tc], axis=0))
    out = left_product(t["row_inv"], jnp.concatenate(parts, axis=1))
    return jnp.concatenate([out[:, :128], out[:, 128:]], axis=0).reshape(16, 16, 128)


def kernel(
    lit, disp, nonlin, slot_item, take, take_fibre, field,
    rfh, rfl, cfh, cfl, cih, cil, rih, ril, twc, tws,
    out,
    filt_c, filt_s, halo, own, psum, pack, near, far, half_sum, total, q_side, q_ext,
    send_items, recv_items,
    halo_ss, halo_rs, near_ss, near_rs, far_ss, far_rs, side_ss, side_rs, item_ss, item_rs,
):
    t = dict(
        row_fwd=(rfh, rfl), col_fwd=(cfh, cfl), col_inv=(cih, cil), row_inv=(rih, ril),
        twist_cos=twc, twist_sin=tws,
    )
    me = lax.axis_index("wave")
    at = lax.axis_index("tm")
    my_z = me // 8
    my_y = lax.rem(me // 2, 4)
    my_core = lax.rem(me, 2)
    right = lax.rem(at + 1, TM)
    left = lax.rem(at + TM - 1, TM)

    def mate(k):
        kz, ky, kc = k // 8, (k // 2) % 4, k % 2
        return lax.rem(my_z + kz, 2) * 8 + lax.rem(my_y + ky, 4) * 2 + lax.rem(my_core + kc, 2)

    q_right = (lax.rem(me + 8 * (at // (TM - 1)), WAVE), right)
    q_left = (lax.rem(me + 8 * ((TM - 1 - at) // (TM - 1)), WAVE), left)
    d_right, d_left = (me, right), (me, left)

    barrier = pltpu.get_barrier_semaphore()
    for k in range(1, 16):
        pl.semaphore_signal(barrier, inc=1, device_id=(mate(k), at), device_id_type=MESH)
    for target in (d_right, d_left, q_right, q_left):
        pl.semaphore_signal(barrier, inc=1, device_id=target, device_id_type=MESH)

    r_i = lax.broadcasted_iota(jnp.int32, (16, 128), 0)
    m_i = lax.broadcasted_iota(jnp.int32, (16, 128), 1)
    k_i = r_i + 16 * m_i
    omega = jnp.where(k_i < 1024, k_i, k_i - 2048).astype(F32) * (2.0 * math.pi / 2048.0)

    def fill(i, carry):
        channel = (me * LOC + lax.rem(i, LOC)).astype(F32)
        offset = (math.pi / 2.0) * (2.0 * channel + 1.0 - CH) / CH
        for span in range(2):
            theta = disp[span, i // LOC] * (omega * omega + 2.0 * omega * offset)
            sine, cosine = sin_cos(theta)
            filt_s[span, i] = sine
            filt_c[span, i] = cosine
        return carry

    lax.fori_loop(0, FIB * LOC, fill, 0)
    pl.semaphore_wait(barrier, 19)

    def halo_copy(e, side, f, src):
        rows = pl.ds(8, 8) if side == 0 else pl.ds(0, 8)
        return pltpu.make_async_remote_copy(
            src_ref=src.at[pl.ds(f * 16, 16), rows],
            dst_ref=halo.at[e, side, pl.ds(f * 16, 16)],
            send_sem=halo_ss.at[e, side, f],
            recv_sem=halo_rs.at[e, side, f],
            device_id=d_right if side == 0 else d_left,
            device_id_type=MESH,
        )

    def own_of(e):
        return field if e == 0 else own.at[e - 1]

    def near_copy(e, k):
        return pltpu.make_async_remote_copy(
            src_ref=pack.at[e], dst_ref=near.at[e, k], send_sem=near_ss.at[e, k],
            recv_sem=near_rs.at[e, k], device_id=(mate(k), at), device_id_type=MESH,
        )

    def far_copy(e):
        return pltpu.make_async_remote_copy(
            src_ref=half_sum.at[e], dst_ref=far.at[e], send_sem=far_ss.at[e],
            recv_sem=far_rs.at[e], device_id=(mate(8), at), device_id_type=MESH,
        )

    def side_copy(e, side):
        rows = pl.ds(8, 8) if side == 0 else pl.ds(0, 8)
        return pltpu.make_async_remote_copy(
            src_ref=total.at[e, :, rows], dst_ref=q_side.at[e, side], send_sem=side_ss.at[e, side],
            recv_sem=side_rs.at[e, side], device_id=q_right if side == 0 else q_left,
            device_id_type=MESH,
        )

    def item_copy(k):
        return pltpu.make_async_remote_copy(
            src_ref=send_items.at[pl.ds(2 * k, 2)], dst_ref=recv_items.at[pl.ds(2 * k, 2)],
            send_sem=item_ss.at[k], recv_sem=item_rs.at[k], device_id=(mate(k), at),
            device_id_type=MESH,
        )

    def run_step(e, send_halo):
        span = e // 2
        source = own_of(e)

        def body(f, carry):
            halo_copy(e, 0, f, source).wait_recv()
            halo_copy(e, 1, f, source).wait_recv()
            group = pl.ds(f * 16, 16)
            u = jnp.concatenate([halo[e, 0, group], source[group], halo[e, 1, group]], axis=1)
            if e == 0:
                channel = me * LOC + lax.broadcasted_iota(jnp.int32, u.shape, 0) // 2
                u = jnp.where(channel < lit[f], u, 0.0)
            if e in (1, 3):
                u = rotate(
                    u.reshape(8, 2, 32, 128), q_ext[f], nonlin[span, f] * (1.0 / CH)
                ).reshape(16, 32, 128)
            table = pl.ds(f * LOC, LOC)
            result = disperse(u, t, filt_c[span, table], filt_s[span, table])
            own[e, group] = result
            if send_halo:
                halo_copy(e + 1, 0, f, own.at[e]).start()
                halo_copy(e + 1, 1, f, own.at[e]).start()
            both = jnp.sum(result * result, axis=0)
            psum[f] = both + swap(both)
            return carry

        lax.fori_loop(0, FIB, body, 0)
        even = even_rows((16, 128))
        for j in range(2):
            pack[e, j] = jnp.where(even, psum[2 * j], psum[2 * j + 1])
        for k in range(1, 8):
            near_copy(e, k).start()

    def finish_near(e):
        acc = pack[e]
        for k in range(1, 8):
            near_copy(e, k).wait_recv()
            acc = acc + near[e, k]
        half_sum[e] = acc
        far_copy(e).start()

    def finish_far(e, sides):
        far_copy(e).wait_recv()
        total[e] = half_sum[e] + far[e]
        if sides:
            side_copy(e, 0).start()
            side_copy(e, 1).start()
        for j in range(2):
            first, second = unpack_pair(total[e, j])
            q_ext[2 * j, 8:24] = first
            q_ext[2 * j + 1, 8:24] = second
        if sides:
            for side, rows in ((0, pl.ds(0, 8)), (1, pl.ds(24, 8))):
                side_copy(e, side).wait_recv()
                for j in range(2):
                    first, second = unpack_pair(q_side[e, side, j])
                    q_ext[2 * j, rows] = first
                    q_ext[2 * j + 1, rows] = second

    def start_halo(e, f, carry):
        halo_copy(e, 0, f, own_of(e)).start()
        halo_copy(e, 1, f, own_of(e)).start()
        return carry

    lax.fori_loop(0, FIB, functools.partial(start_halo, 0), 0)
    run_step(0, True)
    finish_near(0)
    finish_far(0, True)
    run_step(1, False)

    def gather(s, carry):
        send_items[s] = own[1, pl.ds(slot_item[s] * 4, 4)]
        return carry

    lax.fori_loop(0, 2 * WAVE, gather, 0)
    item_copy(8).start()
    finish_near(1)
    for k in (9, 10, 11, 12, 13, 14, 15, 1, 2, 3, 4, 5, 6, 7):
        item_copy(k).start()
    recv_items[0:2] = send_items[0:2]
    finish_far(1, False)
    for k in range(1, 16):
        item_copy(k).wait_recv()

    def place(i, carry):
        fibre = take_fibre[i]
        u = recv_items[take[i]].reshape(2, 2, 16, 128)
        u = rotate(u, q_ext[fibre, 8:24], nonlin[0, fibre] * (1.0 / CH))
        own[1, pl.ds(i * 4, 4)] = u.reshape(4, 16, 128)
        return carry

    def place_fibre(f, carry):
        lax.fori_loop(f * 4, f * 4 + 4, place, 0)
        return start_halo(2, f, carry)

    lax.fori_loop(0, FIB, place_fibre, 0)

    run_step(2, True)
    finish_near(2)
    finish_far(2, True)
    run_step(3, False)
    finish_near(3)
    finish_far(3, False)

    def last(f, carry):
        group = pl.ds(f * 16, 16)
        u = own[3, group].reshape(8, 2, 16, 128)
        u = rotate(u, q_ext[f, 8:24], nonlin[1, f] * (1.0 / CH))
        out[group] = u.reshape(16, 16, 128)
        return carry

    lax.fori_loop(0, FIB, last, 0)

    def drain_halo(f, carry):
        for e in range(4):
            halo_copy(e, 0, f, own_of(e)).wait_send()
            halo_copy(e, 1, f, own_of(e)).wait_send()
        return carry

    lax.fori_loop(0, FIB, drain_halo, 0)
    for e in range(4):
        for k in range(1, 8):
            near_copy(e, k).wait_send()
        far_copy(e).wait_send()
    for e in (0, 2):
        side_copy(e, 0).wait_send()
        side_copy(e, 1).wait_send()
    for k in range(1, 16):
        item_copy(k).wait_send()


def switch_tables(route_fibre, route_slot):
    me = lax.axis_index("wave")
    groups, blocks = WAVE, 4
    sends = FIB * blocks
    slot_all = route_slot.reshape(FIB, groups, blocks).transpose(1, 0, 2).reshape(groups, sends)
    fibre_all = route_fibre.reshape(FIB, groups, blocks).transpose(1, 0, 2).reshape(groups, sends)
    target_all = slot_all // blocks
    landing_all = fibre_all * blocks + slot_all % blocks
    position = jnp.arange(sends)
    earlier = (target_all[:, :, None] == target_all[:, None, :]) & (
        position[None, None, :] < position[None, :, None]
    )
    arrival_all = jnp.sum(earlier.astype(jnp.int32), axis=2)
    group = jnp.arange(groups)

    def offset(a, b):
        return (
            (a // 8 - b // 8) % 2 * 8
            + ((a // 2) % 4 - (b // 2) % 4) % 4 * 2
            + (a % 2 - b % 2) % 2
        )

    mine_from = (group == me)[:, None]
    my_target = jnp.sum(jnp.where(mine_from, target_all, 0), axis=0)
    my_arrival = jnp.sum(jnp.where(mine_from, arrival_all, 0), axis=0)
    slot_index = offset(my_target, me) * 2 + my_arrival
    matches = slot_index[None, :] == jnp.arange(2 * groups)[:, None]
    slot_item = jnp.sum(jnp.where(matches, position[None, :], 0), axis=1)
    receive = offset(me, group)[:, None] * 2 + arrival_all
    hits = (target_all == me)[:, :, None] & (landing_all[:, :, None] == position[None, None, :])
    take = jnp.sum(jnp.where(hits, receive[:, :, None], 0), axis=(0, 1))
    source_fibre = (position // blocks)[None, :, None]
    take_fibre = jnp.sum(jnp.where(hits, source_fibre, 0), axis=(0, 1))
    return slot_item.astype(jnp.int32), take.astype(jnp.int32), take_fibre.astype(jnp.int32)


def local(field, lit_count, route_fibre, route_slot, dispersion, nonlinearity):
    rows = field.reshape(FIB, LOC, 2, 2, 8, 128).transpose(0, 1, 2, 4, 3, 5).reshape(SEQ, 16, 128)
    slot_item, take, take_fibre = switch_tables(route_fibre, route_slot)
    constants = [jnp.asarray(v) for v in tables()]
    smem = pl.BlockSpec(memory_space=pltpu.SMEM)
    vmem = pl.BlockSpec(memory_space=pltpu.VMEM)
    dma = pltpu.SemaphoreType.DMA
    result = pl.pallas_call(
        kernel,
        out_shape=jax.ShapeDtypeStruct((SEQ, 16, 128), F32),
        in_specs=[smem] * 6 + [vmem] * 11,
        out_specs=vmem,
        scratch_shapes=[
            pltpu.VMEM((2, FIB * LOC, 16, 128), F32),
            pltpu.VMEM((2, FIB * LOC, 16, 128), F32),
            pltpu.VMEM((4, 2, SEQ, 8, 128), F32),
            pltpu.VMEM((4, SEQ, 16, 128), F32),
            pltpu.VMEM((FIB, 16, 128), F32),
            pltpu.VMEM((4, 2, 16, 128), F32),
            pltpu.VMEM((4, 8, 2, 16, 128), F32),
            pltpu.VMEM((4, 2, 16, 128), F32),
            pltpu.VMEM((4, 2, 16, 128), F32),
            pltpu.VMEM((4, 2, 16, 128), F32),
            pltpu.VMEM((4, 2, 2, 8, 128), F32),
            pltpu.VMEM((FIB, 32, 128), F32),
            pltpu.VMEM((2 * WAVE, 4, 16, 128), F32),
            pltpu.VMEM((2 * WAVE, 4, 16, 128), F32),
            dma((4, 2, FIB)), dma((4, 2, FIB)),
            dma((4, 8)), dma((4, 8)),
            dma((4,)), dma((4,)),
            dma((4, 2)), dma((4, 2)),
            dma((WAVE,)), dma((WAVE,)),
        ],
        compiler_params=pltpu.CompilerParams(
            collective_id=0, has_side_effects=True, vmem_limit_bytes=40 * 1024 * 1024
        ),
        name="propagate",
    )(lit_count, dispersion, nonlinearity, slot_item, take, take_fibre, rows, *constants)
    back = result.reshape(FIB, LOC, 2, 8, 2, 128).transpose(0, 1, 2, 4, 3, 5)
    return back.reshape(FIB, LOC, 2, 2, 1024)


def solution(mesh):
    return jax.shard_map(
        local,
        mesh=mesh,
        in_specs=(P(None, "wave", None, None, "tm"), P(), P(), P(), P(), P()),
        out_specs=P(None, "wave", None, None, "tm"),
        check_vma=False,
    )
```

```python
import functools
import math

import jax
import jax.numpy as jnp
import numpy as np
from jax import lax
from jax.experimental import pallas as pl
from jax.experimental.pallas import tpu as pltpu
from jax.sharding import PartitionSpec as P

CH = 128
FIB = 4
LOC = 8
SEQ = 64
WAVE = 16
TM = 32
MESH = pl.DeviceIdType.MESH
F32 = jnp.float32
BF16 = jnp.bfloat16


def split_table(table):
    high = table.astype(jnp.bfloat16)
    low = (table - high.astype(np.float64)).astype(jnp.bfloat16)
    return high, low


def tables():
    eye = np.eye(8)
    r16 = np.arange(16)
    angle = 2.0 * np.pi * np.outer(r16, r16) / 16.0
    cos_a, sin_a = np.cos(angle), np.sin(angle)
    fwd = np.zeros((2, 16, 16, 2))
    fwd[0, :, :, 0], fwd[0, :, :, 1] = cos_a, sin_a
    fwd[1, :, :, 0], fwd[1, :, :, 1] = -sin_a, cos_a
    native = fwd.reshape(2, 16, 32)
    apart = np.concatenate(
        [
            fwd[:, :, lo:hi].transpose(0, 1, 3, 2).reshape(2, 16, -1)
            for lo, hi in ((0, 4), (4, 12), (12, 16))
        ],
        axis=2,
    )
    fwd_native, fwd_apart = (
        np.einsum("xrq,st->xsrtq", v, eye).reshape(256, 256) for v in (native, apart)
    )
    keep = np.zeros((8, 2, 2, 16))
    kc, ks = cos_a[4:12] / 2048.0, sin_a[4:12] / 2048.0
    keep[:, 0, 0], keep[:, 0, 1] = kc, -ks
    keep[:, 1, 0], keep[:, 1, 1] = ks, kc
    inv_native = np.einsum("apxr,st->sapxtr", keep, eye).reshape(128, 256)
    inv_apart = np.einsum("apxr,st->spaxtr", keep, eye).reshape(128, 256)
    b = np.arange(128)
    angle = 2.0 * np.pi * (np.outer(b, b) % 128) / 128.0
    cos_b, sin_b = np.cos(angle), np.sin(angle)
    col_fwd = np.block([[cos_b, -sin_b], [sin_b, cos_b]])
    col_inv = np.block([[cos_b, sin_b], [-sin_b, cos_b]])
    twist = 2.0 * np.pi * np.outer(r16, b) / 2048.0
    wide = []
    for table in (fwd_native, fwd_apart, col_fwd, col_inv):
        wide.extend(split_table(table))
    for table in (inv_native, inv_apart):
        wide.append(np.concatenate(split_table(table), axis=0))
    twist = np.stack([np.cos(twist), np.sin(twist)]).astype(np.float32)
    return jnp.asarray(np.stack(wide)), jnp.asarray(twist)


def fit(function, terms):
    nodes = np.cos(np.pi * (np.arange(400) + 0.5) / 400) * (np.pi * 1.02)
    square = nodes * nodes
    basis = np.stack([square**k for k in range(terms)], axis=1)
    return [float(v) for v in np.linalg.lstsq(basis, function(nodes), rcond=None)[0]]


SIN_POLY = fit(lambda x: np.sinc(x / np.pi), 7)
COS_POLY = fit(np.cos, 7)
TWO_PI = 2.0 * math.pi
PI_A = float(np.float32(6.28125))
PI_B = float(np.float32(np.round((TWO_PI - PI_A) * 2.0**24) / 2.0**24))
PI_B = float(np.floor((TWO_PI - PI_A) * 2.0**20) / 2.0**20)
PI_C = float(TWO_PI - PI_A - PI_B)


def sin_cos(angle):
    turns = jnp.floor(angle * (1.0 / TWO_PI) + 0.5)
    rest = ((angle - turns * PI_A) - turns * PI_B) - turns * PI_C
    square = rest * rest
    sine = jnp.full_like(square, SIN_POLY[-1])
    for value in SIN_POLY[-2::-1]:
        sine = sine * square + value
    cosine = jnp.full_like(square, COS_POLY[-1])
    for value in COS_POLY[-2::-1]:
        cosine = cosine * square + value
    return sine * rest, cosine


def split(x):
    high = x.astype(BF16)
    low = (x - high.astype(F32)).astype(BF16)
    return high, low


def dot(a, b):
    return jnp.dot(a, b, preferred_element_type=F32)


def left_product(table, data):
    high, low = split(data)
    return dot(table[0][...], high) + (dot(table[1][...], high) + dot(table[0][...], low))


def right_product(data, table):
    high, low = split(data)
    return dot(high, table[0][...]) + (dot(low, table[0][...]) + dot(high, table[1][...]))


def low_rows():
    return lax.broadcasted_iota(jnp.int32, (8, 128), 0) < 4


def even_rows():
    return lax.rem(lax.broadcasted_iota(jnp.int32, (8, 128), 0), 2) == 0


def turn(x, shift):
    return pltpu.roll(x.reshape(-1, 8, 128), shift, 1).reshape(x.shape)


def swap(x):
    t = x.reshape(-1, 8, 128)
    return jnp.where(even_rows()[None], pltpu.roll(t, 7, 1), pltpu.roll(t, 1, 1)).reshape(x.shape)


def unpack_pair(x):
    t = x.reshape(-1, 8, 128)
    even = even_rows()[None]
    first = jnp.where(even, t, pltpu.roll(t, 1, 1)).reshape(x.shape)
    second = jnp.where(even, pltpu.roll(t, 7, 1), t).reshape(x.shape)
    return first, second


def rotate_native(u, total, gain):
    square = u * u
    both = square[:, 0] + square[:, 1]
    phase = gain * (2.0 * total[None] - (both + swap(both)))
    sine, cosine = sin_cos(phase)
    t = sine.reshape(-1, 8, 128)
    signed = jnp.where(even_rows()[None], -t, t).reshape(sine.shape)
    return u * cosine[:, None] + swap(u) * signed[:, None]


def rotate_apart(u, total, gain):
    re, im = u[:, :, :8], u[:, :, 8:]
    square = re * re + im * im
    phase = gain * (2.0 * total[None] - (square[:, 0] + square[:, 1]))
    sine, cosine = sin_cos(phase)
    sine, cosine = sine[:, None], cosine[:, None]
    return jnp.concatenate([re * cosine - im * sine, re * sine + im * cosine], axis=2)


def rotate_edge(u, total, gain):
    square = u * u
    both = square[:, 0] + square[:, 1]
    phase = gain * (2.0 * total[None] - (both + turn(both, 4)))
    sine, cosine = sin_cos(phase)
    signed = jnp.where(low_rows()[None], -sine, sine)
    return u * cosine[:, None] + turn(u, 4) * signed[:, None]


def edges(u):
    re, im = u[..., :8, :], u[..., 8:, :]
    low = low_rows()
    return jnp.where(low, turn(re, 4), im), jnp.where(low, re, turn(im, 4))


def disperse(u, t, fwd, inv, filt_cos, filt_sin):
    rows = u.reshape(512, 128)
    x = jnp.concatenate([rows[:256], rows[256:]], axis=1)
    y = left_product(t[fwd], x)
    tc = jnp.broadcast_to(t["twist_cos"][...][None], (8, 16, 128)).reshape(128, 128)
    ts = jnp.broadcast_to(t["twist_sin"][...][None], (8, 16, 128)).reshape(128, 128)
    halves = []
    for h in range(2):
        re = y[:128, h * 128 : (h + 1) * 128]
        im = y[128:, h * 128 : (h + 1) * 128]
        halves.append(jnp.concatenate([re * tc + im * ts, im * tc - re * ts], axis=1))
    spectrum = right_product(jnp.concatenate(halves, axis=0), t["col_fwd"])
    sr, si = spectrum[:, :128], spectrum[:, 128:]
    fc = jnp.broadcast_to(filt_cos[:, None], (8, 2, 16, 128)).reshape(256, 128)
    fs = jnp.broadcast_to(filt_sin[:, None], (8, 2, 16, 128)).reshape(256, 128)
    shaped = jnp.concatenate([sr * fc - si * fs, sr * fs + si * fc], axis=1)
    back = right_product(shaped, t["col_inv"])
    br, bi = back[:, :128], back[:, 128:]
    parts = []
    for h in range(2):
        re, im = br[h * 128 : (h + 1) * 128], bi[h * 128 : (h + 1) * 128]
        parts.append(jnp.concatenate([re * tc - im * ts, re * ts + im * tc], axis=0))
    out = left_product(t[inv], jnp.concatenate(parts, axis=1))
    return jnp.concatenate([out[:, :128], out[:, 128:]], axis=0).reshape(16, 16, 128)


def kernel(
    lit, disp, nonlin, fibre_hbm, slot_hbm, field_hbm, wide_hbm, twist_hbm,
    out_hbm,
    wide, twist, route_f, route_s, launch, result_buf,
    filt_c, filt_s, halo, own, edge, pack, near, far, half_sum, total, q_side,
    send_items, recv_items, slot_item, take, take_fibre,
    load_s, out_s,
    halo_ss, halo_rs, near_ss, near_rs, far_ss, far_rs, side_ss, side_rs, item_ss, item_rs,
):
    t = dict(
        fwd_native=(wide.at[0], wide.at[1]), fwd_apart=(wide.at[2], wide.at[3]),
        col_fwd=(wide.at[4], wide.at[5]), col_inv=(wide.at[6], wide.at[7]),
        inv_native=(wide.at[8, pl.ds(0, 128)], wide.at[8, pl.ds(128, 128)]),
        inv_apart=(wide.at[9, pl.ds(0, 128)], wide.at[9, pl.ds(128, 128)]),
        twist_cos=twist.at[0], twist_sin=twist.at[1],
    )
    me = lax.axis_index("wave")
    at = lax.axis_index("tm")
    my_z = me // 8
    my_y = lax.rem(me // 2, 4)
    my_core = lax.rem(me, 2)
    right = lax.rem(at + 1, TM)
    left = lax.rem(at + TM - 1, TM)

    def mate(k):
        kz, ky, kc = k // 8, (k // 2) % 4, k % 2
        return lax.rem(my_z + kz, 2) * 8 + lax.rem(my_y + ky, 4) * 2 + lax.rem(my_core + kc, 2)

    q_right = (lax.rem(me + 8 * (at // (TM - 1)), WAVE), right)
    q_left = (lax.rem(me + 8 * ((TM - 1 - at) // (TM - 1)), WAVE), left)
    d_right, d_left = (me, right), (me, left)

    barrier = pltpu.get_barrier_semaphore()
    for k in range(1, 16):
        pl.semaphore_signal(barrier, inc=1, device_id=(mate(k), at), device_id_type=MESH)
    for target in (d_right, d_left, q_right, q_left):
        pl.semaphore_signal(barrier, inc=1, device_id=target, device_id_type=MESH)
    loads = [
        pltpu.make_async_copy(src, dst, load_s.at[i])
        for i, (src, dst) in enumerate(
            ((field_hbm, launch), (wide_hbm, wide), (twist_hbm, twist), (fibre_hbm, route_f), (slot_hbm, route_s))
        )
    ]
    for load in loads:
        load.start()

    r_i = lax.broadcasted_iota(jnp.int32, (16, 128), 0)
    m_i = lax.broadcasted_iota(jnp.int32, (16, 128), 1)
    k_i = r_i + 16 * m_i
    omega = jnp.where(k_i < 1024, k_i, k_i - 2048).astype(F32) * (2.0 * math.pi / 2048.0)

    def fill_tables(span):
        def fill(i, carry):
            channel = (me * LOC + lax.rem(i, LOC)).astype(F32)
            offset = (math.pi / 2.0) * (2.0 * channel + 1.0 - CH) / CH
            theta = disp[span, i // LOC] * (omega * omega + 2.0 * omega * offset)
            sine, cosine = sin_cos(theta)
            filt_s[span, i] = sine
            filt_c[span, i] = cosine
            return carry

        lax.fori_loop(0, FIB * LOC, fill, 0)

    def plan_switch():
        fibre_of = lax.broadcasted_iota(jnp.int32, (FIB, 64), 0)
        block_of = lax.broadcasted_iota(jnp.int32, (FIB, 64), 1)
        group_of = block_of // 4
        slot = route_s[...]
        target = slot // 4
        landing = route_f[...] * 4 + slot % 4
        key = landing * 16 + fibre_of * 4 + block_of % 4
        mine = group_of == me
        for k in range(16):
            here = mine & (target == mate(k))
            low = jnp.min(jnp.where(here, key, 4095))
            high = jnp.max(jnp.where(here, key, 0))
            slot_item[2 * k] = lax.rem(low, 16)
            slot_item[2 * k + 1] = lax.rem(high, 16)
        code = group_of * 4 + fibre_of
        groups = []
        for i in range(16):
            value = jnp.sum(jnp.where((target == me) & (landing == i), code, 0))
            group = lax.rem(value // 4, WAVE)
            before = jnp.int32(0)
            for other in groups:
                before = before + jnp.where(other == group, 1, 0)
            groups.append(group)
            kz = lax.rem(my_z - group // 8 + 2, 2)
            ky = lax.rem(my_y - lax.rem(group // 2, 4) + 4, 4)
            kc = lax.rem(my_core - lax.rem(group, 2) + 2, 2)
            take[i] = (kz * 8 + ky * 2 + kc) * 2 + jnp.minimum(before, 1)
            take_fibre[i] = lax.rem(value, 4)

    fill_tables(0)
    for load in loads:
        load.wait()
    pl.semaphore_wait(barrier, 19)

    def halo_copy(e, side, f):
        group = pl.ds(f * 16, 16)
        if e == 0:
            src = launch.at[group, pl.ds(8, 8) if side == 0 else pl.ds(0, 8)]
        else:
            src = edge.at[e - 1, side, group]
        return pltpu.make_async_remote_copy(
            src_ref=src,
            dst_ref=halo.at[e, side, group],
            send_sem=halo_ss.at[e, side, f],
            recv_sem=halo_rs.at[e, side, f],
            device_id=d_right if side == 0 else d_left,
            device_id_type=MESH,
        )

    def near_copy(e, k):
        return pltpu.make_async_remote_copy(
            src_ref=pack.at[e], dst_ref=near.at[e, k], send_sem=near_ss.at[e, k],
            recv_sem=near_rs.at[e, k], device_id=(mate(k), at), device_id_type=MESH,
        )

    def far_copy(e):
        return pltpu.make_async_remote_copy(
            src_ref=half_sum.at[e], dst_ref=far.at[e], send_sem=far_ss.at[e],
            recv_sem=far_rs.at[e], device_id=(mate(8), at), device_id_type=MESH,
        )

    def side_copy(e, side):
        return pltpu.make_async_remote_copy(
            src_ref=total.at[e], dst_ref=q_side.at[e, side], send_sem=side_ss.at[e, side],
            recv_sem=side_rs.at[e, side], device_id=q_right if side == 0 else q_left,
            device_id_type=MESH,
        )

    def item_copy(k):
        return pltpu.make_async_remote_copy(
            src_ref=send_items.at[pl.ds(2 * k, 2)], dst_ref=recv_items.at[pl.ds(2 * k, 2)],
            send_sem=item_ss.at[k], recv_sem=item_rs.at[k], device_id=(mate(k), at),
            device_id_type=MESH,
        )

    def keep_edges(e, f, u):
        group = pl.ds(f * 16, 16)
        edge[e, 0, group], edge[e, 1, group] = edges(u)
        halo_copy(e + 1, 0, f).start()
        halo_copy(e + 1, 1, f).start()

    def run_step(e, send_halo):
        span = e // 2

        def body(f, carry):
            halo_copy(e, 0, f).wait_recv()
            halo_copy(e, 1, f).wait_recv()
            group = pl.ds(f * 16, 16)
            parts = [halo[e, 0, group], launch[group] if e == 0 else own[e - 1, group], halo[e, 1, group]]
            if e in (1, 3):
                gain = nonlin[span, f] * (1.0 / CH)
                low = low_rows()
                before, after = q_side[e - 1, 0, f], q_side[e - 1, 1, f]
                sums = (
                    jnp.where(low, turn(before, 4), before),
                    total[e - 1, f],
                    jnp.where(low, after, turn(after, 4)),
                )
                turns = (rotate_edge, rotate_apart, rotate_edge)
                parts = [
                    rule(part.reshape(8, 2, *part.shape[1:]), q, gain).reshape(part.shape)
                    for rule, part, q in zip(turns, parts, sums)
                ]
            u = jnp.concatenate(parts, axis=1)
            if e == 0:
                channel = me * LOC + lax.broadcasted_iota(jnp.int32, (16, 1, 128), 0) // 2
                u = jnp.where(channel < lit[f], u, 0.0)
            table = pl.ds(f * LOC, LOC)
            result = disperse(
                u, t, "fwd_native" if e == 0 else "fwd_apart", "inv_native" if e == 3 else "inv_apart",
                filt_c[span, table], filt_s[span, table],
            )
            own[e, group] = result
            if send_halo:
                keep_edges(e, f, result)
            both = jnp.sum(result * result, axis=0)
            if e < 3:
                pack[e, f] = both[:8] + both[8:]
            else:
                full = both + swap(both)
                even = even_rows()
                row = f // 2 * 2
                for h in range(2):
                    part = full[h * 8 : h * 8 + 8]
                    old = pack[e, row + h]
                    pack[e, row + h] = jnp.where(even, jnp.where(lax.rem(f, 2) == 0, part, old), part)
            return carry

        lax.fori_loop(0, FIB, body, 0)
        for k in range(1, 8):
            near_copy(e, k).start()

    def finish_near(e):
        acc = pack[e]
        for k in range(1, 8):
            near_copy(e, k).wait_recv()
            acc = acc + near[e, k]
        half_sum[e] = acc
        far_copy(e).start()

    def finish_far(e, sides):
        far_copy(e).wait_recv()
        total[e] = half_sum[e] + far[e]
        if sides:
            side_copy(e, 0).start()
            side_copy(e, 1).start()
            side_copy(e, 0).wait_recv()
            side_copy(e, 1).wait_recv()

    def start_halo(f, carry):
        halo_copy(0, 0, f).start()
        halo_copy(0, 1, f).start()
        return carry

    lax.fori_loop(0, FIB, start_halo, 0)
    run_step(0, True)
    fill_tables(1)
    plan_switch()
    finish_near(0)
    finish_far(0, True)
    run_step(1, False)

    def gather(s, carry):
        send_items[s] = own[1, pl.ds(slot_item[s] * 4, 4)]
        return carry

    lax.fori_loop(0, 2 * WAVE, gather, 0)
    item_copy(8).start()
    finish_near(1)
    for k in (9, 10, 11, 12, 13, 14, 15, 1, 2, 3, 4, 5, 6, 7):
        item_copy(k).start()
    recv_items[0:2] = send_items[0:2]
    finish_far(1, False)
    for k in range(1, 16):
        item_copy(k).wait_recv()

    def place(i, carry):
        fibre = take_fibre[i]
        u = recv_items[take[i]].reshape(2, 2, 16, 128)
        u = rotate_apart(u, total[1, fibre], nonlin[0, fibre] * (1.0 / CH))
        own[1, pl.ds(i * 4, 4)] = u.reshape(4, 16, 128)
        return carry

    def place_fibre(f, carry):
        for i in range(4):
            place(f * 4 + i, carry)
        keep_edges(1, f, own[1, pl.ds(f * 16, 16)])
        return carry

    lax.fori_loop(0, FIB, place_fibre, 0)

    run_step(2, True)
    finish_near(2)
    finish_far(2, True)
    run_step(3, False)
    finish_near(3)
    finish_far(3, False)

    def store(f):
        group = pl.ds(f * 16, 16)
        return pltpu.make_async_copy(result_buf.at[group], out_hbm.at[group], out_s.at[f])

    def last(f, carry):
        group = pl.ds(f * 16, 16)
        u = own[3, group].reshape(8, 2, 16, 128)
        first, second = unpack_pair(total[3, pl.ds(f // 2 * 2, 2)].reshape(16, 128))
        q = jnp.where(lax.rem(f, 2) == 0, first, second)
        u = rotate_native(u, q, nonlin[1, f] * (1.0 / CH))
        result_buf[group] = u.reshape(16, 16, 128)
        store(f).start()
        return carry

    lax.fori_loop(0, FIB, last, 0)

    def drain_halo(f, carry):
        for e in range(4):
            halo_copy(e, 0, f).wait_send()
            halo_copy(e, 1, f).wait_send()
        return carry

    lax.fori_loop(0, FIB, drain_halo, 0)
    for e in range(4):
        for k in range(1, 8):
            near_copy(e, k).wait_send()
        far_copy(e).wait_send()
    for e in (0, 2):
        side_copy(e, 0).wait_send()
        side_copy(e, 1).wait_send()
    for k in range(1, 16):
        item_copy(k).wait_send()
    for f in range(FIB):
        store(f).wait()


def local(field, lit_count, route_fibre, route_slot, dispersion, nonlinearity):
    rows = field.reshape(FIB, LOC, 2, 2, 8, 128).transpose(0, 1, 2, 4, 3, 5).reshape(SEQ, 16, 128)
    wide, twist = tables()
    smem = pl.BlockSpec(memory_space=pltpu.SMEM)
    hbm = pl.BlockSpec(memory_space=pltpu.HBM)
    dma = pltpu.SemaphoreType.DMA
    result = pl.pallas_call(
        kernel,
        out_shape=jax.ShapeDtypeStruct((SEQ, 16, 128), F32),
        in_specs=[smem] * 3 + [hbm] * 5,
        out_specs=hbm,
        scratch_shapes=[
            pltpu.VMEM((10, 256, 256), BF16),
            pltpu.VMEM((2, 16, 128), F32),
            pltpu.VMEM((FIB, 64), jnp.int32),
            pltpu.VMEM((FIB, 64), jnp.int32),
            pltpu.VMEM((SEQ, 16, 128), F32),
            pltpu.VMEM((SEQ, 16, 128), F32),
            pltpu.VMEM((2, FIB * LOC, 16, 128), F32),
            pltpu.VMEM((2, FIB * LOC, 16, 128), F32),
            pltpu.VMEM((4, 2, SEQ, 8, 128), F32),
            pltpu.VMEM((4, SEQ, 16, 128), F32),
            pltpu.VMEM((3, 2, SEQ, 8, 128), F32),
            pltpu.VMEM((4, FIB, 8, 128), F32),
            pltpu.VMEM((4, 8, FIB, 8, 128), F32),
            pltpu.VMEM((4, FIB, 8, 128), F32),
            pltpu.VMEM((4, FIB, 8, 128), F32),
            pltpu.VMEM((4, FIB, 8, 128), F32),
            pltpu.VMEM((4, 2, FIB, 8, 128), F32),
            pltpu.VMEM((2 * WAVE, 4, 16, 128), F32),
            pltpu.VMEM((2 * WAVE, 4, 16, 128), F32),
            pltpu.SMEM((2 * WAVE,), jnp.int32),
            pltpu.SMEM((WAVE,), jnp.int32),
            pltpu.SMEM((WAVE,), jnp.int32),
            dma((5,)), dma((FIB,)),
            dma((4, 2, FIB)), dma((4, 2, FIB)),
            dma((4, 8)), dma((4, 8)),
            dma((4,)), dma((4,)),
            dma((4, 2)), dma((4, 2)),
            dma((WAVE,)), dma((WAVE,)),
        ],
        compiler_params=pltpu.CompilerParams(
            collective_id=0, has_side_effects=True, vmem_limit_bytes=67043328
        ),
        name="propagate",
    )(lit_count, dispersion, nonlinearity, route_fibre, route_slot, rows, wide, twist)
    back = result.reshape(FIB, LOC, 2, 8, 2, 128).transpose(0, 1, 2, 4, 3, 5)
    return back.reshape(FIB, LOC, 2, 2, 1024)


def solution(mesh):
    return jax.shard_map(
        local,
        mesh=mesh,
        in_specs=(P(None, "wave", None, None, "tm"), P(), P(), P(), P(), P()),
        out_specs=P(None, "wave", None, None, "tm"),
        check_vma=False,
    )
```

```python
import functools
import math

import jax
import jax.numpy as jnp
import numpy as np
from jax import lax
from jax.experimental import pallas as pl
from jax.experimental.pallas import tpu as pltpu
from jax.sharding import PartitionSpec as P

CH = 128
BLK = 2
FIB = 4
LOC = 8
SEQ = 64
WAVE = 16
TM = 32
MESH = pl.DeviceIdType.MESH
F32 = jnp.float32
BF16 = jnp.bfloat16


def split_table(table):
    high = table.astype(jnp.bfloat16)
    low = (table - high.astype(np.float64)).astype(jnp.bfloat16)
    return high, low


def tables():
    eye = np.eye(8)
    r16 = np.arange(16)
    angle = 2.0 * np.pi * np.outer(r16, r16) / 16.0
    cos_a, sin_a = np.cos(angle), np.sin(angle)
    fwd = np.zeros((2, 16, 16, 2))
    fwd[0, :, :, 0], fwd[0, :, :, 1] = cos_a, sin_a
    fwd[1, :, :, 0], fwd[1, :, :, 1] = -sin_a, cos_a
    native = fwd.reshape(2, 16, 32)
    apart = np.concatenate(
        [
            fwd[:, :, lo:hi].transpose(0, 1, 3, 2).reshape(2, 16, -1)
            for lo, hi in ((0, 4), (4, 12), (12, 16))
        ],
        axis=2,
    )
    fwd_native, fwd_apart = (
        np.einsum("xrq,st->xsrtq", v, eye).reshape(256, 256) for v in (native, apart)
    )
    keep = np.zeros((8, 2, 2, 16))
    kc, ks = cos_a[4:12] / 2048.0, sin_a[4:12] / 2048.0
    keep[:, 0, 0], keep[:, 0, 1] = kc, -ks
    keep[:, 1, 0], keep[:, 1, 1] = ks, kc
    inv_native = np.einsum("apxr,st->sapxtr", keep, eye).reshape(128, 256)
    inv_apart = np.einsum("apxr,st->spaxtr", keep, eye).reshape(128, 256)
    b = np.arange(128)
    angle = 2.0 * np.pi * (np.outer(b, b) % 128) / 128.0
    cos_b, sin_b = np.cos(angle), np.sin(angle)
    col_fwd = np.block([[cos_b, -sin_b], [sin_b, cos_b]])
    col_inv = np.block([[cos_b, sin_b], [-sin_b, cos_b]])
    twist = 2.0 * np.pi * np.outer(r16, b) / 2048.0
    wide = []
    for table in (fwd_native, fwd_apart, col_fwd, col_inv):
        wide.extend(split_table(table))
    for table in (inv_native, inv_apart):
        wide.append(np.concatenate(split_table(table), axis=0))
    twist = np.stack([np.cos(twist), np.sin(twist)]).astype(np.float32)
    return jnp.asarray(np.stack(wide)), jnp.asarray(twist)


def fit(function, terms):
    nodes = np.cos(np.pi * (np.arange(400) + 0.5) / 400) * (np.pi * 1.02)
    square = nodes * nodes
    basis = np.stack([square**k for k in range(terms)], axis=1)
    return [float(v) for v in np.linalg.lstsq(basis, function(nodes), rcond=None)[0]]


SIN_POLY = fit(lambda x: np.sinc(x / np.pi), 7)
COS_POLY = fit(np.cos, 7)
TWO_PI = 2.0 * math.pi
PI_A = float(np.float32(6.28125))
PI_B = float(np.float32(np.round((TWO_PI - PI_A) * 2.0**24) / 2.0**24))
PI_B = float(np.floor((TWO_PI - PI_A) * 2.0**20) / 2.0**20)
PI_C = float(TWO_PI - PI_A - PI_B)


def sin_cos(angle):
    turns = jnp.floor(angle * (1.0 / TWO_PI) + 0.5)
    rest = ((angle - turns * PI_A) - turns * PI_B) - turns * PI_C
    square = rest * rest
    sine = jnp.full_like(square, SIN_POLY[-1])
    for value in SIN_POLY[-2::-1]:
        sine = sine * square + value
    cosine = jnp.full_like(square, COS_POLY[-1])
    for value in COS_POLY[-2::-1]:
        cosine = cosine * square + value
    return sine * rest, cosine


def split(x):
    high = x.astype(BF16)
    low = (x - high.astype(F32)).astype(BF16)
    return high, low


def dot(a, b):
    return jnp.dot(a, b, preferred_element_type=F32)


def left_product(table, data):
    high, low = split(data)
    return dot(table[0][...], high) + (dot(table[1][...], high) + dot(table[0][...], low))


def right_product(data, table):
    high, low = split(data)
    return dot(high, table[0][...]) + (dot(low, table[0][...]) + dot(high, table[1][...]))


def low_rows():
    return lax.broadcasted_iota(jnp.int32, (8, 128), 0) < 4


def even_rows():
    return lax.rem(lax.broadcasted_iota(jnp.int32, (8, 128), 0), 2) == 0


def turn(x, shift):
    return pltpu.roll(x.reshape(-1, 8, 128), shift, 1).reshape(x.shape)


def swap(x):
    t = x.reshape(-1, 8, 128)
    return jnp.where(even_rows()[None], pltpu.roll(t, 7, 1), pltpu.roll(t, 1, 1)).reshape(x.shape)


def unpack_pair(x):
    t = x.reshape(-1, 8, 128)
    even = even_rows()[None]
    first = jnp.where(even, t, pltpu.roll(t, 1, 1)).reshape(x.shape)
    second = jnp.where(even, pltpu.roll(t, 7, 1), t).reshape(x.shape)
    return first, second


def rotate_native(u, total, gain):
    square = u * u
    both = square[:, 0] + square[:, 1]
    phase = gain * (2.0 * total[None] - (both + swap(both)))
    sine, cosine = sin_cos(phase)
    t = sine.reshape(-1, 8, 128)
    signed = jnp.where(even_rows()[None], -t, t).reshape(sine.shape)
    return u * cosine[:, None] + swap(u) * signed[:, None]


def rotate_apart(u, total, gain):
    re, im = u[:, :, :8], u[:, :, 8:]
    square = re * re + im * im
    phase = gain * (2.0 * total[None] - (square[:, 0] + square[:, 1]))
    sine, cosine = sin_cos(phase)
    sine, cosine = sine[:, None], cosine[:, None]
    return jnp.concatenate([re * cosine - im * sine, re * sine + im * cosine], axis=2)


def rotate_edge(u, total, gain):
    square = u * u
    both = square[:, 0] + square[:, 1]
    phase = gain * (2.0 * total[None] - (both + turn(both, 4)))
    sine, cosine = sin_cos(phase)
    signed = jnp.where(low_rows()[None], -sine, sine)
    return u * cosine[:, None] + turn(u, 4) * signed[:, None]


def edges(u):
    re, im = u[..., :8, :], u[..., 8:, :]
    low = low_rows()
    return jnp.where(low, turn(re, 4), im), jnp.where(low, re, turn(im, 4))


def disperse(u, t, fwd, inv, filt_cos, filt_sin):
    rows = u.reshape(512, 128)
    x = jnp.concatenate([rows[:256], rows[256:]], axis=1)
    y = left_product(t[fwd], x)
    tc = jnp.broadcast_to(t["twist_cos"][...][None], (8, 16, 128)).reshape(128, 128)
    ts = jnp.broadcast_to(t["twist_sin"][...][None], (8, 16, 128)).reshape(128, 128)
    halves = []
    for h in range(2):
        re = y[:128, h * 128 : (h + 1) * 128]
        im = y[128:, h * 128 : (h + 1) * 128]
        halves.append(jnp.concatenate([re * tc + im * ts, im * tc - re * ts], axis=1))
    spectrum = right_product(jnp.concatenate(halves, axis=0), t["col_fwd"])
    sr, si = spectrum[:, :128], spectrum[:, 128:]
    fc = jnp.broadcast_to(filt_cos[:, None], (8, 2, 16, 128)).reshape(256, 128)
    fs = jnp.broadcast_to(filt_sin[:, None], (8, 2, 16, 128)).reshape(256, 128)
    shaped = jnp.concatenate([sr * fc - si * fs, sr * fs + si * fc], axis=1)
    back = right_product(shaped, t["col_inv"])
    br, bi = back[:, :128], back[:, 128:]
    parts = []
    for h in range(2):
        re, im = br[h * 128 : (h + 1) * 128], bi[h * 128 : (h + 1) * 128]
        parts.append(jnp.concatenate([re * tc - im * ts, re * ts + im * tc], axis=0))
    out = left_product(t[inv], jnp.concatenate(parts, axis=1))
    return jnp.concatenate([out[:, :128], out[:, 128:]], axis=0).reshape(16, 16, 128)


def kernel(
    lit, disp, nonlin, fibre_hbm, slot_hbm, field_hbm, wide_hbm, twist_hbm,
    out_hbm,
    wide, twist, route_f, route_s, launch, result_buf,
    filt_c, filt_s, halo, own, edge, pack, near, far, half_sum, total, q_side0, q_side1, q_side2,
    send_items, first_own, first_edge, first_halo, slot_own, slot_edge, slot_halo, slot_fc, slot_fs,
    slot_item, slot_from, take, take_fibre,
    load_s, out_s,
    halo_ss, halo_rs, near_ss, near_rs, far_ss, far_rs, side_ss, side_rs, item_ss, item_rs,
    first_ss, first_rs, group_ss, group_rs, second_ss, second_rs,
):
    t = dict(
        fwd_native=(wide.at[0], wide.at[1]), fwd_apart=(wide.at[2], wide.at[3]),
        col_fwd=(wide.at[4], wide.at[5]), col_inv=(wide.at[6], wide.at[7]),
        inv_native=(wide.at[8, pl.ds(0, 128)], wide.at[8, pl.ds(128, 128)]),
        inv_apart=(wide.at[9, pl.ds(0, 128)], wide.at[9, pl.ds(128, 128)]),
        twist_cos=twist.at[0], twist_sin=twist.at[1],
    )
    q_side = (q_side0, q_side1, q_side2)
    me = lax.axis_index("wave")
    at = lax.axis_index("tm")
    my_z = me // 8
    my_y = lax.rem(me // 2, 4)
    my_core = lax.rem(me, 2)
    right = lax.rem(at + 1, TM)
    left = lax.rem(at + TM - 1, TM)

    def mate(k, sign=1):
        kz, ky, kc = lax.div(k, 8), lax.rem(lax.div(k, 2), 4), lax.rem(k, 2)
        if sign < 0:
            ky = 4 - ky
        return lax.rem(my_z + kz, 2) * 8 + lax.rem(my_y + ky, 4) * 2 + lax.rem(my_core + kc, 2)

    q_right = (lax.rem(me + 8 * (at // (TM - 1)), WAVE), right)
    q_left = (lax.rem(me + 8 * ((TM - 1 - at) // (TM - 1)), WAVE), left)
    d_right, d_left = (me, right), (me, left)

    barrier = pltpu.get_barrier_semaphore()
    for k in range(1, 16):
        pl.semaphore_signal(barrier, inc=1, device_id=(mate(k), at), device_id_type=MESH)
    for target in (d_right, d_left, q_right, q_left):
        pl.semaphore_signal(barrier, inc=1, device_id=target, device_id_type=MESH)
    loads = [
        pltpu.make_async_copy(src, dst, load_s.at[i])
        for i, (src, dst) in enumerate(
            ((field_hbm, launch), (wide_hbm, wide), (twist_hbm, twist), (fibre_hbm, route_f), (slot_hbm, route_s))
        )
    ]
    for load in loads:
        load.start()

    r_i = lax.broadcasted_iota(jnp.int32, (16, 128), 0)
    m_i = lax.broadcasted_iota(jnp.int32, (16, 128), 1)
    k_i = r_i + 16 * m_i
    omega = jnp.where(k_i < 1024, k_i, k_i - 2048).astype(F32) * (2.0 * math.pi / 2048.0)

    def fill_tables(span):
        def fill(i, carry):
            channel = (me * LOC + lax.rem(i, LOC)).astype(F32)
            offset = (math.pi / 2.0) * (2.0 * channel + 1.0 - CH) / CH
            theta = disp[span, i // LOC] * (omega * omega + 2.0 * omega * offset)
            sine, cosine = sin_cos(theta)
            filt_s[span, i] = sine
            filt_c[span, i] = cosine
            return carry

        lax.fori_loop(0, FIB * LOC, fill, 0)

    def plan_switch():
        fibre_of = lax.broadcasted_iota(jnp.int32, (FIB, 64), 0)
        block_of = lax.broadcasted_iota(jnp.int32, (FIB, 64), 1)
        group_of = block_of // 4
        slot = route_s[...]
        target = slot // 4
        landing = route_f[...] * 4 + slot % 4
        key = landing * 16 + fibre_of * 4 + block_of % 4
        mine = group_of == me
        for k in range(16):
            here = mine & (target == mate(k))
            low = jnp.min(jnp.where(here, key, 4095))
            high = jnp.max(jnp.where(here, key, 0))
            slot_item[k] = lax.rem(low, 16)
            slot_item[16 + k] = lax.rem(high, 16)
            here = (group_of == mate(k, -1)) & (target == me)
            slot_from[k] = lax.rem(jnp.min(jnp.where(here, key, 4095)), 16)
        code = group_of * 4 + fibre_of
        groups = []
        for i in range(16):
            value = jnp.sum(jnp.where((target == me) & (landing == i), code, 0))
            group = lax.rem(value // 4, WAVE)
            before = jnp.int32(0)
            for other in groups:
                before = before + jnp.where(other == group, 1, 0)
            groups.append(group)
            kz = lax.rem(my_z - group // 8 + 2, 2)
            ky = lax.rem(my_y - lax.rem(group // 2, 4) + 4, 4)
            kc = lax.rem(my_core - lax.rem(group, 2) + 2, 2)
            take[i] = jnp.minimum(before, 1) * 16 + kz * 8 + ky * 2 + kc
            take_fibre[i] = lax.rem(value, 4)

    def fill_slots(k, carry):
        item = slot_from[k]
        source = mate(k, -1)
        for c in range(BLK):
            channel = (source * LOC + lax.rem(item, 4) * BLK + c).astype(F32)
            offset = (math.pi / 2.0) * (2.0 * channel + 1.0 - CH) / CH
            theta = disp[0, lax.div(item, 4)] * (omega * omega + 2.0 * omega * offset)
            sine, cosine = sin_cos(theta)
            slot_fs[k * BLK + c] = sine
            slot_fc[k * BLK + c] = cosine
        return carry

    fill_tables(0)
    for load in loads:
        load.wait()
    plan_switch()
    pl.semaphore_wait(barrier, 19)

    def halo_copy(e, side, f):
        group = pl.ds(f * 16, 16)
        if e == 0:
            src = launch.at[group, pl.ds(8, 8) if side == 0 else pl.ds(0, 8)]
        else:
            src = edge.at[e - 1, side, group]
        return pltpu.make_async_remote_copy(
            src_ref=src,
            dst_ref=halo.at[e, side, group],
            send_sem=halo_ss.at[e, side, f],
            recv_sem=halo_rs.at[e, side, f],
            device_id=d_right if side == 0 else d_left,
            device_id_type=MESH,
        )

    def near_copy(e, k):
        return pltpu.make_async_remote_copy(
            src_ref=pack.at[e], dst_ref=near.at[e, k], send_sem=near_ss.at[e, k],
            recv_sem=near_rs.at[e, k], device_id=(mate(k), at), device_id_type=MESH,
        )

    def far_copy(e):
        return pltpu.make_async_remote_copy(
            src_ref=half_sum.at[e], dst_ref=far.at[e], send_sem=far_ss.at[e],
            recv_sem=far_rs.at[e], device_id=(mate(8), at), device_id_type=MESH,
        )

    def side_copy(e, side):
        return pltpu.make_async_remote_copy(
            src_ref=total.at[e], dst_ref=q_side[e].at[side], send_sem=side_ss.at[e, side],
            recv_sem=side_rs.at[e, side], device_id=q_right if side == 0 else q_left,
            device_id_type=MESH,
        )

    def item_copy(j, k):
        return pltpu.make_async_remote_copy(
            src_ref=send_items.at[j, k], dst_ref=first_own.at[k] if j == 0 else slot_own.at[16 + k],
            send_sem=item_ss.at[j, k], recv_sem=item_rs.at[j, k], device_id=(mate(k), at),
            device_id_type=MESH,
        )

    def to_side(src, dst, send_sem, recv_sem, side):
        return pltpu.make_async_remote_copy(
            src_ref=src, dst_ref=dst, send_sem=send_sem, recv_sem=recv_sem,
            device_id=d_right if side == 0 else d_left, device_id_type=MESH,
        )

    def first_copy(side, k):
        return to_side(
            first_edge.at[side, k], first_halo.at[side, k], first_ss.at[side, k], first_rs.at[side, k], side
        )

    def group_copy(side, g):
        slots = pl.ds(g * 4, 4)
        return to_side(
            slot_edge.at[side, slots], slot_halo.at[side, slots], group_ss.at[side, g],
            group_rs.at[side, g], side,
        )

    def second_copy(side, k):
        return to_side(
            slot_edge.at[side, 16 + k], slot_halo.at[side, 16 + k], second_ss.at[side, k],
            second_rs.at[side, k], side,
        )

    def keep_edges(e, f, u):
        group = pl.ds(f * 16, 16)
        edge[e, 0, group], edge[e, 1, group] = edges(u)
        halo_copy(e + 1, 0, f).start()
        halo_copy(e + 1, 1, f).start()

    def turned(parts, channels, e, fibre, gain):
        low = low_rows()
        before, after = q_side[e][0, fibre], q_side[e][1, fibre]
        sums = (
            jnp.where(low, turn(before, 4), before),
            total[e, fibre],
            jnp.where(low, after, turn(after, 4)),
        )
        turns = (rotate_edge, rotate_apart, rotate_edge)
        return jnp.concatenate(
            [
                rule(part.reshape(channels, 2, *part.shape[1:]), q, gain).reshape(part.shape)
                for rule, part, q in zip(turns, parts, sums)
            ],
            axis=1,
        )

    def placed(f):
        blocks = []
        for i in range(4):
            slot, fibre = take[f * 4 + i], take_fibre[f * 4 + i]
            parts = [slot_halo[0, slot], slot_own[slot], slot_halo[1, slot]]
            blocks.append(turned(parts, BLK, 1, fibre, nonlin[0, fibre] * (1.0 / CH)))
        return jnp.concatenate(blocks, axis=0)

    def run_step(e, send_halo):
        span = e // 2

        def body(f, carry):
            group = pl.ds(f * 16, 16)
            if e == 2:
                u = placed(f)
            else:
                halo_copy(e, 0, f).wait_recv()
                halo_copy(e, 1, f).wait_recv()
                parts = [halo[e, 0, group], launch[group] if e == 0 else own[e - 1, group], halo[e, 1, group]]
                if e == 0:
                    channel = me * LOC + lax.broadcasted_iota(jnp.int32, (16, 1, 128), 0) // 2
                    u = jnp.where(channel < lit[f], jnp.concatenate(parts, axis=1), 0.0)
                else:
                    u = turned(parts, LOC, e - 1, f, nonlin[span, f] * (1.0 / CH))
            table = pl.ds(f * LOC, LOC)
            result = disperse(
                u, t, "fwd_native" if e == 0 else "fwd_apart", "inv_native" if e == 3 else "inv_apart",
                filt_c[span, table], filt_s[span, table],
            )
            own[e, group] = result
            if send_halo:
                keep_edges(e, f, result)
            both = jnp.sum(result * result, axis=0)
            if e < 3:
                pack[e, f] = both[:8] + both[8:]
            else:
                full = both + swap(both)
                even = even_rows()
                row = f // 2 * 2
                for h in range(2):
                    part = full[h * 8 : h * 8 + 8]
                    old = pack[e, row + h]
                    pack[e, row + h] = jnp.where(even, jnp.where(lax.rem(f, 2) == 0, part, old), part)
            return carry

        lax.fori_loop(0, FIB, body, 0)
        for k in range(1, 8):
            near_copy(e, k).start()

    def gather(j):
        def one(k, carry):
            send_items[j, k] = own[j, pl.ds(slot_item[16 * j + k] * 4, 4)]
            return carry

        lax.fori_loop(0, WAVE, one, 0)
        (first_own if j == 0 else slot_own)[16 * j] = send_items[j, 0]

    def forward_first(k):
        first_edge[0, k], first_edge[1, k] = edges(first_own[k])
        first_copy(0, k).start()
        first_copy(1, k).start()

    def forward_second(k):
        slot_edge[0, 16 + k], slot_edge[1, 16 + k] = edges(slot_own[16 + k])
        second_copy(0, k).start()
        second_copy(1, k).start()

    def first_slots(g, carry):
        blocks = []
        for i in range(4):
            k = g * 4 + i
            first_copy(0, k).wait_recv()
            first_copy(1, k).wait_recv()
            fibre = lax.div(slot_from[k], 4)
            parts = [first_halo[0, k], first_own[k], first_halo[1, k]]
            blocks.append(turned(parts, BLK, 0, fibre, nonlin[0, fibre] * (1.0 / CH)))
        table = pl.ds(g * LOC, LOC)
        result = disperse(
            jnp.concatenate(blocks, axis=0), t, "fwd_apart", "inv_apart", slot_fc[table], slot_fs[table]
        )
        slots = pl.ds(g * 4, 4)
        slot_own[slots] = result.reshape(4, 4, 16, 128)
        up, down = edges(result)
        slot_edge[0, slots] = up.reshape(4, 4, 8, 128)
        slot_edge[1, slots] = down.reshape(4, 4, 8, 128)
        group_copy(0, g).start()
        group_copy(1, g).start()
        return carry

    def finish_near(e):
        acc = pack[e]
        for k in range(1, 8):
            near_copy(e, k).wait_recv()
            acc = acc + near[e, k]
        half_sum[e] = acc
        far_copy(e).start()

    def finish_far(e, sides):
        far_copy(e).wait_recv()
        total[e] = half_sum[e] + far[e]
        if sides:
            side_copy(e, 0).start()
            side_copy(e, 1).start()
            side_copy(e, 0).wait_recv()
            side_copy(e, 1).wait_recv()

    def start_halo(f, carry):
        halo_copy(0, 0, f).start()
        halo_copy(0, 1, f).start()
        return carry

    lax.fori_loop(0, FIB, start_halo, 0)
    fill_tables(1)
    lax.fori_loop(0, WAVE, fill_slots, 0)
    run_step(0, True)
    gather(0)
    item_copy(0, 8).start()
    finish_near(0)
    order = (9, 10, 11, 12, 13, 14, 15, 1, 2, 3, 4, 5, 6, 7)
    for k in order:
        item_copy(0, k).start()
    finish_far(0, True)
    run_step(1, False)
    gather(1)
    item_copy(1, 8).start()
    finish_near(1)
    for k in order:
        item_copy(1, k).start()

    forward_first(0)
    for k in (1, 2, 3, 4, 5, 6, 7, 8, 9, 10, 11, 12, 13, 14, 15):
        item_copy(0, k).wait_recv()
        forward_first(k)
    forward_second(0)
    lax.fori_loop(0, 4, first_slots, 0)
    finish_far(1, True)
    for k in (1, 2, 3, 4, 5, 6, 7, 8, 9, 10, 11, 12, 13, 14, 15):
        item_copy(1, k).wait_recv()
        forward_second(k)
    for g in range(4):
        group_copy(0, g).wait_recv()
        group_copy(1, g).wait_recv()
    for k in range(16):
        second_copy(0, k).wait_recv()
        second_copy(1, k).wait_recv()

    run_step(2, True)
    finish_near(2)
    finish_far(2, True)
    run_step(3, False)
    finish_near(3)
    finish_far(3, False)

    def store(f):
        group = pl.ds(f * 16, 16)
        return pltpu.make_async_copy(result_buf.at[group], out_hbm.at[group], out_s.at[f])

    def last(f, carry):
        group = pl.ds(f * 16, 16)
        u = own[3, group].reshape(8, 2, 16, 128)
        first, second = unpack_pair(total[3, pl.ds(f // 2 * 2, 2)].reshape(16, 128))
        q = jnp.where(lax.rem(f, 2) == 0, first, second)
        u = rotate_native(u, q, nonlin[1, f] * (1.0 / CH))
        result_buf[group] = u.reshape(16, 16, 128)
        store(f).start()
        return carry

    lax.fori_loop(0, FIB, last, 0)

    def drain_halo(f, carry):
        for e in (0, 1, 3):
            halo_copy(e, 0, f).wait_send()
            halo_copy(e, 1, f).wait_send()
        return carry

    lax.fori_loop(0, FIB, drain_halo, 0)
    for e in range(4):
        for k in range(1, 8):
            near_copy(e, k).wait_send()
        far_copy(e).wait_send()
    for e in range(3):
        side_copy(e, 0).wait_send()
        side_copy(e, 1).wait_send()
    for k in range(1, 16):
        item_copy(0, k).wait_send()
        item_copy(1, k).wait_send()
    for side in range(2):
        for k in range(16):
            first_copy(side, k).wait_send()
            second_copy(side, k).wait_send()
        for g in range(4):
            group_copy(side, g).wait_send()
    for f in range(FIB):
        store(f).wait()


def local(field, lit_count, route_fibre, route_slot, dispersion, nonlinearity):
    rows = field.reshape(FIB, LOC, 2, 2, 8, 128).transpose(0, 1, 2, 4, 3, 5).reshape(SEQ, 16, 128)
    wide, twist = tables()
    smem = pl.BlockSpec(memory_space=pltpu.SMEM)
    hbm = pl.BlockSpec(memory_space=pltpu.HBM)
    dma = pltpu.SemaphoreType.DMA
    result = pl.pallas_call(
        kernel,
        out_shape=jax.ShapeDtypeStruct((SEQ, 16, 128), F32),
        in_specs=[smem] * 3 + [hbm] * 5,
        out_specs=hbm,
        scratch_shapes=[
            pltpu.VMEM((10, 256, 256), BF16),
            pltpu.VMEM((2, 16, 128), F32),
            pltpu.VMEM((FIB, 64), jnp.int32),
            pltpu.VMEM((FIB, 64), jnp.int32),
            pltpu.VMEM((SEQ, 16, 128), F32),
            pltpu.VMEM((SEQ, 16, 128), F32),
            pltpu.VMEM((2, FIB * LOC, 16, 128), F32),
            pltpu.VMEM((2, FIB * LOC, 16, 128), F32),
            pltpu.VMEM((4, 2, SEQ, 8, 128), F32),
            pltpu.VMEM((4, SEQ, 16, 128), F32),
            pltpu.VMEM((3, 2, SEQ, 8, 128), F32),
            pltpu.VMEM((4, FIB, 8, 128), F32),
            pltpu.VMEM((4, 8, FIB, 8, 128), F32),
            pltpu.VMEM((4, FIB, 8, 128), F32),
            pltpu.VMEM((4, FIB, 8, 128), F32),
            pltpu.VMEM((4, FIB, 8, 128), F32),
            pltpu.VMEM((2, FIB, 8, 128), F32),
            pltpu.VMEM((2, FIB, 8, 128), F32),
            pltpu.VMEM((2, FIB, 8, 128), F32),
            pltpu.VMEM((2, WAVE, 4, 16, 128), F32),
            pltpu.VMEM((WAVE, 4, 16, 128), F32),
            pltpu.VMEM((2, WAVE, 4, 8, 128), F32),
            pltpu.VMEM((2, WAVE, 4, 8, 128), F32),
            pltpu.VMEM((2 * WAVE, 4, 16, 128), F32),
            pltpu.VMEM((2, 2 * WAVE, 4, 8, 128), F32),
            pltpu.VMEM((2, 2 * WAVE, 4, 8, 128), F32),
            pltpu.VMEM((2 * WAVE, 16, 128), F32),
            pltpu.VMEM((2 * WAVE, 16, 128), F32),
            pltpu.SMEM((2 * WAVE,), jnp.int32),
            pltpu.SMEM((WAVE,), jnp.int32),
            pltpu.SMEM((WAVE,), jnp.int32),
            pltpu.SMEM((WAVE,), jnp.int32),
            dma((5,)), dma((FIB,)),
            dma((4, 2, FIB)), dma((4, 2, FIB)),
            dma((4, 8)), dma((4, 8)),
            dma((4,)), dma((4,)),
            dma((4, 2)), dma((4, 2)),
            dma((2, WAVE)), dma((2, WAVE)),
            dma((2, WAVE)), dma((2, WAVE)),
            dma((2, FIB)), dma((2, FIB)),
            dma((2, WAVE)), dma((2, WAVE)),
        ],
        compiler_params=pltpu.CompilerParams(
            collective_id=0, has_side_effects=True, vmem_limit_bytes=67043328
        ),
        name="propagate",
    )(lit_count, dispersion, nonlinearity, route_fibre, route_slot, rows, wide, twist)
    back = result.reshape(FIB, LOC, 2, 8, 2, 128).transpose(0, 1, 2, 4, 3, 5)
    return back.reshape(FIB, LOC, 2, 2, 1024)


def solution(mesh):
    return jax.shard_map(
        local,
        mesh=mesh,
        in_specs=(P(None, "wave", None, None, "tm"), P(), P(), P(), P(), P()),
        out_specs=P(None, "wave", None, None, "tm"),
        check_vma=False,
    )
```

```python
import functools
import math

import jax
import jax.numpy as jnp
import numpy as np
from jax import lax
from jax.experimental import pallas as pl
from jax.experimental.pallas import tpu as pltpu
from jax.sharding import PartitionSpec as P

CH = 128
BLK = 2
FIB = 4
LOC = 8
SEQ = 64
WAVE = 16
TM = 32
MESH = pl.DeviceIdType.MESH
F32 = jnp.float32
BF16 = jnp.bfloat16


def split_table(table):
    high = table.astype(jnp.bfloat16)
    low = (table - high.astype(np.float64)).astype(jnp.bfloat16)
    return high, low


def tables():
    eye = np.eye(8)
    r16 = np.arange(16)
    angle = 2.0 * np.pi * np.outer(r16, r16) / 16.0
    cos_a, sin_a = np.cos(angle), np.sin(angle)
    fwd = np.zeros((2, 16, 16, 2))
    fwd[0, :, :, 0], fwd[0, :, :, 1] = cos_a, sin_a
    fwd[1, :, :, 0], fwd[1, :, :, 1] = -sin_a, cos_a
    native = fwd.reshape(2, 16, 32)
    apart = np.concatenate(
        [
            fwd[:, :, lo:hi].transpose(0, 1, 3, 2).reshape(2, 16, -1)
            for lo, hi in ((0, 4), (4, 12), (12, 16))
        ],
        axis=2,
    )
    fwd_native, fwd_apart = (
        np.einsum("xrq,st->xsrtq", v, eye).reshape(256, 256) for v in (native, apart)
    )
    keep = np.zeros((8, 2, 2, 16))
    kc, ks = cos_a[4:12] / 2048.0, sin_a[4:12] / 2048.0
    keep[:, 0, 0], keep[:, 0, 1] = kc, -ks
    keep[:, 1, 0], keep[:, 1, 1] = ks, kc
    inv_native = np.einsum("apxr,st->sapxtr", keep, eye).reshape(128, 256)
    inv_apart = np.einsum("apxr,st->spaxtr", keep, eye).reshape(128, 256)
    b = np.arange(128)
    angle = 2.0 * np.pi * (np.outer(b, b) % 128) / 128.0
    cos_b, sin_b = np.cos(angle), np.sin(angle)
    col_fwd = np.block([[cos_b, -sin_b], [sin_b, cos_b]])
    col_inv = np.block([[cos_b, sin_b], [-sin_b, cos_b]])
    twist = 2.0 * np.pi * np.outer(r16, b) / 2048.0
    wide = []
    for table in (fwd_native, fwd_apart, col_fwd, col_inv):
        wide.extend(split_table(table))
    for table in (inv_native, inv_apart):
        wide.append(np.concatenate(split_table(table), axis=0))
    twist = np.stack([np.cos(twist), np.sin(twist)]).astype(np.float32)
    return jnp.asarray(np.stack(wide)), jnp.asarray(twist)


def fit(function, terms):
    nodes = np.cos(np.pi * (np.arange(400) + 0.5) / 400) * (np.pi * 1.02)
    square = nodes * nodes
    basis = np.stack([square**k for k in range(terms)], axis=1)
    return [float(v) for v in np.linalg.lstsq(basis, function(nodes), rcond=None)[0]]


SIN_POLY = fit(lambda x: np.sinc(x / np.pi), 7)
COS_POLY = fit(np.cos, 7)
TWO_PI = 2.0 * math.pi
PI_A = float(np.float32(6.28125))
PI_B = float(np.float32(np.round((TWO_PI - PI_A) * 2.0**24) / 2.0**24))
PI_B = float(np.floor((TWO_PI - PI_A) * 2.0**20) / 2.0**20)
PI_C = float(TWO_PI - PI_A - PI_B)


def sin_cos(angle):
    turns = jnp.floor(angle * (1.0 / TWO_PI) + 0.5)
    rest = ((angle - turns * PI_A) - turns * PI_B) - turns * PI_C
    square = rest * rest
    sine = jnp.full_like(square, SIN_POLY[-1])
    for value in SIN_POLY[-2::-1]:
        sine = sine * square + value
    cosine = jnp.full_like(square, COS_POLY[-1])
    for value in COS_POLY[-2::-1]:
        cosine = cosine * square + value
    return sine * rest, cosine


def split(x):
    high = x.astype(BF16)
    low = (x - high.astype(F32)).astype(BF16)
    return high, low


def dot(a, b):
    return jnp.dot(a, b, preferred_element_type=F32)


def left_product(table, data):
    high, low = split(data)
    return dot(table[0][...], high) + (dot(table[1][...], high) + dot(table[0][...], low))


def right_product(data, table):
    high, low = split(data)
    return dot(high, table[0][...]) + (dot(low, table[0][...]) + dot(high, table[1][...]))


def low_rows():
    return lax.broadcasted_iota(jnp.int32, (8, 128), 0) < 4


def even_rows():
    return lax.rem(lax.broadcasted_iota(jnp.int32, (8, 128), 0), 2) == 0


def turn(x, shift):
    return pltpu.roll(x.reshape(-1, 8, 128), shift, 1).reshape(x.shape)


def swap(x):
    t = x.reshape(-1, 8, 128)
    return jnp.where(even_rows()[None], pltpu.roll(t, 7, 1), pltpu.roll(t, 1, 1)).reshape(x.shape)


def unpack_pair(x):
    t = x.reshape(-1, 8, 128)
    even = even_rows()[None]
    first = jnp.where(even, t, pltpu.roll(t, 1, 1)).reshape(x.shape)
    second = jnp.where(even, pltpu.roll(t, 7, 1), t).reshape(x.shape)
    return first, second


def rotate_native(u, total, gain):
    square = u * u
    both = square[:, 0] + square[:, 1]
    phase = gain * (2.0 * total[None] - (both + swap(both)))
    sine, cosine = sin_cos(phase)
    t = sine.reshape(-1, 8, 128)
    signed = jnp.where(even_rows()[None], -t, t).reshape(sine.shape)
    return u * cosine[:, None] + swap(u) * signed[:, None]


def rotate_apart(u, total, gain):
    re, im = u[:, :, :8], u[:, :, 8:]
    square = re * re + im * im
    phase = gain * (2.0 * total[None] - (square[:, 0] + square[:, 1]))
    sine, cosine = sin_cos(phase)
    sine, cosine = sine[:, None], cosine[:, None]
    return jnp.concatenate([re * cosine - im * sine, re * sine + im * cosine], axis=2)


def rotate_edge(u, total, gain):
    square = u * u
    both = square[:, 0] + square[:, 1]
    phase = gain * (2.0 * total[None] - (both + turn(both, 4)))
    sine, cosine = sin_cos(phase)
    signed = jnp.where(low_rows()[None], -sine, sine)
    return u * cosine[:, None] + turn(u, 4) * signed[:, None]


def edges(u):
    re, im = u[..., :8, :], u[..., 8:, :]
    low = low_rows()
    return jnp.where(low, turn(re, 4), im), jnp.where(low, re, turn(im, 4))


def disperse(u, t, fwd, inv, filt_cos, filt_sin):
    rows = u.reshape(512, 128)
    x = jnp.concatenate([rows[:256], rows[256:]], axis=1)
    y = left_product(t[fwd], x)
    tc = jnp.broadcast_to(t["twist_cos"][...][None], (8, 16, 128)).reshape(128, 128)
    ts = jnp.broadcast_to(t["twist_sin"][...][None], (8, 16, 128)).reshape(128, 128)
    halves = []
    for h in range(2):
        re = y[:128, h * 128 : (h + 1) * 128]
        im = y[128:, h * 128 : (h + 1) * 128]
        halves.append(jnp.concatenate([re * tc + im * ts, im * tc - re * ts], axis=1))
    spectrum = right_product(jnp.concatenate(halves, axis=0), t["col_fwd"])
    sr, si = spectrum[:, :128], spectrum[:, 128:]
    fc = jnp.broadcast_to(filt_cos[:, None], (8, 2, 16, 128)).reshape(256, 128)
    fs = jnp.broadcast_to(filt_sin[:, None], (8, 2, 16, 128)).reshape(256, 128)
    shaped = jnp.concatenate([sr * fc - si * fs, sr * fs + si * fc], axis=1)
    back = right_product(shaped, t["col_inv"])
    br, bi = back[:, :128], back[:, 128:]
    parts = []
    for h in range(2):
        re, im = br[h * 128 : (h + 1) * 128], bi[h * 128 : (h + 1) * 128]
        parts.append(jnp.concatenate([re * tc - im * ts, re * ts + im * tc], axis=0))
    out = left_product(t[inv], jnp.concatenate(parts, axis=1))
    return jnp.concatenate([out[:, :128], out[:, 128:]], axis=0).reshape(16, 16, 128)


def kernel(
    lit, disp, nonlin, fibre_hbm, slot_hbm, field_hbm, wide_hbm, twist_hbm,
    out_hbm,
    wide, twist, route_f, route_s, launch, result_buf,
    filt_c, filt_s, halo, own, edge, pack, near, far, half_sum, total, q_side0, q_side2,
    send_items, send_edge, first_own, first_edge, first_halo, slot_own, slot_fc, slot_fs,
    slot_item, slot_from, take, take_fibre,
    load_s, out_s,
    halo_ss, halo_rs, near_ss, near_rs, far_ss, far_rs, side_ss, side_rs, item_ss, item_rs,
    first_ss, first_rs,
):
    t = dict(
        fwd_native=(wide.at[0], wide.at[1]), fwd_apart=(wide.at[2], wide.at[3]),
        col_fwd=(wide.at[4], wide.at[5]), col_inv=(wide.at[6], wide.at[7]),
        inv_native=(wide.at[8, pl.ds(0, 128)], wide.at[8, pl.ds(128, 128)]),
        inv_apart=(wide.at[9, pl.ds(0, 128)], wide.at[9, pl.ds(128, 128)]),
        twist_cos=twist.at[0], twist_sin=twist.at[1],
    )
    q_side = {0: q_side0, 2: q_side2}
    me = lax.axis_index("wave")
    at = lax.axis_index("tm")
    my_z = me // 8
    my_y = lax.rem(me // 2, 4)
    my_core = lax.rem(me, 2)
    right = lax.rem(at + 1, TM)
    left = lax.rem(at + TM - 1, TM)

    def mate(k, sign=1):
        kz, ky, kc = lax.div(k, 8), lax.rem(lax.div(k, 2), 4), lax.rem(k, 2)
        if sign < 0:
            ky = 4 - ky
        return lax.rem(my_z + kz, 2) * 8 + lax.rem(my_y + ky, 4) * 2 + lax.rem(my_core + kc, 2)

    q_right = (lax.rem(me + 8 * (at // (TM - 1)), WAVE), right)
    q_left = (lax.rem(me + 8 * ((TM - 1 - at) // (TM - 1)), WAVE), left)
    d_right, d_left = (me, right), (me, left)

    barrier = pltpu.get_barrier_semaphore()
    for k in range(1, 16):
        pl.semaphore_signal(barrier, inc=1, device_id=(mate(k), at), device_id_type=MESH)
    for target in (d_right, d_left, q_right, q_left):
        pl.semaphore_signal(barrier, inc=1, device_id=target, device_id_type=MESH)
    is_last = at // (TM - 1)
    is_first = (TM - 1 - at) // (TM - 1)

    @pl.when(is_last + is_first > 0)
    def _():
        across = lax.rem(at + is_last + TM - is_first, TM)
        for k in range(8, 16):
            pl.semaphore_signal(barrier, inc=1, device_id=(mate(k), across), device_id_type=MESH)

    loads = [
        pltpu.make_async_copy(src, dst, load_s.at[i])
        for i, (src, dst) in enumerate(
            ((field_hbm, launch), (wide_hbm, wide), (twist_hbm, twist), (fibre_hbm, route_f), (slot_hbm, route_s))
        )
    ]
    for load in loads:
        load.start()

    r_i = lax.broadcasted_iota(jnp.int32, (16, 128), 0)
    m_i = lax.broadcasted_iota(jnp.int32, (16, 128), 1)
    k_i = r_i + 16 * m_i
    omega = jnp.where(k_i < 1024, k_i, k_i - 2048).astype(F32) * (2.0 * math.pi / 2048.0)

    def fill_tables(span):
        def fill(i, carry):
            channel = (me * LOC + lax.rem(i, LOC)).astype(F32)
            offset = (math.pi / 2.0) * (2.0 * channel + 1.0 - CH) / CH
            theta = disp[span, i // LOC] * (omega * omega + 2.0 * omega * offset)
            sine, cosine = sin_cos(theta)
            filt_s[span, i] = sine
            filt_c[span, i] = cosine
            return carry

        lax.fori_loop(0, FIB * LOC, fill, 0)

    def plan_switch():
        fibre_of = lax.broadcasted_iota(jnp.int32, (FIB, 64), 0)
        block_of = lax.broadcasted_iota(jnp.int32, (FIB, 64), 1)
        group_of = block_of // 4
        slot = route_s[...]
        target = slot // 4
        landing = route_f[...] * 4 + slot % 4
        key = landing * 16 + fibre_of * 4 + block_of % 4
        mine = group_of == me
        for k in range(16):
            here = mine & (target == mate(k))
            low = jnp.min(jnp.where(here, key, 4095))
            high = jnp.max(jnp.where(here, key, 0))
            slot_item[k] = lax.rem(low, 16)
            slot_item[16 + k] = lax.rem(high, 16)
            here = (group_of == mate(k, -1)) & (target == me)
            slot_from[k] = lax.rem(jnp.min(jnp.where(here, key, 4095)), 16)
        code = group_of * 4 + fibre_of
        groups = []
        for i in range(16):
            value = jnp.sum(jnp.where((target == me) & (landing == i), code, 0))
            group = lax.rem(value // 4, WAVE)
            before = jnp.int32(0)
            for other in groups:
                before = before + jnp.where(other == group, 1, 0)
            groups.append(group)
            kz = lax.rem(my_z - group // 8 + 2, 2)
            ky = lax.rem(my_y - lax.rem(group // 2, 4) + 4, 4)
            kc = lax.rem(my_core - lax.rem(group, 2) + 2, 2)
            take[i] = jnp.minimum(before, 1) * 16 + kz * 8 + ky * 2 + kc
            take_fibre[i] = lax.rem(value, 4)

    def fill_slots(k, carry):
        item = slot_from[8 + k]
        source = mate(8 + k, -1)
        for c in range(BLK):
            channel = (source * LOC + lax.rem(item, 4) * BLK + c).astype(F32)
            offset = (math.pi / 2.0) * (2.0 * channel + 1.0 - CH) / CH
            theta = disp[0, lax.div(item, 4)] * (omega * omega + 2.0 * omega * offset)
            sine, cosine = sin_cos(theta)
            slot_fs[k * BLK + c] = sine
            slot_fc[k * BLK + c] = cosine
        return carry

    fill_tables(0)
    for load in loads:
        load.wait()
    plan_switch()
    pl.semaphore_wait(barrier, 19 + 8 * (is_last + is_first))

    def halo_copy(e, side, f):
        group = pl.ds(f * 16, 16)
        if e == 0:
            src = launch.at[group, pl.ds(8, 8) if side == 0 else pl.ds(0, 8)]
        else:
            src = edge.at[e - 1, side, group]
        return pltpu.make_async_remote_copy(
            src_ref=src,
            dst_ref=halo.at[e, side, group],
            send_sem=halo_ss.at[e, side, f],
            recv_sem=halo_rs.at[e, side, f],
            device_id=d_right if side == 0 else d_left,
            device_id_type=MESH,
        )

    def near_copy(e, k):
        return pltpu.make_async_remote_copy(
            src_ref=pack.at[e], dst_ref=near.at[e, k], send_sem=near_ss.at[e, k],
            recv_sem=near_rs.at[e, k], device_id=(mate(k), at), device_id_type=MESH,
        )

    def far_copy(e):
        return pltpu.make_async_remote_copy(
            src_ref=half_sum.at[e], dst_ref=far.at[e], send_sem=far_ss.at[e],
            recv_sem=far_rs.at[e], device_id=(mate(8), at), device_id_type=MESH,
        )

    def side_copy(e, side):
        return pltpu.make_async_remote_copy(
            src_ref=total.at[e], dst_ref=q_side[e].at[side], send_sem=side_ss.at[e, side],
            recv_sem=side_rs.at[e, side], device_id=q_right if side == 0 else q_left,
            device_id_type=MESH,
        )

    def item_copy(j, k):
        early = j == 0 and k >= 8
        return pltpu.make_async_remote_copy(
            src_ref=send_items.at[j, k], dst_ref=first_own.at[k - 8] if early else slot_own.at[16 * j + k],
            send_sem=item_ss.at[j, k], recv_sem=item_rs.at[j, k], device_id=(mate(k), at),
            device_id_type=MESH,
        )

    def first_copy(side, k, straight=False):
        target = right if side == 0 else left
        return pltpu.make_async_remote_copy(
            src_ref=(send_edge if straight else first_edge).at[side, k], dst_ref=first_halo.at[side, k],
            send_sem=first_ss.at[side, k], recv_sem=first_rs.at[side, k],
            device_id=(mate(8 + k) if straight else me, target), device_id_type=MESH,
        )

    def keep_edges(e, f, u):
        group = pl.ds(f * 16, 16)
        edge[e, 0, group], edge[e, 1, group] = edges(u)
        halo_copy(e + 1, 0, f).start()
        halo_copy(e + 1, 1, f).start()

    def turned(parts, channels, e, fibre, gain):
        low = low_rows()
        before, after = q_side[e][0, fibre], q_side[e][1, fibre]
        sums = (
            jnp.where(low, turn(before, 4), before),
            total[e, fibre],
            jnp.where(low, after, turn(after, 4)),
        )
        turns = (rotate_edge, rotate_apart, rotate_edge)
        return jnp.concatenate(
            [
                rule(part.reshape(channels, 2, *part.shape[1:]), q, gain).reshape(part.shape)
                for rule, part, q in zip(turns, parts, sums)
            ],
            axis=1,
        )

    def run_step(e, send_halo):
        span = e // 2

        def body(f, carry):
            group = pl.ds(f * 16, 16)
            halo_copy(e, 0, f).wait_recv()
            halo_copy(e, 1, f).wait_recv()
            parts = [halo[e, 0, group], launch[group] if e == 0 else own[e - 1, group], halo[e, 1, group]]
            if e in (1, 3):
                u = turned(parts, LOC, e - 1, f, nonlin[span, f] * (1.0 / CH))
            else:
                u = jnp.concatenate(parts, axis=1)
            if e == 0:
                channel = me * LOC + lax.broadcasted_iota(jnp.int32, (16, 1, 128), 0) // 2
                u = jnp.where(channel < lit[f], u, 0.0)
            table = pl.ds(f * LOC, LOC)
            result = disperse(
                u, t, "fwd_native" if e == 0 else "fwd_apart", "inv_native" if e == 3 else "inv_apart",
                filt_c[span, table], filt_s[span, table],
            )
            own[e, group] = result
            if send_halo:
                keep_edges(e, f, result)
            both = jnp.sum(result * result, axis=0)
            if e < 3:
                pack[e, f] = both[:8] + both[8:]
            else:
                full = both + swap(both)
                even = even_rows()
                row = f // 2 * 2
                for h in range(2):
                    part = full[h * 8 : h * 8 + 8]
                    old = pack[e, row + h]
                    pack[e, row + h] = jnp.where(even, jnp.where(lax.rem(f, 2) == 0, part, old), part)
            return carry

        lax.fori_loop(0, FIB, body, 0)
        for k in range(1, 8):
            near_copy(e, k).start()

    def gather(step, j, first, last):
        def one(k, carry):
            send_items[j, k] = own[step, pl.ds(slot_item[16 * j + k] * 4, 4)]
            return carry

        lax.fori_loop(first, last, one, 0)

    def straight_edges():
        def one(k, carry):
            send_edge[0, k], send_edge[1, k] = edges(send_items[0, 8 + k])
            return carry

        lax.fori_loop(0, 8, one, 0)
        for side, here in ((0, is_last), (1, is_first)):

            @pl.when(here > 0)
            def _(side=side):
                for k in range(8):
                    first_copy(side, k, True).start()

    def forward_first(k):
        first_edge[0, k], first_edge[1, k] = edges(first_own[k])
        for side, here in ((0, is_last), (1, is_first)):

            @pl.when(here == 0)
            def _(side=side):
                first_copy(side, k).start()

    def first_slots(g, carry):
        blocks = []
        for i in range(4):
            k = g * 4 + i
            first_copy(0, k).wait_recv()
            first_copy(1, k).wait_recv()
            fibre = lax.div(slot_from[8 + k], 4)
            parts = [first_halo[0, k], first_own[k], first_halo[1, k]]
            blocks.append(turned(parts, BLK, 0, fibre, nonlin[0, fibre] * (1.0 / CH)))
        table = pl.ds(g * LOC, LOC)
        result = disperse(
            jnp.concatenate(blocks, axis=0), t, "fwd_apart", "inv_apart", slot_fc[table], slot_fs[table]
        )
        slots = pl.ds(8 + g * 4, 4)
        slot_own[slots] = result.reshape(4, 4, 16, 128)
        return carry

    def finish_near(e):
        acc = pack[e]
        for k in range(1, 8):
            near_copy(e, k).wait_recv()
            acc = acc + near[e, k]
        half_sum[e] = acc
        far_copy(e).start()

    def finish_far(e, sides):
        far_copy(e).wait_recv()
        total[e] = half_sum[e] + far[e]
        if sides:
            side_copy(e, 0).start()
            side_copy(e, 1).start()
            side_copy(e, 0).wait_recv()
            side_copy(e, 1).wait_recv()

    def start_halo(f, carry):
        halo_copy(0, 0, f).start()
        halo_copy(0, 1, f).start()
        return carry

    lax.fori_loop(0, FIB, start_halo, 0)
    fill_tables(1)
    lax.fori_loop(0, 8, fill_slots, 0)
    run_step(0, True)
    gather(0, 0, 8, 16)
    finish_near(0)
    straight_edges()
    for k in range(8, 16):
        item_copy(0, k).start()
    finish_far(0, True)
    run_step(1, False)
    gather(1, 1, 0, 16)
    item_copy(1, 8).start()
    gather(1, 0, 0, 8)
    finish_near(1)
    for k in range(9, 16):
        item_copy(1, k).start()
    for k in range(1, 8):
        item_copy(0, k).start()
        item_copy(1, k).start()
    slot_own[0] = send_items[0, 0]
    slot_own[16] = send_items[1, 0]

    for k in range(8, 16):
        item_copy(0, k).wait_recv()
        forward_first(k - 8)
    lax.fori_loop(0, 2, first_slots, 0)
    finish_far(1, False)
    for k in range(1, 8):
        item_copy(0, k).wait_recv()
    for k in range(1, 16):
        item_copy(1, k).wait_recv()

    def place_fibre(f, carry):
        for i in range(4):
            fibre = take_fibre[f * 4 + i]
            u = slot_own[take[f * 4 + i]].reshape(2, 2, 16, 128)
            u = rotate_apart(u, total[1, fibre], nonlin[0, fibre] * (1.0 / CH))
            own[1, pl.ds(f * 16 + i * 4, 4)] = u.reshape(4, 16, 128)
        keep_edges(1, f, own[1, pl.ds(f * 16, 16)])
        return carry

    lax.fori_loop(0, FIB, place_fibre, 0)

    run_step(2, True)
    finish_near(2)
    finish_far(2, True)
    run_step(3, False)
    finish_near(3)
    finish_far(3, False)

    def store(f):
        group = pl.ds(f * 16, 16)
        return pltpu.make_async_copy(result_buf.at[group], out_hbm.at[group], out_s.at[f])

    def last(f, carry):
        group = pl.ds(f * 16, 16)
        u = own[3, group].reshape(8, 2, 16, 128)
        first, second = unpack_pair(total[3, pl.ds(f // 2 * 2, 2)].reshape(16, 128))
        q = jnp.where(lax.rem(f, 2) == 0, first, second)
        u = rotate_native(u, q, nonlin[1, f] * (1.0 / CH))
        result_buf[group] = u.reshape(16, 16, 128)
        store(f).start()
        return carry

    lax.fori_loop(0, FIB, last, 0)

    def drain_halo(f, carry):
        for e in range(4):
            halo_copy(e, 0, f).wait_send()
            halo_copy(e, 1, f).wait_send()
        return carry

    lax.fori_loop(0, FIB, drain_halo, 0)
    for e in range(4):
        for k in range(1, 8):
            near_copy(e, k).wait_send()
        far_copy(e).wait_send()
    for e in (0, 2):
        side_copy(e, 0).wait_send()
        side_copy(e, 1).wait_send()
    for k in range(1, 16):
        item_copy(0, k).wait_send()
        item_copy(1, k).wait_send()
    for side in range(2):
        for k in range(8):
            first_copy(side, k).wait_send()
    for f in range(FIB):
        store(f).wait()


def local(field, lit_count, route_fibre, route_slot, dispersion, nonlinearity):
    rows = field.reshape(FIB, LOC, 2, 2, 8, 128).transpose(0, 1, 2, 4, 3, 5).reshape(SEQ, 16, 128)
    wide, twist = tables()
    smem = pl.BlockSpec(memory_space=pltpu.SMEM)
    hbm = pl.BlockSpec(memory_space=pltpu.HBM)
    dma = pltpu.SemaphoreType.DMA
    result = pl.pallas_call(
        kernel,
        out_shape=jax.ShapeDtypeStruct((SEQ, 16, 128), F32),
        in_specs=[smem] * 3 + [hbm] * 5,
        out_specs=hbm,
        scratch_shapes=[
            pltpu.VMEM((10, 256, 256), BF16),
            pltpu.VMEM((2, 16, 128), F32),
            pltpu.VMEM((FIB, 64), jnp.int32),
            pltpu.VMEM((FIB, 64), jnp.int32),
            pltpu.VMEM((SEQ, 16, 128), F32),
            pltpu.VMEM((SEQ, 16, 128), F32),
            pltpu.VMEM((2, FIB * LOC, 16, 128), F32),
            pltpu.VMEM((2, FIB * LOC, 16, 128), F32),
            pltpu.VMEM((4, 2, SEQ, 8, 128), F32),
            pltpu.VMEM((4, SEQ, 16, 128), F32),
            pltpu.VMEM((3, 2, SEQ, 8, 128), F32),
            pltpu.VMEM((4, FIB, 8, 128), F32),
            pltpu.VMEM((4, 8, FIB, 8, 128), F32),
            pltpu.VMEM((4, FIB, 8, 128), F32),
            pltpu.VMEM((4, FIB, 8, 128), F32),
            pltpu.VMEM((4, FIB, 8, 128), F32),
            pltpu.VMEM((2, FIB, 8, 128), F32),
            pltpu.VMEM((2, FIB, 8, 128), F32),
            pltpu.VMEM((2, WAVE, 4, 16, 128), F32),
            pltpu.VMEM((2, 8, 4, 8, 128), F32),
            pltpu.VMEM((8, 4, 16, 128), F32),
            pltpu.VMEM((2, 8, 4, 8, 128), F32),
            pltpu.VMEM((2, 8, 4, 8, 128), F32),
            pltpu.VMEM((2 * WAVE, 4, 16, 128), F32),
            pltpu.VMEM((WAVE, 16, 128), F32),
            pltpu.VMEM((WAVE, 16, 128), F32),
            pltpu.SMEM((2 * WAVE,), jnp.int32),
            pltpu.SMEM((WAVE,), jnp.int32),
            pltpu.SMEM((WAVE,), jnp.int32),
            pltpu.SMEM((WAVE,), jnp.int32),
            dma((5,)), dma((FIB,)),
            dma((4, 2, FIB)), dma((4, 2, FIB)),
            dma((4, 8)), dma((4, 8)),
            dma((4,)), dma((4,)),
            dma((4, 2)), dma((4, 2)),
            dma((2, WAVE)), dma((2, WAVE)),
            dma((2, 8)), dma((2, 8)),
        ],
        compiler_params=pltpu.CompilerParams(
            collective_id=0, has_side_effects=True, vmem_limit_bytes=67043328
        ),
        name="propagate",
    )(lit_count, dispersion, nonlinearity, route_fibre, route_slot, rows, wide, twist)
    back = result.reshape(FIB, LOC, 2, 8, 2, 128).transpose(0, 1, 2, 4, 3, 5)
    return back.reshape(FIB, LOC, 2, 2, 1024)


def solution(mesh):
    return jax.shard_map(
        local,
        mesh=mesh,
        in_specs=(P(None, "wave", None, None, "tm"), P(), P(), P(), P(), P()),
        out_specs=P(None, "wave", None, None, "tm"),
        check_vma=False,
    )
```

```python
import functools
import math

import jax
import jax.numpy as jnp
import numpy as np
from jax import lax
from jax.experimental import pallas as pl
from jax.experimental.pallas import tpu as pltpu
from jax.sharding import PartitionSpec as P

CH = 128
FIB = 4
LOC = 8
SEQ = 64
WAVE = 16
TM = 32
MESH = pl.DeviceIdType.MESH
F32 = jnp.float32
BF16 = jnp.bfloat16


def split_table(table):
    high = table.astype(jnp.bfloat16)
    low = (table - high.astype(np.float64)).astype(jnp.bfloat16)
    return high, low


def tables():
    eye = np.eye(8)
    r16 = np.arange(16)
    angle = 2.0 * np.pi * np.outer(r16, r16) / 16.0
    cos_a, sin_a = np.cos(angle), np.sin(angle)
    fwd = np.zeros((2, 16, 16, 2))
    fwd[0, :, :, 0], fwd[0, :, :, 1] = cos_a, sin_a
    fwd[1, :, :, 0], fwd[1, :, :, 1] = -sin_a, cos_a
    native = fwd.reshape(2, 16, 32)
    apart = np.concatenate(
        [
            fwd[:, :, lo:hi].transpose(0, 1, 3, 2).reshape(2, 16, -1)
            for lo, hi in ((0, 4), (4, 12), (12, 16))
        ],
        axis=2,
    )
    fwd_native, fwd_apart = (
        np.einsum("xrq,st->xsrtq", v, eye).reshape(256, 256) for v in (native, apart)
    )
    keep = np.zeros((8, 2, 2, 16))
    kc, ks = cos_a[4:12] / 2048.0, sin_a[4:12] / 2048.0
    keep[:, 0, 0], keep[:, 0, 1] = kc, -ks
    keep[:, 1, 0], keep[:, 1, 1] = ks, kc
    inv_native = np.einsum("apxr,st->sapxtr", keep, eye).reshape(128, 256)
    inv_apart = np.einsum("apxr,st->spaxtr", keep, eye).reshape(128, 256)
    b = np.arange(128)
    angle = 2.0 * np.pi * (np.outer(b, b) % 128) / 128.0
    cos_b, sin_b = np.cos(angle), np.sin(angle)
    col_fwd = np.block([[cos_b, -sin_b], [sin_b, cos_b]])
    col_inv = np.block([[cos_b, sin_b], [-sin_b, cos_b]])
    twist = 2.0 * np.pi * np.outer(r16, b) / 2048.0
    wide = []
    for table in (fwd_native, fwd_apart, col_fwd, col_inv):
        wide.extend(split_table(table))
    for table in (inv_native, inv_apart):
        wide.append(np.concatenate(split_table(table), axis=0))
    twist = np.stack([np.cos(twist), np.sin(twist)]).astype(np.float32)
    return jnp.asarray(np.stack(wide)), jnp.asarray(twist)


def fit(function, terms):
    nodes = np.cos(np.pi * (np.arange(400) + 0.5) / 400) * (np.pi * 1.02)
    square = nodes * nodes
    basis = np.stack([square**k for k in range(terms)], axis=1)
    return [float(v) for v in np.linalg.lstsq(basis, function(nodes), rcond=None)[0]]


SIN_POLY = fit(lambda x: np.sinc(x / np.pi), 7)
COS_POLY = fit(np.cos, 7)
TWO_PI = 2.0 * math.pi
PI_A = float(np.float32(6.28125))
PI_B = float(np.float32(np.round((TWO_PI - PI_A) * 2.0**24) / 2.0**24))
PI_B = float(np.floor((TWO_PI - PI_A) * 2.0**20) / 2.0**20)
PI_C = float(TWO_PI - PI_A - PI_B)


def sin_cos(angle):
    turns = jnp.floor(angle * (1.0 / TWO_PI) + 0.5)
    rest = ((angle - turns * PI_A) - turns * PI_B) - turns * PI_C
    square = rest * rest
    sine = jnp.full_like(square, SIN_POLY[-1])
    for value in SIN_POLY[-2::-1]:
        sine = sine * square + value
    cosine = jnp.full_like(square, COS_POLY[-1])
    for value in COS_POLY[-2::-1]:
        cosine = cosine * square + value
    return sine * rest, cosine


def split(x):
    high = x.astype(BF16)
    low = (x - high.astype(F32)).astype(BF16)
    return high, low


def dot(a, b):
    return jnp.dot(a, b, preferred_element_type=F32)


def left_product(table, data):
    high, low = split(data)
    return dot(table[0][...], high) + (dot(table[1][...], high) + dot(table[0][...], low))


def right_product(data, table):
    high, low = split(data)
    return dot(high, table[0][...]) + (dot(low, table[0][...]) + dot(high, table[1][...]))


def low_rows():
    return lax.broadcasted_iota(jnp.int32, (8, 128), 0) < 4


def even_rows():
    return lax.rem(lax.broadcasted_iota(jnp.int32, (8, 128), 0), 2) == 0


def turn(x, shift):
    return pltpu.roll(x.reshape(-1, 8, 128), shift, 1).reshape(x.shape)


def swap(x):
    t = x.reshape(-1, 8, 128)
    return jnp.where(even_rows()[None], pltpu.roll(t, 7, 1), pltpu.roll(t, 1, 1)).reshape(x.shape)


def unpack_pair(x):
    t = x.reshape(-1, 8, 128)
    even = even_rows()[None]
    first = jnp.where(even, t, pltpu.roll(t, 1, 1)).reshape(x.shape)
    second = jnp.where(even, pltpu.roll(t, 7, 1), t).reshape(x.shape)
    return first, second


def rotate_native(u, total, gain):
    square = u * u
    both = square[:, 0] + square[:, 1]
    phase = gain * (2.0 * total[None] - (both + swap(both)))
    sine, cosine = sin_cos(phase)
    t = sine.reshape(-1, 8, 128)
    signed = jnp.where(even_rows()[None], -t, t).reshape(sine.shape)
    return u * cosine[:, None] + swap(u) * signed[:, None]


def rotate_apart(u, total, gain):
    re, im = u[:, :, :8], u[:, :, 8:]
    square = re * re + im * im
    phase = gain * (2.0 * total[None] - (square[:, 0] + square[:, 1]))
    sine, cosine = sin_cos(phase)
    sine, cosine = sine[:, None], cosine[:, None]
    return jnp.concatenate([re * cosine - im * sine, re * sine + im * cosine], axis=2)


def rotate_edge(u, total, gain):
    square = u * u
    both = square[:, 0] + square[:, 1]
    phase = gain * (2.0 * total[None] - (both + turn(both, 4)))
    sine, cosine = sin_cos(phase)
    signed = jnp.where(low_rows()[None], -sine, sine)
    return u * cosine[:, None] + turn(u, 4) * signed[:, None]


def edges(u):
    re, im = u[..., :8, :], u[..., 8:, :]
    low = low_rows()
    return jnp.where(low, turn(re, 4), im), jnp.where(low, re, turn(im, 4))


def disperse(u, t, fwd, inv, filt_cos, filt_sin):
    eights = u.shape[0] // 8
    rows = u.reshape(eights, 256, 128)
    x = jnp.concatenate([rows[h] for h in range(eights)], axis=1)
    y = left_product(t[fwd], x)
    tc = jnp.broadcast_to(t["twist_cos"][...][None], (8, 16, 128)).reshape(128, 128)
    ts = jnp.broadcast_to(t["twist_sin"][...][None], (8, 16, 128)).reshape(128, 128)
    halves = []
    for h in range(eights):
        re = y[:128, h * 128 : (h + 1) * 128]
        im = y[128:, h * 128 : (h + 1) * 128]
        halves.append(jnp.concatenate([re * tc + im * ts, im * tc - re * ts], axis=1))
    spectrum = right_product(jnp.concatenate(halves, axis=0), t["col_fwd"])
    sr, si = spectrum[:, :128], spectrum[:, 128:]
    channels = eights * 4
    fc = jnp.broadcast_to(filt_cos[:, None], (channels, 2, 16, 128)).reshape(eights * 128, 128)
    fs = jnp.broadcast_to(filt_sin[:, None], (channels, 2, 16, 128)).reshape(eights * 128, 128)
    shaped = jnp.concatenate([sr * fc - si * fs, sr * fs + si * fc], axis=1)
    back = right_product(shaped, t["col_inv"])
    br, bi = back[:, :128], back[:, 128:]
    parts = []
    for h in range(eights):
        re, im = br[h * 128 : (h + 1) * 128], bi[h * 128 : (h + 1) * 128]
        parts.append(jnp.concatenate([re * tc - im * ts, re * ts + im * tc], axis=0))
    out = left_product(t[inv], jnp.concatenate(parts, axis=1))
    return jnp.concatenate([out[:, h * 128 : (h + 1) * 128] for h in range(eights)], axis=0).reshape(
        eights * 8, 16, 128
    )


def kernel(
    lit, disp, nonlin, fibre_hbm, slot_hbm, field_hbm, wide_hbm, twist_hbm,
    out_hbm, total_hbm,
    wide, twist, route_f, route_s, launch,
    filt_c, filt_s, halo, own, edge, pack, near, far, half_sum, total, q_side,
    send_items, recv_items, slot_item, take, take_fibre,
    load_s, out_s,
    halo_ss, halo_rs, near_ss, near_rs, far_ss, far_rs, side_ss, side_rs, item_ss, item_rs, vouch,
):
    t = dict(
        fwd_native=(wide.at[0], wide.at[1]), fwd_apart=(wide.at[2], wide.at[3]),
        col_fwd=(wide.at[4], wide.at[5]), col_inv=(wide.at[6], wide.at[7]),
        inv_native=(wide.at[8, pl.ds(0, 128)], wide.at[8, pl.ds(128, 128)]),
        inv_apart=(wide.at[9, pl.ds(0, 128)], wide.at[9, pl.ds(128, 128)]),
        twist_cos=twist.at[0], twist_sin=twist.at[1],
    )
    me = lax.axis_index("wave")
    at = lax.axis_index("tm")
    my_z = me // 8
    my_y = lax.rem(me // 2, 4)
    my_core = lax.rem(me, 2)
    right = lax.rem(at + 1, TM)
    left = lax.rem(at + TM - 1, TM)

    def mate(k):
        kz, ky, kc = k // 8, (k // 2) % 4, k % 2
        return lax.rem(my_z + kz, 2) * 8 + lax.rem(my_y + ky, 4) * 2 + lax.rem(my_core + kc, 2)

    q_right = (lax.rem(me + 8 * (at // (TM - 1)), WAVE), right)
    q_left = (lax.rem(me + 8 * ((TM - 1 - at) // (TM - 1)), WAVE), left)
    d_right, d_left = (me, right), (me, left)

    barrier = pltpu.get_barrier_semaphore()
    upper = at // 16
    z_up = (lax.rem(me + 8 * upper, WAVE), lax.rem(at + 16, TM))
    z_down = (lax.rem(me + 8 * (1 - upper), WAVE), lax.rem(at + 16, TM))
    for k in range(1, 8):
        pl.semaphore_signal(barrier, inc=1, device_id=(mate(k), at), device_id_type=MESH)
    for target in (d_right, d_left, q_right, q_left, z_up, z_down):
        pl.semaphore_signal(barrier, inc=1, device_id=target, device_id_type=MESH)
    loads = [
        pltpu.make_async_copy(src, dst, load_s.at[i])
        for i, (src, dst) in enumerate(
            ((field_hbm, launch), (wide_hbm, wide), (twist_hbm, twist), (fibre_hbm, route_f), (slot_hbm, route_s))
        )
    ]
    for load in loads:
        load.start()

    r_i = lax.broadcasted_iota(jnp.int32, (16, 128), 0)
    m_i = lax.broadcasted_iota(jnp.int32, (16, 128), 1)
    k_i = r_i + 16 * m_i
    omega = jnp.where(k_i < 1024, k_i, k_i - 2048).astype(F32) * (2.0 * math.pi / 2048.0)

    def fill_tables(span):
        def fill(i, carry):
            channel = (me * LOC + lax.rem(i, LOC)).astype(F32)
            offset = (math.pi / 2.0) * (2.0 * channel + 1.0 - CH) / CH
            theta = disp[span, i // LOC] * (omega * omega + 2.0 * omega * offset)
            sine, cosine = sin_cos(theta)
            filt_s[span, i] = sine
            filt_c[span, i] = cosine
            return carry

        lax.fori_loop(0, FIB * LOC, fill, 0)

    def plan_switch():
        fibre_of = lax.broadcasted_iota(jnp.int32, (FIB, 64), 0)
        block_of = lax.broadcasted_iota(jnp.int32, (FIB, 64), 1)
        group_of = block_of // 4
        slot = route_s[...]
        target = slot // 4
        landing = route_f[...] * 4 + slot % 4
        key = landing * 16 + fibre_of * 4 + block_of % 4
        mine = group_of == me
        for k in range(16):
            here = mine & (target == mate(k))
            low = jnp.min(jnp.where(here, key, 4095))
            high = jnp.max(jnp.where(here, key, 0))
            slot_item[2 * k] = lax.rem(low, 16)
            slot_item[2 * k + 1] = lax.rem(high, 16)
        code = group_of * 4 + fibre_of
        groups = []
        for i in range(16):
            value = jnp.sum(jnp.where((target == me) & (landing == i), code, 0))
            group = lax.rem(value // 4, WAVE)
            before = jnp.int32(0)
            for other in groups:
                before = before + jnp.where(other == group, 1, 0)
            groups.append(group)
            kz = lax.rem(my_z - group // 8 + 2, 2)
            ky = lax.rem(my_y - lax.rem(group // 2, 4) + 4, 4)
            kc = lax.rem(my_core - lax.rem(group, 2) + 2, 2)
            take[i] = (kz * 8 + ky * 2 + kc) * 2 + jnp.minimum(before, 1)
            take_fibre[i] = lax.rem(value, 4)

    fill_tables(0)
    for load in loads:
        load.wait()
    pl.semaphore_wait(barrier, 13)
    pl.semaphore_signal(vouch.at[0], inc=1, device_id=z_up, device_id_type=MESH)

    def halo_copy(e, side, f):
        group = pl.ds(f * 16, 16)
        if e == 0:
            src = launch.at[group, pl.ds(8, 8) if side == 0 else pl.ds(0, 8)]
        else:
            src = edge.at[e - 1, side, group]
        return pltpu.make_async_remote_copy(
            src_ref=src,
            dst_ref=halo.at[e, side, group],
            send_sem=halo_ss.at[e, side, f],
            recv_sem=halo_rs.at[e, side, f],
            device_id=d_right if side == 0 else d_left,
            device_id_type=MESH,
        )

    def near_copy(e, k):
        return pltpu.make_async_remote_copy(
            src_ref=pack.at[e], dst_ref=near.at[e, k], send_sem=near_ss.at[e, k],
            recv_sem=near_rs.at[e, k], device_id=(mate(k), at), device_id_type=MESH,
        )

    def far_copy(e):
        return pltpu.make_async_remote_copy(
            src_ref=half_sum.at[e], dst_ref=far.at[e], send_sem=far_ss.at[e],
            recv_sem=far_rs.at[e], device_id=(mate(8), at), device_id_type=MESH,
        )

    def side_copy(e, side):
        return pltpu.make_async_remote_copy(
            src_ref=total.at[e], dst_ref=q_side.at[e, side], send_sem=side_ss.at[e, side],
            recv_sem=side_rs.at[e, side], device_id=q_right if side == 0 else q_left,
            device_id_type=MESH,
        )

    def item_copy(k):
        return pltpu.make_async_remote_copy(
            src_ref=send_items.at[pl.ds(2 * k, 2)], dst_ref=recv_items.at[pl.ds(2 * k, 2)],
            send_sem=item_ss.at[k], recv_sem=item_rs.at[k], device_id=(mate(k), at),
            device_id_type=MESH,
        )

    def keep_edges(e, f, u):
        group = pl.ds(f * 16, 16)
        edge[e, 0, group], edge[e, 1, group] = edges(u)
        halo_copy(e + 1, 0, f).start()
        halo_copy(e + 1, 1, f).start()

    def run_step(e, send_halo):
        span = e // 2

        def fetch(f):
            halo_copy(e, 0, f).wait_recv()
            halo_copy(e, 1, f).wait_recv()
            group = pl.ds(f * 16, 16)
            parts = [halo[e, 0, group], launch[group] if e == 0 else own[e - 1, group], halo[e, 1, group]]
            if e in (1, 3):
                gain = nonlin[span, f] * (1.0 / CH)
                low = low_rows()
                before, after = q_side[e - 1, 0, f], q_side[e - 1, 1, f]
                sums = (
                    jnp.where(low, turn(before, 4), before),
                    total[e - 1, f],
                    jnp.where(low, after, turn(after, 4)),
                )
                turns = (rotate_edge, rotate_apart, rotate_edge)
                parts = [
                    rule(part.reshape(8, 2, *part.shape[1:]), q, gain).reshape(part.shape)
                    for rule, part, q in zip(turns, parts, sums)
                ]
            u = jnp.concatenate(parts, axis=1)
            if e == 0:
                channel = me * LOC + lax.broadcasted_iota(jnp.int32, (16, 1, 128), 0) // 2
                u = jnp.where(channel < lit[f], u, 0.0)
            return u

        def keep(f, result):
            own[e, pl.ds(f * 16, 16)] = result
            if send_halo:
                keep_edges(e, f, result)
            both = jnp.sum(result * result, axis=0)
            return both[:8] + both[8:] if e < 3 else both + swap(both)

        fwd = "fwd_native" if e == 0 else "fwd_apart"
        inv = "inv_native" if e == 3 else "inv_apart"
        if e in (1, 3):
            u = jnp.concatenate([fetch(f) for f in range(FIB)], axis=0)
            result = disperse(u, t, fwd, inv, filt_c[span], filt_s[span])
            powers = [keep(f, result[f * 16 : f * 16 + 16]) for f in range(FIB)]
            for f in range(FIB):
                if e == 1:
                    pack[e, f] = powers[f]
                else:
                    j, h = f // 2 * 2, f % 2
                    rows = slice(h * 8, h * 8 + 8)
                    pack[e, f] = jnp.where(even_rows(), powers[j][rows], powers[j + 1][rows])
        else:

            def body(f, carry):
                table = pl.ds(f * LOC, LOC)
                pack[e, f] = keep(f, disperse(fetch(f), t, fwd, inv, filt_c[span, table], filt_s[span, table]))
                return carry

            lax.fori_loop(0, FIB, body, 0)
        for k in range(1, 8):
            near_copy(e, k).start()

    def finish_near(e):
        acc = pack[e]
        for k in range(1, 8):
            near_copy(e, k).wait_recv()
            acc = acc + near[e, k]
        half_sum[e] = acc
        far_copy(e).start()

    def finish_far(e, sides):
        far_copy(e).wait_recv()
        total[e] = half_sum[e] + far[e]
        if sides:
            side_copy(e, 0).start()
            side_copy(e, 1).start()
            side_copy(e, 0).wait_recv()
            side_copy(e, 1).wait_recv()

    def start_halo(f, carry):
        halo_copy(0, 0, f).start()
        halo_copy(0, 1, f).start()
        return carry

    lax.fori_loop(0, FIB, start_halo, 0)
    fill_tables(1)
    plan_switch()
    pl.semaphore_wait(vouch.at[0], 1)
    pl.semaphore_signal(vouch.at[1], inc=1, device_id=z_up, device_id_type=MESH)
    run_step(0, True)
    pl.semaphore_wait(vouch.at[1], 1)
    finish_near(0)
    finish_far(0, True)
    run_step(1, False)

    def gather(s, carry):
        send_items[s] = own[1, pl.ds(slot_item[s] * 4, 4)]
        return carry

    lax.fori_loop(WAVE, 2 * WAVE, gather, 0)
    for k in (8, 9, 10, 11, 12, 13):
        item_copy(k).start()
    lax.fori_loop(0, WAVE, gather, 0)
    for k in (1, 2, 3, 4, 5, 6, 7):
        item_copy(k).start()
    recv_items[0:2] = send_items[0:2]
    finish_near(1)
    for k in (14, 15):
        item_copy(k).start()
    finish_far(1, False)
    for k in range(1, 16):
        item_copy(k).wait_recv()

    def place(i, carry):
        fibre = take_fibre[i]
        u = recv_items[take[i]].reshape(2, 2, 16, 128)
        u = rotate_apart(u, total[1, fibre], nonlin[0, fibre] * (1.0 / CH))
        own[1, pl.ds(i * 4, 4)] = u.reshape(4, 16, 128)
        return carry

    def place_fibre(f, carry):
        for i in range(4):
            place(f * 4 + i, carry)
        keep_edges(1, f, own[1, pl.ds(f * 16, 16)])
        return carry

    lax.fori_loop(0, FIB, place_fibre, 0)

    run_step(2, True)
    finish_near(2)
    finish_far(2, True)
    run_step(3, False)
    result_store = pltpu.make_async_copy(own.at[3], out_hbm, out_s.at[0])
    result_store.start()
    finish_near(3)
    finish_far(3, False)
    total_store = pltpu.make_async_copy(total.at[3], total_hbm, out_s.at[1])
    total_store.start()

    def drain_halo(f, carry):
        for e in range(4):
            halo_copy(e, 0, f).wait_send()
            halo_copy(e, 1, f).wait_send()
        return carry

    lax.fori_loop(0, FIB, drain_halo, 0)
    for e in range(4):
        for k in range(1, 8):
            near_copy(e, k).wait_send()
        far_copy(e).wait_send()
    for e in (0, 2):
        side_copy(e, 0).wait_send()
        side_copy(e, 1).wait_send()
    for k in range(1, 16):
        item_copy(k).wait_send()
    result_store.wait()
    total_store.wait()


def last_phase(nonlin, own, total, out):
    f = pl.program_id(0)
    first, second = unpack_pair(total[...].reshape(16, 128))
    q = jnp.where(lax.rem(f, 2) == 0, first, second)
    u = rotate_native(own[...].reshape(8, 2, 16, 128), q, nonlin[1, f] * (1.0 / CH))
    out[...] = u.reshape(16, 16, 128)


def local(field, lit_count, route_fibre, route_slot, dispersion, nonlinearity):
    rows = field.reshape(FIB, LOC, 2, 2, 8, 128).transpose(0, 1, 2, 4, 3, 5).reshape(SEQ, 16, 128)
    wide, twist = tables()
    smem = pl.BlockSpec(memory_space=pltpu.SMEM)
    hbm = pl.BlockSpec(memory_space=pltpu.HBM)
    dma = pltpu.SemaphoreType.DMA
    field_out, total_out = pl.pallas_call(
        kernel,
        out_shape=[
            jax.ShapeDtypeStruct((SEQ, 16, 128), F32),
            jax.ShapeDtypeStruct((FIB, 8, 128), F32),
        ],
        in_specs=[smem] * 3 + [hbm] * 5,
        out_specs=[hbm, hbm],
        scratch_shapes=[
            pltpu.VMEM((10, 256, 256), BF16),
            pltpu.VMEM((2, 16, 128), F32),
            pltpu.VMEM((FIB, 64), jnp.int32),
            pltpu.VMEM((FIB, 64), jnp.int32),
            pltpu.VMEM((SEQ, 16, 128), F32),
            pltpu.VMEM((2, FIB * LOC, 16, 128), F32),
            pltpu.VMEM((2, FIB * LOC, 16, 128), F32),
            pltpu.VMEM((4, 2, SEQ, 8, 128), F32),
            pltpu.VMEM((4, SEQ, 16, 128), F32),
            pltpu.VMEM((3, 2, SEQ, 8, 128), F32),
            pltpu.VMEM((4, FIB, 8, 128), F32),
            pltpu.VMEM((4, 8, FIB, 8, 128), F32),
            pltpu.VMEM((4, FIB, 8, 128), F32),
            pltpu.VMEM((4, FIB, 8, 128), F32),
            pltpu.VMEM((4, FIB, 8, 128), F32),
            pltpu.VMEM((4, 2, FIB, 8, 128), F32),
            pltpu.VMEM((2 * WAVE, 4, 16, 128), F32),
            pltpu.VMEM((2 * WAVE, 4, 16, 128), F32),
            pltpu.SMEM((2 * WAVE,), jnp.int32),
            pltpu.SMEM((WAVE,), jnp.int32),
            pltpu.SMEM((WAVE,), jnp.int32),
            dma((5,)), dma((2,)),
            dma((4, 2, FIB)), dma((4, 2, FIB)),
            dma((4, 8)), dma((4, 8)),
            dma((4,)), dma((4,)),
            dma((4, 2)), dma((4, 2)),
            dma((WAVE,)), dma((WAVE,)), pltpu.SemaphoreType.REGULAR((2,)),
        ],
        compiler_params=pltpu.CompilerParams(
            collective_id=0, has_side_effects=True, vmem_limit_bytes=67043328
        ),
        name="propagate",
    )(lit_count, dispersion, nonlinearity, route_fibre, route_slot, rows, wide, twist)
    block = pl.BlockSpec((16, 16, 128), lambda f: (f, 0, 0))
    result = pl.pallas_call(
        last_phase,
        grid=(FIB,),
        out_shape=jax.ShapeDtypeStruct((SEQ, 16, 128), F32),
        in_specs=[smem, block, pl.BlockSpec((2, 8, 128), lambda f: (f // 2, 0, 0))],
        out_specs=block,
        name="last_phase",
    )(nonlinearity, field_out, total_out)
    back = result.reshape(FIB, LOC, 2, 8, 2, 128).transpose(0, 1, 2, 4, 3, 5)
    return back.reshape(FIB, LOC, 2, 2, 1024)


def solution(mesh):
    return jax.shard_map(
        local,
        mesh=mesh,
        in_specs=(P(None, "wave", None, None, "tm"), P(), P(), P(), P(), P()),
        out_specs=P(None, "wave", None, None, "tm"),
        check_vma=False,
    )
```

```python
import functools
import math

import jax
import jax.numpy as jnp
import numpy as np
from jax import lax
from jax.experimental import pallas as pl
from jax.experimental.pallas import tpu as pltpu
from jax.sharding import PartitionSpec as P

CH = 128
FIB = 4
LOC = 8
SEQ = 64
WAVE = 16
TM = 32
MESH = pl.DeviceIdType.MESH
F32 = jnp.float32
BF16 = jnp.bfloat16


def split_table(table):
    high = table.astype(jnp.bfloat16)
    low = (table - high.astype(np.float64)).astype(jnp.bfloat16)
    return high, low


def tables():
    eye = np.eye(8)
    r16 = np.arange(16)
    angle = 2.0 * np.pi * np.outer(r16, r16) / 16.0
    cos_a, sin_a = np.cos(angle), np.sin(angle)
    fwd = np.zeros((2, 16, 16, 2))
    fwd[0, :, :, 0], fwd[0, :, :, 1] = cos_a, sin_a
    fwd[1, :, :, 0], fwd[1, :, :, 1] = -sin_a, cos_a
    native = fwd.reshape(2, 16, 32)
    apart = np.concatenate(
        [
            fwd[:, :, lo:hi].transpose(0, 1, 3, 2).reshape(2, 16, -1)
            for lo, hi in ((0, 4), (4, 12), (12, 16))
        ],
        axis=2,
    )
    fwd_native, fwd_apart = (
        np.einsum("xrq,st->xsrtq", v, eye).reshape(256, 256) for v in (native, apart)
    )
    keep = np.zeros((8, 2, 2, 16))
    kc, ks = cos_a[4:12] / 2048.0, sin_a[4:12] / 2048.0
    keep[:, 0, 0], keep[:, 0, 1] = kc, -ks
    keep[:, 1, 0], keep[:, 1, 1] = ks, kc
    inv_native = np.einsum("apxr,st->sapxtr", keep, eye).reshape(128, 256)
    inv_apart = np.einsum("apxr,st->spaxtr", keep, eye).reshape(128, 256)
    b = np.arange(128)
    angle = 2.0 * np.pi * (np.outer(b, b) % 128) / 128.0
    cos_b, sin_b = np.cos(angle), np.sin(angle)
    col_fwd = np.block([[cos_b, -sin_b], [sin_b, cos_b]])
    col_inv = np.block([[cos_b, sin_b], [-sin_b, cos_b]])
    twist = 2.0 * np.pi * np.outer(r16, b) / 2048.0
    wide = []
    for table in (fwd_native, fwd_apart, col_fwd, col_inv):
        wide.extend(split_table(table))
    for table in (inv_native, inv_apart):
        wide.append(np.concatenate(split_table(table), axis=0))
    twist = np.stack([np.cos(twist), np.sin(twist)]).astype(np.float32)
    return jnp.asarray(np.stack(wide)), jnp.asarray(twist)


def fit(function, terms):
    nodes = np.cos(np.pi * (np.arange(400) + 0.5) / 400) * (np.pi * 1.02)
    square = nodes * nodes
    basis = np.stack([square**k for k in range(terms)], axis=1)
    return [float(v) for v in np.linalg.lstsq(basis, function(nodes), rcond=None)[0]]


SIN_POLY = fit(lambda x: np.sinc(x / np.pi), 7)
COS_POLY = fit(np.cos, 7)
TWO_PI = 2.0 * math.pi
PI_A = float(np.float32(6.28125))
PI_B = float(np.float32(np.round((TWO_PI - PI_A) * 2.0**24) / 2.0**24))
PI_B = float(np.floor((TWO_PI - PI_A) * 2.0**20) / 2.0**20)
PI_C = float(TWO_PI - PI_A - PI_B)


def sin_cos(angle):
    turns = jnp.floor(angle * (1.0 / TWO_PI) + 0.5)
    rest = ((angle - turns * PI_A) - turns * PI_B) - turns * PI_C
    square = rest * rest
    sine = jnp.full_like(square, SIN_POLY[-1])
    for value in SIN_POLY[-2::-1]:
        sine = sine * square + value
    cosine = jnp.full_like(square, COS_POLY[-1])
    for value in COS_POLY[-2::-1]:
        cosine = cosine * square + value
    return sine * rest, cosine


def split(x):
    high = x.astype(BF16)
    low = (x - high.astype(F32)).astype(BF16)
    return high, low


def dot(a, b):
    return jnp.dot(a, b, preferred_element_type=F32)


def left_product(table, data):
    high, low = split(data)
    return dot(table[0][...], high) + (dot(table[1][...], high) + dot(table[0][...], low))


def right_product(data, table):
    high, low = split(data)
    return dot(high, table[0][...]) + (dot(low, table[0][...]) + dot(high, table[1][...]))


def low_rows():
    return lax.broadcasted_iota(jnp.int32, (8, 128), 0) < 4


def even_rows():
    return lax.rem(lax.broadcasted_iota(jnp.int32, (8, 128), 0), 2) == 0


def turn(x, shift):
    return pltpu.roll(x.reshape(-1, 8, 128), shift, 1).reshape(x.shape)


def swap(x):
    t = x.reshape(-1, 8, 128)
    return jnp.where(even_rows()[None], pltpu.roll(t, 7, 1), pltpu.roll(t, 1, 1)).reshape(x.shape)


def unpack_pair(x):
    t = x.reshape(-1, 8, 128)
    even = even_rows()[None]
    first = jnp.where(even, t, pltpu.roll(t, 1, 1)).reshape(x.shape)
    second = jnp.where(even, pltpu.roll(t, 7, 1), t).reshape(x.shape)
    return first, second


def rotate_native(u, total, gain):
    square = u * u
    both = square[:, 0] + square[:, 1]
    phase = gain * (2.0 * total[None] - (both + swap(both)))
    sine, cosine = sin_cos(phase)
    t = sine.reshape(-1, 8, 128)
    signed = jnp.where(even_rows()[None], -t, t).reshape(sine.shape)
    return u * cosine[:, None] + swap(u) * signed[:, None]


def rotate_apart(u, total, gain):
    re, im = u[:, :, :8], u[:, :, 8:]
    square = re * re + im * im
    phase = gain * (2.0 * total[None] - (square[:, 0] + square[:, 1]))
    sine, cosine = sin_cos(phase)
    sine, cosine = sine[:, None], cosine[:, None]
    return jnp.concatenate([re * cosine - im * sine, re * sine + im * cosine], axis=2)


def rotate_edge(u, total, gain):
    square = u * u
    both = square[:, 0] + square[:, 1]
    phase = gain * (2.0 * total[None] - (both + turn(both, 4)))
    sine, cosine = sin_cos(phase)
    signed = jnp.where(low_rows()[None], -sine, sine)
    return u * cosine[:, None] + turn(u, 4) * signed[:, None]


def edges(u):
    re, im = u[..., :8, :], u[..., 8:, :]
    low = low_rows()
    return jnp.where(low, turn(re, 4), im), jnp.where(low, re, turn(im, 4))


def disperse(u, t, fwd, inv, filt_cos, filt_sin):
    eights = u.shape[0] // 8
    rows = u.reshape(eights, 256, 128)
    x = jnp.concatenate([rows[h] for h in range(eights)], axis=1)
    y = left_product(t[fwd], x)
    tc = jnp.broadcast_to(t["twist_cos"][...][None], (8, 16, 128)).reshape(128, 128)
    ts = jnp.broadcast_to(t["twist_sin"][...][None], (8, 16, 128)).reshape(128, 128)
    halves = []
    for h in range(eights):
        re = y[:128, h * 128 : (h + 1) * 128]
        im = y[128:, h * 128 : (h + 1) * 128]
        halves.append(jnp.concatenate([re * tc + im * ts, im * tc - re * ts], axis=1))
    spectrum = right_product(jnp.concatenate(halves, axis=0), t["col_fwd"])
    sr, si = spectrum[:, :128], spectrum[:, 128:]
    channels = eights * 4
    fc = jnp.broadcast_to(filt_cos[:, None], (channels, 2, 16, 128)).reshape(eights * 128, 128)
    fs = jnp.broadcast_to(filt_sin[:, None], (channels, 2, 16, 128)).reshape(eights * 128, 128)
    shaped = jnp.concatenate([sr * fc - si * fs, sr * fs + si * fc], axis=1)
    back = right_product(shaped, t["col_inv"])
    br, bi = back[:, :128], back[:, 128:]
    parts = []
    for h in range(eights):
        re, im = br[h * 128 : (h + 1) * 128], bi[h * 128 : (h + 1) * 128]
        parts.append(jnp.concatenate([re * tc - im * ts, re * ts + im * tc], axis=0))
    out = left_product(t[inv], jnp.concatenate(parts, axis=1))
    return jnp.concatenate([out[:, h * 128 : (h + 1) * 128] for h in range(eights)], axis=0).reshape(
        eights * 8, 16, 128
    )


def kernel(
    lit, disp, nonlin, fibre_hbm, slot_hbm, field_hbm, wide_hbm, twist_hbm,
    out_hbm,
    wide, twist, route_f, route_s, launch, result_buf,
    filt_c, filt_s, halo, own, edge, pack, near, far, half_sum, total, q_side,
    send_items, recv_items, slot_item, take, take_fibre,
    load_s, out_s,
    halo_ss, halo_rs, near_ss, near_rs, far_ss, far_rs, side_ss, side_rs, item_ss, item_rs, vouch, column,
):
    t = dict(
        fwd_native=(wide.at[0], wide.at[1]), fwd_apart=(wide.at[2], wide.at[3]),
        col_fwd=(wide.at[4], wide.at[5]), col_inv=(wide.at[6], wide.at[7]),
        inv_native=(wide.at[8, pl.ds(0, 128)], wide.at[8, pl.ds(128, 128)]),
        inv_apart=(wide.at[9, pl.ds(0, 128)], wide.at[9, pl.ds(128, 128)]),
        twist_cos=twist.at[0], twist_sin=twist.at[1],
    )
    me = lax.axis_index("wave")
    at = lax.axis_index("tm")
    my_z = me // 8
    my_y = lax.rem(me // 2, 4)
    my_core = lax.rem(me, 2)
    right = lax.rem(at + 1, TM)
    left = lax.rem(at + TM - 1, TM)

    def mate(k):
        kz, ky, kc = k // 8, (k // 2) % 4, k % 2
        return lax.rem(my_z + kz, 2) * 8 + lax.rem(my_y + ky, 4) * 2 + lax.rem(my_core + kc, 2)

    q_right = (lax.rem(me + 8 * (at // (TM - 1)), WAVE), right)
    q_left = (lax.rem(me + 8 * ((TM - 1 - at) // (TM - 1)), WAVE), left)
    d_right, d_left = (me, right), (me, left)

    barrier = pltpu.get_barrier_semaphore()
    upper = at // 16
    z_up = (lax.rem(me + 8 * upper, WAVE), lax.rem(at + 16, TM))
    z_down = (lax.rem(me + 8 * (1 - upper), WAVE), lax.rem(at + 16, TM))
    for k in range(1, 8):
        pl.semaphore_signal(barrier, inc=1, device_id=(mate(k), at), device_id_type=MESH)
    my_high = my_z * 8 + at // 4

    def along_z(step):
        high = lax.rem(my_high + step + 16, 16)
        return (lax.div(high, 8) * 8 + lax.rem(me, 8), lax.rem(high, 8) * 4 + lax.rem(at, 4))

    first_round = [along_z(step) for step in (-5, 5)]
    second_round = [along_z(step) for step in (-2, -1, 1, 2, 3)]
    answers = [along_z(-3)]
    for target in (d_right, d_left, q_right, q_left, z_up, z_down, *first_round, *second_round, *answers):
        pl.semaphore_signal(barrier, inc=1, device_id=target, device_id_type=MESH)
    loads = [
        pltpu.make_async_copy(src, dst, load_s.at[i])
        for i, (src, dst) in enumerate(
            ((field_hbm, launch), (wide_hbm, wide), (twist_hbm, twist), (fibre_hbm, route_f), (slot_hbm, route_s))
        )
    ]
    for load in loads:
        load.start()

    r_i = lax.broadcasted_iota(jnp.int32, (16, 128), 0)
    m_i = lax.broadcasted_iota(jnp.int32, (16, 128), 1)
    k_i = r_i + 16 * m_i
    omega = jnp.where(k_i < 1024, k_i, k_i - 2048).astype(F32) * (2.0 * math.pi / 2048.0)

    def fill_tables(span):
        def fill(i, carry):
            channel = (me * LOC + lax.rem(i, LOC)).astype(F32)
            offset = (math.pi / 2.0) * (2.0 * channel + 1.0 - CH) / CH
            theta = disp[span, i // LOC] * (omega * omega + 2.0 * omega * offset)
            sine, cosine = sin_cos(theta)
            filt_s[span, i] = sine
            filt_c[span, i] = cosine
            return carry

        lax.fori_loop(0, FIB * LOC, fill, 0)

    def plan_switch():
        fibre_of = lax.broadcasted_iota(jnp.int32, (FIB, 64), 0)
        block_of = lax.broadcasted_iota(jnp.int32, (FIB, 64), 1)
        group_of = block_of // 4
        slot = route_s[...]
        target = slot // 4
        landing = route_f[...] * 4 + slot % 4
        key = landing * 16 + fibre_of * 4 + block_of % 4
        mine = group_of == me
        for k in range(16):
            here = mine & (target == mate(k))
            low = jnp.min(jnp.where(here, key, 4095))
            high = jnp.max(jnp.where(here, key, 0))
            slot_item[2 * k] = lax.rem(low, 16)
            slot_item[2 * k + 1] = lax.rem(high, 16)
        code = group_of * 4 + fibre_of
        groups = []
        for i in range(16):
            value = jnp.sum(jnp.where((target == me) & (landing == i), code, 0))
            group = lax.rem(value // 4, WAVE)
            before = jnp.int32(0)
            for other in groups:
                before = before + jnp.where(other == group, 1, 0)
            groups.append(group)
            kz = lax.rem(my_z - group // 8 + 2, 2)
            ky = lax.rem(my_y - lax.rem(group // 2, 4) + 4, 4)
            kc = lax.rem(my_core - lax.rem(group, 2) + 2, 2)
            take[i] = (kz * 8 + ky * 2 + kc) * 2 + jnp.minimum(before, 1)
            take_fibre[i] = lax.rem(value, 4)

    fill_tables(0)
    for load in loads:
        load.wait()
    pl.semaphore_wait(barrier, 21)
    pl.semaphore_signal(vouch.at[0], inc=1, device_id=z_up, device_id_type=MESH)

    def halo_copy(e, side, f):
        group = pl.ds(f * 16, 16)
        if e == 0:
            src = launch.at[group, pl.ds(8, 8) if side == 0 else pl.ds(0, 8)]
        else:
            src = edge.at[e - 1, side, group]
        return pltpu.make_async_remote_copy(
            src_ref=src,
            dst_ref=halo.at[e, side, group],
            send_sem=halo_ss.at[e, side, f],
            recv_sem=halo_rs.at[e, side, f],
            device_id=d_right if side == 0 else d_left,
            device_id_type=MESH,
        )

    def near_copy(e, k):
        return pltpu.make_async_remote_copy(
            src_ref=pack.at[e], dst_ref=near.at[e, k], send_sem=near_ss.at[e, k],
            recv_sem=near_rs.at[e, k], device_id=(mate(k), at), device_id_type=MESH,
        )

    def far_copy(e):
        return pltpu.make_async_remote_copy(
            src_ref=half_sum.at[e], dst_ref=far.at[e], send_sem=far_ss.at[e],
            recv_sem=far_rs.at[e], device_id=(mate(8), at), device_id_type=MESH,
        )

    def side_copy(e, side):
        return pltpu.make_async_remote_copy(
            src_ref=total.at[e], dst_ref=q_side.at[e, side], send_sem=side_ss.at[e, side],
            recv_sem=side_rs.at[e, side], device_id=q_right if side == 0 else q_left,
            device_id_type=MESH,
        )

    def item_copy(k):
        return pltpu.make_async_remote_copy(
            src_ref=send_items.at[pl.ds(2 * k, 2)], dst_ref=recv_items.at[pl.ds(2 * k, 2)],
            send_sem=item_ss.at[k], recv_sem=item_rs.at[k], device_id=(mate(k), at),
            device_id_type=MESH,
        )

    def keep_edges(e, f, u):
        group = pl.ds(f * 16, 16)
        edge[e, 0, group], edge[e, 1, group] = edges(u)
        halo_copy(e + 1, 0, f).start()
        halo_copy(e + 1, 1, f).start()

    def run_step(e, send_halo):
        span = e // 2

        def fetch(f):
            halo_copy(e, 0, f).wait_recv()
            halo_copy(e, 1, f).wait_recv()
            group = pl.ds(f * 16, 16)
            middle = launch[group] if e == 0 else own[e - 1, group]
            u = jnp.concatenate([halo[e, 0, group], middle, halo[e, 1, group]], axis=1)
            if e == 0:
                channel = me * LOC + lax.broadcasted_iota(jnp.int32, (16, 1, 128), 0) // 2
                u = jnp.where(channel < lit[f], u, 0.0)
            return u

        def turned(rule, part, f, q):
            gain = nonlin[span, f] * (1.0 / CH)
            return rule(part.reshape(8, 2, *part.shape[1:]), q, gain).reshape(part.shape)

        def fetch_turned():
            middle = []
            for f in range(FIB):
                middle.append(turned(rotate_apart, own[e - 1, pl.ds(f * 16, 16)], f, total[e - 1, f]))
            side_copy(e - 1, 0).wait_recv()
            side_copy(e - 1, 1).wait_recv()
            if e == 1:
                pl.semaphore_wait(column.at[0], 2)
                for target in second_round:
                    pl.semaphore_signal(column.at[1], inc=1, device_id=target, device_id_type=MESH)
            low = low_rows()
            parts = []
            for f in range(FIB):
                group = pl.ds(f * 16, 16)
                before, after = q_side[e - 1, 0, f], q_side[e - 1, 1, f]
                halo_copy(e, 0, f).wait_recv()
                halo_copy(e, 1, f).wait_recv()
                parts.append(
                    jnp.concatenate(
                        [
                            turned(rotate_edge, halo[e, 0, group], f, jnp.where(low, turn(before, 4), before)),
                            middle[f],
                            turned(rotate_edge, halo[e, 1, group], f, jnp.where(low, after, turn(after, 4))),
                        ],
                        axis=1,
                    )
                )
            return jnp.concatenate(parts, axis=0)

        def keep(f, result):
            own[e, pl.ds(f * 16, 16)] = result
            if send_halo:
                keep_edges(e, f, result)
            both = jnp.sum(result * result, axis=0)
            return both[:8] + both[8:] if e < 3 else both + swap(both)

        fwd = "fwd_native" if e == 0 else "fwd_apart"
        inv = "inv_native" if e == 3 else "inv_apart"
        if e in (1, 3):
            result = disperse(fetch_turned(), t, fwd, inv, filt_c[span], filt_s[span])
            powers = [keep(f, result[f * 16 : f * 16 + 16]) for f in range(FIB)]
            for f in range(FIB):
                if e == 1:
                    pack[e, f] = powers[f]
                else:
                    j, h = f // 2 * 2, f % 2
                    rows = slice(h * 8, h * 8 + 8)
                    pack[e, f] = jnp.where(even_rows(), powers[j][rows], powers[j + 1][rows])
        else:

            def body(f, carry):
                table = pl.ds(f * LOC, LOC)
                pack[e, f] = keep(f, disperse(fetch(f), t, fwd, inv, filt_c[span, table], filt_s[span, table]))
                return carry

            lax.fori_loop(0, FIB, body, 0)
        for k in range(1, 8):
            near_copy(e, k).start()

    def finish_near(e):
        acc = pack[e]
        for k in range(1, 8):
            near_copy(e, k).wait_recv()
            acc = acc + near[e, k]
        half_sum[e] = acc
        far_copy(e).start()

    def finish_far(e, sides):
        far_copy(e).wait_recv()
        total[e] = half_sum[e] + far[e]
        if e == 0:
            for target in first_round:
                pl.semaphore_signal(column.at[0], inc=1, device_id=target, device_id_type=MESH)
        if sides:
            side_copy(e, 0).start()
            side_copy(e, 1).start()

    def start_halo(f, carry):
        halo_copy(0, 0, f).start()
        halo_copy(0, 1, f).start()
        return carry

    lax.fori_loop(0, FIB, start_halo, 0)
    fill_tables(1)
    plan_switch()
    pl.semaphore_wait(vouch.at[0], 1)
    pl.semaphore_signal(vouch.at[1], inc=1, device_id=z_up, device_id_type=MESH)
    run_step(0, True)
    pl.semaphore_wait(vouch.at[1], 1)
    finish_near(0)
    finish_far(0, True)
    run_step(1, False)

    def gather(s, carry):
        send_items[s] = own[1, pl.ds(slot_item[s] * 4, 4)]
        return carry

    lax.fori_loop(WAVE, 2 * WAVE, gather, 0)
    pl.semaphore_wait(column.at[1], 5)
    for k in (8, 9, 10, 11, 12, 13):
        item_copy(k).start()
    lax.fori_loop(0, WAVE, gather, 0)
    for k in (1, 2, 3, 4, 5, 6, 7):
        item_copy(k).start()
    recv_items[0:2] = send_items[0:2]
    finish_near(1)
    for k in (14, 15):
        item_copy(k).start()
    finish_far(1, False)
    for k in range(1, 16):
        item_copy(k).wait_recv()

    def place(i, carry):
        fibre = take_fibre[i]
        u = recv_items[take[i]].reshape(2, 2, 16, 128)
        u = rotate_apart(u, total[1, fibre], nonlin[0, fibre] * (1.0 / CH))
        own[1, pl.ds(i * 4, 4)] = u.reshape(4, 16, 128)
        return carry

    def place_fibre(f, carry):
        for i in range(4):
            place(f * 4 + i, carry)
        keep_edges(1, f, own[1, pl.ds(f * 16, 16)])
        return carry

    lax.fori_loop(0, FIB, place_fibre, 0)

    run_step(2, True)
    finish_near(2)
    finish_far(2, True)
    run_step(3, False)
    finish_near(3)
    finish_far(3, False)

    def store(f):
        group = pl.ds(f * 16, 16)
        return pltpu.make_async_copy(result_buf.at[group], out_hbm.at[group], out_s.at[f])

    def last(f, carry):
        group = pl.ds(f * 16, 16)
        u = own[3, group].reshape(8, 2, 16, 128)
        first, second = unpack_pair(total[3, pl.ds(f // 2 * 2, 2)].reshape(16, 128))
        q = jnp.where(lax.rem(f, 2) == 0, first, second)
        u = rotate_native(u, q, nonlin[1, f] * (1.0 / CH))
        result_buf[group] = u.reshape(16, 16, 128)
        store(f).start()
        return carry

    lax.fori_loop(0, FIB, last, 0)

    def drain_halo(f, carry):
        for e in range(4):
            halo_copy(e, 0, f).wait_send()
            halo_copy(e, 1, f).wait_send()
        return carry

    lax.fori_loop(0, FIB, drain_halo, 0)
    for e in range(4):
        for k in range(1, 8):
            near_copy(e, k).wait_send()
        far_copy(e).wait_send()
    for e in (0, 2):
        side_copy(e, 0).wait_send()
        side_copy(e, 1).wait_send()
    for k in range(1, 16):
        item_copy(k).wait_send()
    for f in range(FIB):
        store(f).wait()


def local(field, lit_count, route_fibre, route_slot, dispersion, nonlinearity):
    rows = field.reshape(FIB, LOC, 2, 2, 8, 128).transpose(0, 1, 2, 4, 3, 5).reshape(SEQ, 16, 128)
    wide, twist = tables()
    smem = pl.BlockSpec(memory_space=pltpu.SMEM)
    hbm = pl.BlockSpec(memory_space=pltpu.HBM)
    dma = pltpu.SemaphoreType.DMA
    result = pl.pallas_call(
        kernel,
        out_shape=jax.ShapeDtypeStruct((SEQ, 16, 128), F32),
        in_specs=[smem] * 3 + [hbm] * 5,
        out_specs=hbm,
        scratch_shapes=[
            pltpu.VMEM((10, 256, 256), BF16),
            pltpu.VMEM((2, 16, 128), F32),
            pltpu.VMEM((FIB, 64), jnp.int32),
            pltpu.VMEM((FIB, 64), jnp.int32),
            pltpu.VMEM((SEQ, 16, 128), F32),
            pltpu.VMEM((SEQ, 16, 128), F32),
            pltpu.VMEM((2, FIB * LOC, 16, 128), F32),
            pltpu.VMEM((2, FIB * LOC, 16, 128), F32),
            pltpu.VMEM((4, 2, SEQ, 8, 128), F32),
            pltpu.VMEM((4, SEQ, 16, 128), F32),
            pltpu.VMEM((3, 2, SEQ, 8, 128), F32),
            pltpu.VMEM((4, FIB, 8, 128), F32),
            pltpu.VMEM((4, 8, FIB, 8, 128), F32),
            pltpu.VMEM((4, FIB, 8, 128), F32),
            pltpu.VMEM((4, FIB, 8, 128), F32),
            pltpu.VMEM((4, FIB, 8, 128), F32),
            pltpu.VMEM((4, 2, FIB, 8, 128), F32),
            pltpu.VMEM((2 * WAVE, 4, 16, 128), F32),
            pltpu.VMEM((2 * WAVE, 4, 16, 128), F32),
            pltpu.SMEM((2 * WAVE,), jnp.int32),
            pltpu.SMEM((WAVE,), jnp.int32),
            pltpu.SMEM((WAVE,), jnp.int32),
            dma((5,)), dma((FIB,)),
            dma((4, 2, FIB)), dma((4, 2, FIB)),
            dma((4, 8)), dma((4, 8)),
            dma((4,)), dma((4,)),
            dma((4, 2)), dma((4, 2)),
            dma((WAVE,)), dma((WAVE,)), pltpu.SemaphoreType.REGULAR((2,)),
            pltpu.SemaphoreType.REGULAR((2,)),
        ],
        compiler_params=pltpu.CompilerParams(
            collective_id=0, has_side_effects=True, vmem_limit_bytes=67043328
        ),
        name="propagate",
    )(lit_count, dispersion, nonlinearity, route_fibre, route_slot, rows, wide, twist)
    back = result.reshape(FIB, LOC, 2, 8, 2, 128).transpose(0, 1, 2, 4, 3, 5)
    return back.reshape(FIB, LOC, 2, 2, 1024)


def solution(mesh):
    return jax.shard_map(
        local,
        mesh=mesh,
        in_specs=(P(None, "wave", None, None, "tm"), P(), P(), P(), P(), P()),
        out_specs=P(None, "wave", None, None, "tm"),
        check_vma=False,
    )
```

```python
import functools
import math

import jax
import jax.numpy as jnp
import numpy as np
from jax import lax
from jax.experimental import pallas as pl
from jax.experimental.pallas import tpu as pltpu
from jax.sharding import PartitionSpec as P

CH = 128
FIB = 4
LOC = 8
SEQ = 64
WAVE = 16
TM = 32
MESH = pl.DeviceIdType.MESH
F32 = jnp.float32
BF16 = jnp.bfloat16


def split_table(table):
    high = table.astype(jnp.bfloat16)
    low = (table - high.astype(np.float64)).astype(jnp.bfloat16)
    return high, low


def tables():
    eye = np.eye(8)
    r16 = np.arange(16)
    angle = 2.0 * np.pi * np.outer(r16, r16) / 16.0
    cos_a, sin_a = np.cos(angle), np.sin(angle)
    fwd = np.zeros((2, 16, 16, 2))
    fwd[0, :, :, 0], fwd[0, :, :, 1] = cos_a, sin_a
    fwd[1, :, :, 0], fwd[1, :, :, 1] = -sin_a, cos_a
    native = fwd.reshape(2, 16, 32)
    apart = np.concatenate(
        [
            fwd[:, :, lo:hi].transpose(0, 1, 3, 2).reshape(2, 16, -1)
            for lo, hi in ((0, 4), (4, 12), (12, 16))
        ],
        axis=2,
    )
    fwd_native, fwd_apart = (
        np.einsum("xrq,st->xsrtq", v, eye).reshape(256, 256) for v in (native, apart)
    )
    keep = np.zeros((8, 2, 2, 16))
    kc, ks = cos_a[4:12] / 2048.0, sin_a[4:12] / 2048.0
    keep[:, 0, 0], keep[:, 0, 1] = kc, -ks
    keep[:, 1, 0], keep[:, 1, 1] = ks, kc
    inv_native = np.einsum("apxr,st->sapxtr", keep, eye).reshape(128, 256)
    inv_apart = np.einsum("apxr,st->spaxtr", keep, eye).reshape(128, 256)
    b = np.arange(128)
    angle = 2.0 * np.pi * (np.outer(b, b) % 128) / 128.0
    cos_b, sin_b = np.cos(angle), np.sin(angle)
    col_fwd = np.block([[cos_b, -sin_b], [sin_b, cos_b]])
    col_inv = np.block([[cos_b, sin_b], [-sin_b, cos_b]])
    twist = 2.0 * np.pi * np.outer(r16, b) / 2048.0
    wide = []
    for table in (fwd_native, fwd_apart, col_fwd, col_inv):
        wide.extend(split_table(table))
    for table in (inv_native, inv_apart):
        wide.append(np.concatenate(split_table(table), axis=0))
    twist = np.stack([np.cos(twist), np.sin(twist)]).astype(np.float32)
    return jnp.asarray(np.stack(wide)), jnp.asarray(twist)


def fit(function, terms):
    nodes = np.cos(np.pi * (np.arange(400) + 0.5) / 400) * (np.pi * 1.02)
    square = nodes * nodes
    basis = np.stack([square**k for k in range(terms)], axis=1)
    return [float(v) for v in np.linalg.lstsq(basis, function(nodes), rcond=None)[0]]


SIN_POLY = fit(lambda x: np.sinc(x / np.pi), 7)
COS_POLY = fit(np.cos, 7)
TWO_PI = 2.0 * math.pi
PI_A = float(np.float32(6.28125))
PI_B = float(np.float32(np.round((TWO_PI - PI_A) * 2.0**24) / 2.0**24))
PI_B = float(np.floor((TWO_PI - PI_A) * 2.0**20) / 2.0**20)
PI_C = float(TWO_PI - PI_A - PI_B)


def sin_cos(angle):
    turns = jnp.floor(angle * (1.0 / TWO_PI) + 0.5)
    rest = ((angle - turns * PI_A) - turns * PI_B) - turns * PI_C
    square = rest * rest
    sine = jnp.full_like(square, SIN_POLY[-1])
    for value in SIN_POLY[-2::-1]:
        sine = sine * square + value
    cosine = jnp.full_like(square, COS_POLY[-1])
    for value in COS_POLY[-2::-1]:
        cosine = cosine * square + value
    return sine * rest, cosine


def split(x):
    high = x.astype(BF16)
    low = (x - high.astype(F32)).astype(BF16)
    return high, low


def dot(a, b):
    return jnp.dot(a, b, preferred_element_type=F32)


def left_product(table, data):
    high, low = split(data)
    return dot(table[0][...], high) + (dot(table[1][...], high) + dot(table[0][...], low))


def right_product(data, table):
    high, low = split(data)
    return dot(high, table[0][...]) + (dot(low, table[0][...]) + dot(high, table[1][...]))


def low_rows():
    return lax.broadcasted_iota(jnp.int32, (8, 128), 0) < 4


def even_rows():
    return lax.rem(lax.broadcasted_iota(jnp.int32, (8, 128), 0), 2) == 0


def turn(x, shift):
    return pltpu.roll(x.reshape(-1, 8, 128), shift, 1).reshape(x.shape)


def swap(x):
    t = x.reshape(-1, 8, 128)
    return jnp.where(even_rows()[None], pltpu.roll(t, 7, 1), pltpu.roll(t, 1, 1)).reshape(x.shape)


def unpack_pair(x):
    t = x.reshape(-1, 8, 128)
    even = even_rows()[None]
    first = jnp.where(even, t, pltpu.roll(t, 1, 1)).reshape(x.shape)
    second = jnp.where(even, pltpu.roll(t, 7, 1), t).reshape(x.shape)
    return first, second


def rotate_native(u, total, gain):
    square = u * u
    both = square[:, 0] + square[:, 1]
    phase = gain * (2.0 * total[None] - (both + swap(both)))
    sine, cosine = sin_cos(phase)
    t = sine.reshape(-1, 8, 128)
    signed = jnp.where(even_rows()[None], -t, t).reshape(sine.shape)
    return u * cosine[:, None] + swap(u) * signed[:, None]


def rotate_apart(u, total, gain):
    re, im = u[:, :, :8], u[:, :, 8:]
    square = re * re + im * im
    phase = gain * (2.0 * total[None] - (square[:, 0] + square[:, 1]))
    sine, cosine = sin_cos(phase)
    sine, cosine = sine[:, None], cosine[:, None]
    return jnp.concatenate([re * cosine - im * sine, re * sine + im * cosine], axis=2)


def rotate_edge(u, total, gain):
    square = u * u
    both = square[:, 0] + square[:, 1]
    phase = gain * (2.0 * total[None] - (both + turn(both, 4)))
    sine, cosine = sin_cos(phase)
    signed = jnp.where(low_rows()[None], -sine, sine)
    return u * cosine[:, None] + turn(u, 4) * signed[:, None]


def edges(u):
    re, im = u[..., :8, :], u[..., 8:, :]
    low = low_rows()
    return jnp.where(low, turn(re, 4), im), jnp.where(low, re, turn(im, 4))


def disperse(u, t, fwd, inv, filt_cos, filt_sin):
    eights = u.shape[0] // 8
    rows = u.reshape(eights, 256, 128)
    x = jnp.concatenate([rows[h] for h in range(eights)], axis=1)
    y = left_product(t[fwd], x)
    tc = jnp.broadcast_to(t["twist_cos"][...][None], (8, 16, 128)).reshape(128, 128)
    ts = jnp.broadcast_to(t["twist_sin"][...][None], (8, 16, 128)).reshape(128, 128)
    halves = []
    for h in range(eights):
        re = y[:128, h * 128 : (h + 1) * 128]
        im = y[128:, h * 128 : (h + 1) * 128]
        halves.append(jnp.concatenate([re * tc + im * ts, im * tc - re * ts], axis=1))
    spectrum = right_product(jnp.concatenate(halves, axis=0), t["col_fwd"])
    sr, si = spectrum[:, :128], spectrum[:, 128:]
    channels = eights * 4
    fc = jnp.broadcast_to(filt_cos[:, None], (channels, 2, 16, 128)).reshape(eights * 128, 128)
    fs = jnp.broadcast_to(filt_sin[:, None], (channels, 2, 16, 128)).reshape(eights * 128, 128)
    shaped = jnp.concatenate([sr * fc - si * fs, sr * fs + si * fc], axis=1)
    back = right_product(shaped, t["col_inv"])
    br, bi = back[:, :128], back[:, 128:]
    parts = []
    for h in range(eights):
        re, im = br[h * 128 : (h + 1) * 128], bi[h * 128 : (h + 1) * 128]
        parts.append(jnp.concatenate([re * tc - im * ts, re * ts + im * tc], axis=0))
    out = left_product(t[inv], jnp.concatenate(parts, axis=1))
    return jnp.concatenate([out[:, h * 128 : (h + 1) * 128] for h in range(eights)], axis=0).reshape(
        eights * 8, 16, 128
    )


def kernel(
    lit, disp, nonlin, fibre_hbm, slot_hbm, field_hbm, wide_hbm, twist_hbm,
    out_hbm,
    wide, twist, route_f, route_s, launch, result_buf,
    filt_c, filt_s, halo, own, edge, pack, near, far, half_sum, total, q_side,
    send_items, recv_items, slot_item, take, take_fibre,
    load_s, out_s,
    halo_ss, halo_rs, near_ss, near_rs, far_ss, far_rs, side_ss, side_rs, item_ss, item_rs, vouch, column,
):
    t = dict(
        fwd_native=(wide.at[0], wide.at[1]), fwd_apart=(wide.at[2], wide.at[3]),
        col_fwd=(wide.at[4], wide.at[5]), col_inv=(wide.at[6], wide.at[7]),
        inv_native=(wide.at[8, pl.ds(0, 128)], wide.at[8, pl.ds(128, 128)]),
        inv_apart=(wide.at[9, pl.ds(0, 128)], wide.at[9, pl.ds(128, 128)]),
        twist_cos=twist.at[0], twist_sin=twist.at[1],
    )
    me = lax.axis_index("wave")
    at = lax.axis_index("tm")
    my_z = me // 8
    my_y = lax.rem(me // 2, 4)
    my_core = lax.rem(me, 2)
    right = lax.rem(at + 1, TM)
    left = lax.rem(at + TM - 1, TM)

    def mate(k):
        kz, ky, kc = k // 8, (k // 2) % 4, k % 2
        return lax.rem(my_z + kz, 2) * 8 + lax.rem(my_y + ky, 4) * 2 + lax.rem(my_core + kc, 2)

    q_right = (lax.rem(me + 8 * (at // (TM - 1)), WAVE), right)
    q_left = (lax.rem(me + 8 * ((TM - 1 - at) // (TM - 1)), WAVE), left)
    d_right, d_left = (me, right), (me, left)

    barrier = pltpu.get_barrier_semaphore()
    upper = at // 16
    z_up = (lax.rem(me + 8 * upper, WAVE), lax.rem(at + 16, TM))
    z_down = (lax.rem(me + 8 * (1 - upper), WAVE), lax.rem(at + 16, TM))
    for k in range(1, 8):
        pl.semaphore_signal(barrier, inc=1, device_id=(mate(k), at), device_id_type=MESH)
    my_high = my_z * 8 + at // 4

    def along_z(step):
        high = lax.rem(my_high + step + 16, 16)
        return (lax.div(high, 8) * 8 + lax.rem(me, 8), lax.rem(high, 8) * 4 + lax.rem(at, 4))

    first_round = [along_z(step) for step in (-5, 5)]
    second_round = [along_z(step) for step in (-2, -1, 1, 2, 3)]
    answers = [along_z(-3)]
    for target in (d_right, d_left, q_right, q_left, z_up, z_down, *first_round, *second_round, *answers):
        pl.semaphore_signal(barrier, inc=1, device_id=target, device_id_type=MESH)
    loads = [
        pltpu.make_async_copy(src, dst, load_s.at[i])
        for i, (src, dst) in enumerate(
            ((field_hbm, launch), (wide_hbm, wide), (twist_hbm, twist), (fibre_hbm, route_f), (slot_hbm, route_s))
        )
    ]
    for load in loads:
        load.start()

    r_i = lax.broadcasted_iota(jnp.int32, (16, 128), 0)
    m_i = lax.broadcasted_iota(jnp.int32, (16, 128), 1)
    k_i = r_i + 16 * m_i
    omega = jnp.where(k_i < 1024, k_i, k_i - 2048).astype(F32) * (2.0 * math.pi / 2048.0)

    def fill_tables(span):
        def fill(i, carry):
            channel = (me * LOC + lax.rem(i, LOC)).astype(F32)
            offset = (math.pi / 2.0) * (2.0 * channel + 1.0 - CH) / CH
            theta = disp[span, i // LOC] * (omega * omega + 2.0 * omega * offset)
            sine, cosine = sin_cos(theta)
            filt_s[span, i] = sine
            filt_c[span, i] = cosine
            return carry

        lax.fori_loop(0, FIB * LOC, fill, 0)

    def plan_switch():
        fibre_of = lax.broadcasted_iota(jnp.int32, (FIB, 64), 0)
        block_of = lax.broadcasted_iota(jnp.int32, (FIB, 64), 1)
        group_of = block_of // 4
        slot = route_s[...]
        target = slot // 4
        landing = route_f[...] * 4 + slot % 4
        key = landing * 16 + fibre_of * 4 + block_of % 4
        mine = group_of == me
        for k in range(16):
            here = mine & (target == mate(k))
            low = jnp.min(jnp.where(here, key, 4095))
            high = jnp.max(jnp.where(here, key, 0))
            slot_item[2 * k] = lax.rem(low, 16)
            slot_item[2 * k + 1] = lax.rem(high, 16)
        code = group_of * 4 + fibre_of
        groups = []
        for i in range(16):
            value = jnp.sum(jnp.where((target == me) & (landing == i), code, 0))
            group = lax.rem(value // 4, WAVE)
            before = jnp.int32(0)
            for other in groups:
                before = before + jnp.where(other == group, 1, 0)
            groups.append(group)
            kz = lax.rem(my_z - group // 8 + 2, 2)
            ky = lax.rem(my_y - lax.rem(group // 2, 4) + 4, 4)
            kc = lax.rem(my_core - lax.rem(group, 2) + 2, 2)
            take[i] = (kz * 8 + ky * 2 + kc) * 2 + jnp.minimum(before, 1)
            take_fibre[i] = lax.rem(value, 4)

    fill_tables(0)
    for load in loads:
        load.wait()
    pl.semaphore_wait(barrier, 21)
    pl.semaphore_signal(vouch.at[0], inc=1, device_id=z_up, device_id_type=MESH)

    def halo_copy(e, side, f):
        group = pl.ds(f * 16, 16)
        if e == 0:
            src = launch.at[group, pl.ds(8, 8) if side == 0 else pl.ds(0, 8)]
        else:
            src = edge.at[e - 1, side, group]
        return pltpu.make_async_remote_copy(
            src_ref=src,
            dst_ref=halo.at[e, side, group],
            send_sem=halo_ss.at[e, side, f],
            recv_sem=halo_rs.at[e, side, f],
            device_id=d_right if side == 0 else d_left,
            device_id_type=MESH,
        )

    def near_copy(e, h, k):
        half = pl.ds(2 * h, 2)
        return pltpu.make_async_remote_copy(
            src_ref=pack.at[e, half], dst_ref=near.at[e, k, half], send_sem=near_ss.at[e, h, k],
            recv_sem=near_rs.at[e, h, k], device_id=(mate(k), at), device_id_type=MESH,
        )

    def far_copy(e, h):
        half = pl.ds(2 * h, 2)
        return pltpu.make_async_remote_copy(
            src_ref=half_sum.at[e, half], dst_ref=far.at[e, half], send_sem=far_ss.at[e, h],
            recv_sem=far_rs.at[e, h], device_id=(mate(8), at), device_id_type=MESH,
        )

    def side_copy(e, side):
        return pltpu.make_async_remote_copy(
            src_ref=total.at[e], dst_ref=q_side.at[e, side], send_sem=side_ss.at[e, side],
            recv_sem=side_rs.at[e, side], device_id=q_right if side == 0 else q_left,
            device_id_type=MESH,
        )

    def item_copy(k):
        return pltpu.make_async_remote_copy(
            src_ref=send_items.at[pl.ds(2 * k, 2)], dst_ref=recv_items.at[pl.ds(2 * k, 2)],
            send_sem=item_ss.at[k], recv_sem=item_rs.at[k], device_id=(mate(k), at),
            device_id_type=MESH,
        )

    def keep_edges(e, f, u):
        group = pl.ds(f * 16, 16)
        edge[e, 0, group], edge[e, 1, group] = edges(u)
        halo_copy(e + 1, 0, f).start()
        halo_copy(e + 1, 1, f).start()

    def run_step(e, send_halo):
        span = e // 2

        def fetch(f):
            halo_copy(e, 0, f).wait_recv()
            halo_copy(e, 1, f).wait_recv()
            group = pl.ds(f * 16, 16)
            middle = launch[group] if e == 0 else own[e - 1, group]
            u = jnp.concatenate([halo[e, 0, group], middle, halo[e, 1, group]], axis=1)
            if e == 0:
                channel = me * LOC + lax.broadcasted_iota(jnp.int32, (16, 1, 128), 0) // 2
                u = jnp.where(channel < lit[f], u, 0.0)
            return u

        def turned(rule, part, f, q):
            gain = nonlin[span, f] * (1.0 / CH)
            return rule(part.reshape(8, 2, *part.shape[1:]), q, gain).reshape(part.shape)

        def fetch_turned():
            middle = []
            for f in range(FIB):
                middle.append(turned(rotate_apart, own[e - 1, pl.ds(f * 16, 16)], f, total[e - 1, f]))
            side_copy(e - 1, 0).wait_recv()
            side_copy(e - 1, 1).wait_recv()
            if e == 1:
                pl.semaphore_wait(column.at[0], 2)
                for target in second_round:
                    pl.semaphore_signal(column.at[1], inc=1, device_id=target, device_id_type=MESH)
            low = low_rows()
            parts = []
            for f in range(FIB):
                group = pl.ds(f * 16, 16)
                before, after = q_side[e - 1, 0, f], q_side[e - 1, 1, f]
                halo_copy(e, 0, f).wait_recv()
                halo_copy(e, 1, f).wait_recv()
                parts.append(
                    jnp.concatenate(
                        [
                            turned(rotate_edge, halo[e, 0, group], f, jnp.where(low, turn(before, 4), before)),
                            middle[f],
                            turned(rotate_edge, halo[e, 1, group], f, jnp.where(low, after, turn(after, 4))),
                        ],
                        axis=1,
                    )
                )
            return jnp.concatenate(parts, axis=0)

        def keep(f, result):
            own[e, pl.ds(f * 16, 16)] = result
            if send_halo:
                keep_edges(e, f, result)
            both = jnp.sum(result * result, axis=0)
            return both[:8] + both[8:] if e < 3 else both + swap(both)

        fwd = "fwd_native" if e == 0 else "fwd_apart"
        inv = "inv_native" if e == 3 else "inv_apart"
        if e in (1, 3):
            result = disperse(fetch_turned(), t, fwd, inv, filt_c[span], filt_s[span])
            powers = [keep(f, result[f * 16 : f * 16 + 16]) for f in range(FIB)]
            for f in range(FIB):
                if e == 1:
                    pack[e, f] = powers[f]
                else:
                    j, h = f // 2 * 2, f % 2
                    rows = slice(h * 8, h * 8 + 8)
                    pack[e, f] = jnp.where(even_rows(), powers[j][rows], powers[j + 1][rows])
        else:

            def body(f, carry):
                table = pl.ds(f * LOC, LOC)
                pack[e, f] = keep(f, disperse(fetch(f), t, fwd, inv, filt_c[span, table], filt_s[span, table]))

                @pl.when(lax.rem(f, 2) == 1)
                def _():
                    for k in range(1, 8):
                        near_copy(e, lax.div(f, 2), k).start()

                return carry

            lax.fori_loop(0, FIB, body, 0)
        if e in (1, 3):
            for h in range(2):
                for k in range(1, 8):
                    near_copy(e, h, k).start()

    def finish_near(e):
        for h in range(2):
            half = pl.ds(2 * h, 2)
            acc = pack[e, half]
            for k in range(1, 8):
                near_copy(e, h, k).wait_recv()
                acc = acc + near[e, k, half]
            half_sum[e, half] = acc
            far_copy(e, h).start()

    def finish_far(e, sides):
        far_copy(e, 0).wait_recv()
        far_copy(e, 1).wait_recv()
        total[e] = half_sum[e] + far[e]
        if e == 0:
            for target in first_round:
                pl.semaphore_signal(column.at[0], inc=1, device_id=target, device_id_type=MESH)
        if sides:
            side_copy(e, 0).start()
            side_copy(e, 1).start()

    def start_halo(f, carry):
        halo_copy(0, 0, f).start()
        halo_copy(0, 1, f).start()
        return carry

    lax.fori_loop(0, FIB, start_halo, 0)
    fill_tables(1)
    plan_switch()
    pl.semaphore_wait(vouch.at[0], 1)
    pl.semaphore_signal(vouch.at[1], inc=1, device_id=z_up, device_id_type=MESH)
    run_step(0, True)
    pl.semaphore_wait(vouch.at[1], 1)
    finish_near(0)
    finish_far(0, True)
    run_step(1, False)

    def gather(s, carry):
        send_items[s] = own[1, pl.ds(slot_item[s] * 4, 4)]
        return carry

    lax.fori_loop(WAVE, 2 * WAVE, gather, 0)
    pl.semaphore_wait(column.at[1], 5)
    for k in (8, 9, 10, 11, 12, 13):
        item_copy(k).start()
    lax.fori_loop(0, WAVE, gather, 0)
    for k in (1, 2, 3, 4, 5, 6, 7):
        item_copy(k).start()
    recv_items[0:2] = send_items[0:2]
    finish_near(1)
    for k in (14, 15):
        item_copy(k).start()
    finish_far(1, False)
    for k in range(1, 16):
        item_copy(k).wait_recv()

    def place(i, carry):
        fibre = take_fibre[i]
        u = recv_items[take[i]].reshape(2, 2, 16, 128)
        u = rotate_apart(u, total[1, fibre], nonlin[0, fibre] * (1.0 / CH))
        own[1, pl.ds(i * 4, 4)] = u.reshape(4, 16, 128)
        return carry

    def place_fibre(f, carry):
        for i in range(4):
            place(f * 4 + i, carry)
        keep_edges(1, f, own[1, pl.ds(f * 16, 16)])
        return carry

    lax.fori_loop(0, FIB, place_fibre, 0)

    run_step(2, True)
    finish_near(2)
    finish_far(2, True)
    run_step(3, False)
    finish_near(3)

    def drain_halo(f, carry):
        for e in range(4):
            halo_copy(e, 0, f).wait_send()
            halo_copy(e, 1, f).wait_send()
        return carry

    lax.fori_loop(0, FIB, drain_halo, 0)
    for e in range(3):
        for h in range(2):
            for k in range(1, 8):
                near_copy(e, h, k).wait_send()
            far_copy(e, h).wait_send()
    for e in (0, 2):
        side_copy(e, 0).wait_send()
        side_copy(e, 1).wait_send()
    for k in range(1, 16):
        item_copy(k).wait_send()
    finish_far(3, False)

    def store(f):
        group = pl.ds(f * 16, 16)
        return pltpu.make_async_copy(result_buf.at[group], out_hbm.at[group], out_s.at[f])

    def last(f, carry):
        group = pl.ds(f * 16, 16)
        u = own[3, group].reshape(8, 2, 16, 128)
        first, second = unpack_pair(total[3, pl.ds(f // 2 * 2, 2)].reshape(16, 128))
        q = jnp.where(lax.rem(f, 2) == 0, first, second)
        u = rotate_native(u, q, nonlin[1, f] * (1.0 / CH))
        result_buf[group] = u.reshape(16, 16, 128)
        store(f).start()
        return carry

    lax.fori_loop(0, FIB, last, 0)

    for h in range(2):
        for k in range(1, 8):
            near_copy(3, h, k).wait_send()
        far_copy(3, h).wait_send()
    for f in range(FIB):
        store(f).wait()


def local(field, lit_count, route_fibre, route_slot, dispersion, nonlinearity):
    rows = field.reshape(FIB, LOC, 2, 2, 8, 128).transpose(0, 1, 2, 4, 3, 5).reshape(SEQ, 16, 128)
    wide, twist = tables()
    smem = pl.BlockSpec(memory_space=pltpu.SMEM)
    hbm = pl.BlockSpec(memory_space=pltpu.HBM)
    dma = pltpu.SemaphoreType.DMA
    result = pl.pallas_call(
        kernel,
        out_shape=jax.ShapeDtypeStruct((SEQ, 16, 128), F32),
        in_specs=[smem] * 3 + [hbm] * 5,
        out_specs=hbm,
        scratch_shapes=[
            pltpu.VMEM((10, 256, 256), BF16),
            pltpu.VMEM((2, 16, 128), F32),
            pltpu.VMEM((FIB, 64), jnp.int32),
            pltpu.VMEM((FIB, 64), jnp.int32),
            pltpu.VMEM((SEQ, 16, 128), F32),
            pltpu.VMEM((SEQ, 16, 128), F32),
            pltpu.VMEM((2, FIB * LOC, 16, 128), F32),
            pltpu.VMEM((2, FIB * LOC, 16, 128), F32),
            pltpu.VMEM((4, 2, SEQ, 8, 128), F32),
            pltpu.VMEM((4, SEQ, 16, 128), F32),
            pltpu.VMEM((3, 2, SEQ, 8, 128), F32),
            pltpu.VMEM((4, FIB, 8, 128), F32),
            pltpu.VMEM((4, 8, FIB, 8, 128), F32),
            pltpu.VMEM((4, FIB, 8, 128), F32),
            pltpu.VMEM((4, FIB, 8, 128), F32),
            pltpu.VMEM((4, FIB, 8, 128), F32),
            pltpu.VMEM((4, 2, FIB, 8, 128), F32),
            pltpu.VMEM((2 * WAVE, 4, 16, 128), F32),
            pltpu.VMEM((2 * WAVE, 4, 16, 128), F32),
            pltpu.SMEM((2 * WAVE,), jnp.int32),
            pltpu.SMEM((WAVE,), jnp.int32),
            pltpu.SMEM((WAVE,), jnp.int32),
            dma((5,)), dma((FIB,)),
            dma((4, 2, FIB)), dma((4, 2, FIB)),
            dma((4, 2, 8)), dma((4, 2, 8)),
            dma((4, 2)), dma((4, 2)),
            dma((4, 2)), dma((4, 2)),
            dma((WAVE,)), dma((WAVE,)), pltpu.SemaphoreType.REGULAR((2,)),
            pltpu.SemaphoreType.REGULAR((2,)),
        ],
        compiler_params=pltpu.CompilerParams(
            collective_id=0, has_side_effects=True, vmem_limit_bytes=67043328
        ),
        name="propagate",
    )(lit_count, dispersion, nonlinearity, route_fibre, route_slot, rows, wide, twist)
    back = result.reshape(FIB, LOC, 2, 8, 2, 128).transpose(0, 1, 2, 4, 3, 5)
    return back.reshape(FIB, LOC, 2, 2, 1024)


def solution(mesh):
    return jax.shard_map(
        local,
        mesh=mesh,
        in_specs=(P(None, "wave", None, None, "tm"), P(), P(), P(), P(), P()),
        out_specs=P(None, "wave", None, None, "tm"),
        check_vma=False,
    )
```

```python
import functools
import math

import jax
import jax.numpy as jnp
import numpy as np
from jax import lax
from jax.experimental import pallas as pl
from jax.experimental.pallas import tpu as pltpu
from jax.sharding import PartitionSpec as P

CH = 128
FIB = 4
LOC = 8
SEQ = 64
WAVE = 16
TM = 32
MESH = pl.DeviceIdType.MESH
F32 = jnp.float32
BF16 = jnp.bfloat16


def split_table(table):
    high = table.astype(jnp.bfloat16)
    low = (table - high.astype(np.float64)).astype(jnp.bfloat16)
    return high, low


def tables():
    eye = np.eye(8)
    r16 = np.arange(16)
    angle = 2.0 * np.pi * np.outer(r16, r16) / 16.0
    cos_a, sin_a = np.cos(angle), np.sin(angle)
    fwd = np.zeros((2, 16, 16, 2))
    fwd[0, :, :, 0], fwd[0, :, :, 1] = cos_a, sin_a
    fwd[1, :, :, 0], fwd[1, :, :, 1] = -sin_a, cos_a
    native = fwd.reshape(2, 16, 32)
    apart = np.concatenate(
        [
            fwd[:, :, lo:hi].transpose(0, 1, 3, 2).reshape(2, 16, -1)
            for lo, hi in ((0, 4), (4, 12), (12, 16))
        ],
        axis=2,
    )
    fwd_native, fwd_apart = (
        np.einsum("xrq,st->xsrtq", v, eye).reshape(256, 256) for v in (native, apart)
    )
    keep = np.zeros((8, 2, 2, 16))
    kc, ks = cos_a[4:12] / 2048.0, sin_a[4:12] / 2048.0
    keep[:, 0, 0], keep[:, 0, 1] = kc, -ks
    keep[:, 1, 0], keep[:, 1, 1] = ks, kc
    inv_native = np.einsum("apxr,st->sapxtr", keep, eye).reshape(128, 256)
    inv_apart = np.einsum("apxr,st->spaxtr", keep, eye).reshape(128, 256)
    b = np.arange(128)
    angle = 2.0 * np.pi * (np.outer(b, b) % 128) / 128.0
    cos_b, sin_b = np.cos(angle), np.sin(angle)
    col_fwd = np.block([[cos_b, -sin_b], [sin_b, cos_b]])
    col_inv = np.block([[cos_b, sin_b], [-sin_b, cos_b]])
    twist = 2.0 * np.pi * np.outer(r16, b) / 2048.0
    wide = []
    for table in (fwd_native, fwd_apart, col_fwd, col_inv):
        wide.extend(split_table(table))
    for table in (inv_native, inv_apart):
        wide.append(np.concatenate(split_table(table), axis=0))
    twist = np.stack([np.cos(twist), np.sin(twist)]).astype(np.float32)
    return jnp.asarray(np.stack(wide)), jnp.asarray(twist)


def fit(function, terms):
    nodes = np.cos(np.pi * (np.arange(400) + 0.5) / 400) * (np.pi * 1.02)
    square = nodes * nodes
    basis = np.stack([square**k for k in range(terms)], axis=1)
    return [float(v) for v in np.linalg.lstsq(basis, function(nodes), rcond=None)[0]]


SIN_POLY = fit(lambda x: np.sinc(x / np.pi), 7)
COS_POLY = fit(np.cos, 7)
TWO_PI = 2.0 * math.pi
PI_A = float(np.float32(6.28125))
PI_B = float(np.float32(np.round((TWO_PI - PI_A) * 2.0**24) / 2.0**24))
PI_B = float(np.floor((TWO_PI - PI_A) * 2.0**20) / 2.0**20)
PI_C = float(TWO_PI - PI_A - PI_B)


def sin_cos(angle):
    turns = jnp.floor(angle * (1.0 / TWO_PI) + 0.5)
    rest = ((angle - turns * PI_A) - turns * PI_B) - turns * PI_C
    square = rest * rest
    sine = jnp.full_like(square, SIN_POLY[-1])
    for value in SIN_POLY[-2::-1]:
        sine = sine * square + value
    cosine = jnp.full_like(square, COS_POLY[-1])
    for value in COS_POLY[-2::-1]:
        cosine = cosine * square + value
    return sine * rest, cosine


def split(x):
    high = x.astype(BF16)
    low = (x - high.astype(F32)).astype(BF16)
    return high, low


def dot(a, b):
    return jnp.dot(a, b, preferred_element_type=F32)


def left_product(table, data):
    high, low = split(data)
    return dot(table[0][...], high) + (dot(table[1][...], high) + dot(table[0][...], low))


def right_product(data, table):
    high, low = split(data)
    return dot(high, table[0][...]) + (dot(low, table[0][...]) + dot(high, table[1][...]))


def low_rows():
    return lax.broadcasted_iota(jnp.int32, (8, 128), 0) < 4


def even_rows():
    return lax.rem(lax.broadcasted_iota(jnp.int32, (8, 128), 0), 2) == 0


def turn(x, shift):
    return pltpu.roll(x.reshape(-1, 8, 128), shift, 1).reshape(x.shape)


def swap(x):
    t = x.reshape(-1, 8, 128)
    return jnp.where(even_rows()[None], pltpu.roll(t, 7, 1), pltpu.roll(t, 1, 1)).reshape(x.shape)


def unpack_pair(x):
    t = x.reshape(-1, 8, 128)
    even = even_rows()[None]
    first = jnp.where(even, t, pltpu.roll(t, 1, 1)).reshape(x.shape)
    second = jnp.where(even, pltpu.roll(t, 7, 1), t).reshape(x.shape)
    return first, second


def rotate_native(u, total, gain):
    square = u * u
    both = square[:, 0] + square[:, 1]
    phase = gain * (2.0 * total[None] - (both + swap(both)))
    sine, cosine = sin_cos(phase)
    t = sine.reshape(-1, 8, 128)
    signed = jnp.where(even_rows()[None], -t, t).reshape(sine.shape)
    return u * cosine[:, None] + swap(u) * signed[:, None]


def rotate_apart(u, total, gain):
    re, im = u[:, :, :8], u[:, :, 8:]
    square = re * re + im * im
    phase = gain * (2.0 * total[None] - (square[:, 0] + square[:, 1]))
    sine, cosine = sin_cos(phase)
    sine, cosine = sine[:, None], cosine[:, None]
    return jnp.concatenate([re * cosine - im * sine, re * sine + im * cosine], axis=2)


def rotate_edge(u, total, gain):
    square = u * u
    both = square[:, 0] + square[:, 1]
    phase = gain * (2.0 * total[None] - (both + turn(both, 4)))
    sine, cosine = sin_cos(phase)
    signed = jnp.where(low_rows()[None], -sine, sine)
    return u * cosine[:, None] + turn(u, 4) * signed[:, None]


def edges(u):
    re, im = u[..., :8, :], u[..., 8:, :]
    low = low_rows()
    return jnp.where(low, turn(re, 4), im), jnp.where(low, re, turn(im, 4))


def disperse(u, t, fwd, inv, filt_cos, filt_sin):
    eights = u.shape[0] // 8
    rows = u.reshape(eights, 256, 128)
    x = jnp.concatenate([rows[h] for h in range(eights)], axis=1)
    y = left_product(t[fwd], x)
    tc = jnp.broadcast_to(t["twist_cos"][...][None], (8, 16, 128)).reshape(128, 128)
    ts = jnp.broadcast_to(t["twist_sin"][...][None], (8, 16, 128)).reshape(128, 128)
    halves = []
    for h in range(eights):
        re = y[:128, h * 128 : (h + 1) * 128]
        im = y[128:, h * 128 : (h + 1) * 128]
        halves.append(jnp.concatenate([re * tc + im * ts, im * tc - re * ts], axis=1))
    spectrum = right_product(jnp.concatenate(halves, axis=0), t["col_fwd"])
    sr, si = spectrum[:, :128], spectrum[:, 128:]
    channels = eights * 4
    fc = jnp.broadcast_to(filt_cos[:, None], (channels, 2, 16, 128)).reshape(eights * 128, 128)
    fs = jnp.broadcast_to(filt_sin[:, None], (channels, 2, 16, 128)).reshape(eights * 128, 128)
    shaped = jnp.concatenate([sr * fc - si * fs, sr * fs + si * fc], axis=1)
    back = right_product(shaped, t["col_inv"])
    br, bi = back[:, :128], back[:, 128:]
    parts = []
    for h in range(eights):
        re, im = br[h * 128 : (h + 1) * 128], bi[h * 128 : (h + 1) * 128]
        parts.append(jnp.concatenate([re * tc - im * ts, re * ts + im * tc], axis=0))
    out = left_product(t[inv], jnp.concatenate(parts, axis=1))
    return jnp.concatenate([out[:, h * 128 : (h + 1) * 128] for h in range(eights)], axis=0).reshape(
        eights * 8, 16, 128
    )


def kernel(
    lit, disp, nonlin, fibre_hbm, slot_hbm, field_hbm, wide_hbm, twist_hbm,
    out_hbm,
    wide, twist, route_f, route_s, launch, result_buf,
    filt_c, filt_s, halo, own, edge, pack, near, far, half_sum, total, q_side,
    send_items, recv_items, slot_item, take, take_fibre,
    load_s, out_s,
    halo_ss, halo_rs, near_ss, near_rs, far_ss, far_rs, side_ss, side_rs, item_ss, item_rs, vouch, column,
):
    t = dict(
        fwd_native=(wide.at[0], wide.at[1]), fwd_apart=(wide.at[2], wide.at[3]),
        col_fwd=(wide.at[4], wide.at[5]), col_inv=(wide.at[6], wide.at[7]),
        inv_native=(wide.at[8, pl.ds(0, 128)], wide.at[8, pl.ds(128, 128)]),
        inv_apart=(wide.at[9, pl.ds(0, 128)], wide.at[9, pl.ds(128, 128)]),
        twist_cos=twist.at[0], twist_sin=twist.at[1],
    )
    me = lax.axis_index("wave")
    at = lax.axis_index("tm")
    my_z = me // 8
    my_y = lax.rem(me // 2, 4)
    my_core = lax.rem(me, 2)
    right = lax.rem(at + 1, TM)
    left = lax.rem(at + TM - 1, TM)

    def mate(k):
        kz, ky, kc = k // 8, (k // 2) % 4, k % 2
        return lax.rem(my_z + kz, 2) * 8 + lax.rem(my_y + ky, 4) * 2 + lax.rem(my_core + kc, 2)

    q_right = (lax.rem(me + 8 * (at // (TM - 1)), WAVE), right)
    q_left = (lax.rem(me + 8 * ((TM - 1 - at) // (TM - 1)), WAVE), left)
    d_right, d_left = (me, right), (me, left)

    barrier = pltpu.get_barrier_semaphore()
    upper = at // 16
    z_up = (lax.rem(me + 8 * upper, WAVE), lax.rem(at + 16, TM))
    z_down = (lax.rem(me + 8 * (1 - upper), WAVE), lax.rem(at + 16, TM))
    for k in range(1, 8):
        pl.semaphore_signal(barrier, inc=1, device_id=(mate(k), at), device_id_type=MESH)
    my_high = my_z * 8 + at // 4

    def along_z(step):
        high = lax.rem(my_high + step + 16, 16)
        return (lax.div(high, 8) * 8 + lax.rem(me, 8), lax.rem(high, 8) * 4 + lax.rem(at, 4))

    first_round = [along_z(step) for step in (-5, 5)]
    second_round = [along_z(step) for step in (-2, -1, 1, 2, 3)]
    answers = [along_z(-3)]
    for target in (d_right, d_left, q_right, q_left, z_up, z_down, *first_round, *second_round, *answers):
        pl.semaphore_signal(barrier, inc=1, device_id=target, device_id_type=MESH)
    loads = [
        pltpu.make_async_copy(src, dst, load_s.at[i])
        for i, (src, dst) in enumerate(
            ((field_hbm, launch), (wide_hbm, wide), (twist_hbm, twist), (fibre_hbm, route_f), (slot_hbm, route_s))
        )
    ]
    for load in loads:
        load.start()

    r_i = lax.broadcasted_iota(jnp.int32, (16, 128), 0)
    m_i = lax.broadcasted_iota(jnp.int32, (16, 128), 1)
    k_i = r_i + 16 * m_i
    omega = jnp.where(k_i < 1024, k_i, k_i - 2048).astype(F32) * (2.0 * math.pi / 2048.0)

    def fill_tables(span):
        def fill(i, carry):
            channel = (me * LOC + lax.rem(i, LOC)).astype(F32)
            offset = (math.pi / 2.0) * (2.0 * channel + 1.0 - CH) / CH
            theta = disp[span, i // LOC] * (omega * omega + 2.0 * omega * offset)
            sine, cosine = sin_cos(theta)
            filt_s[span, i] = sine
            filt_c[span, i] = cosine
            return carry

        lax.fori_loop(0, FIB * LOC, fill, 0)

    def plan_switch():
        fibre_of = lax.broadcasted_iota(jnp.int32, (FIB, 64), 0)
        block_of = lax.broadcasted_iota(jnp.int32, (FIB, 64), 1)
        group_of = block_of // 4
        slot = route_s[...]
        target = slot // 4
        landing = route_f[...] * 4 + slot % 4
        key = landing * 16 + fibre_of * 4 + block_of % 4
        mine = group_of == me
        for k in range(16):
            here = mine & (target == mate(k))
            low = jnp.min(jnp.where(here, key, 4095))
            high = jnp.max(jnp.where(here, key, 0))
            slot_item[2 * k] = lax.rem(low, 16)
            slot_item[2 * k + 1] = lax.rem(high, 16)
        code = group_of * 4 + fibre_of
        groups = []
        for i in range(16):
            value = jnp.sum(jnp.where((target == me) & (landing == i), code, 0))
            group = lax.rem(value // 4, WAVE)
            before = jnp.int32(0)
            for other in groups:
                before = before + jnp.where(other == group, 1, 0)
            groups.append(group)
            kz = lax.rem(my_z - group // 8 + 2, 2)
            ky = lax.rem(my_y - lax.rem(group // 2, 4) + 4, 4)
            kc = lax.rem(my_core - lax.rem(group, 2) + 2, 2)
            take[i] = (kz * 8 + ky * 2 + kc) * 2 + jnp.minimum(before, 1)
            take_fibre[i] = lax.rem(value, 4)

    fill_tables(0)
    for load in loads:
        load.wait()
    pl.semaphore_wait(barrier, 21)
    pl.semaphore_signal(vouch.at[0], inc=1, device_id=z_up, device_id_type=MESH)

    def halo_copy(e, side, f):
        group = pl.ds(f * 16, 16)
        if e == 0:
            src = launch.at[group, pl.ds(8, 8) if side == 0 else pl.ds(0, 8)]
        else:
            src = edge.at[e - 1, side, group]
        return pltpu.make_async_remote_copy(
            src_ref=src,
            dst_ref=halo.at[e, side, group],
            send_sem=halo_ss.at[e, side, f],
            recv_sem=halo_rs.at[e, side, f],
            device_id=d_right if side == 0 else d_left,
            device_id_type=MESH,
        )

    def near_copy(e, k):
        return pltpu.make_async_remote_copy(
            src_ref=pack.at[e], dst_ref=near.at[e, k], send_sem=near_ss.at[e, k],
            recv_sem=near_rs.at[e, k], device_id=(mate(k), at), device_id_type=MESH,
        )

    def far_copy(e):
        return pltpu.make_async_remote_copy(
            src_ref=half_sum.at[e], dst_ref=far.at[e], send_sem=far_ss.at[e],
            recv_sem=far_rs.at[e], device_id=(mate(8), at), device_id_type=MESH,
        )

    def side_copy(e, side):
        return pltpu.make_async_remote_copy(
            src_ref=total.at[e], dst_ref=q_side.at[e, side], send_sem=side_ss.at[e, side],
            recv_sem=side_rs.at[e, side], device_id=q_right if side == 0 else q_left,
            device_id_type=MESH,
        )

    def item_copy(k):
        return pltpu.make_async_remote_copy(
            src_ref=send_items.at[pl.ds(2 * k, 2)], dst_ref=recv_items.at[pl.ds(2 * k, 2)],
            send_sem=item_ss.at[k], recv_sem=item_rs.at[k], device_id=(mate(k), at),
            device_id_type=MESH,
        )

    def keep_edges(e, f, u):
        group = pl.ds(f * 16, 16)
        edge[e, 0, group], edge[e, 1, group] = edges(u)
        halo_copy(e + 1, 0, f).start()
        halo_copy(e + 1, 1, f).start()

    def run_step(e, send_halo):
        span = e // 2

        def fetch(f):
            halo_copy(e, 0, f).wait_recv()
            halo_copy(e, 1, f).wait_recv()
            group = pl.ds(f * 16, 16)
            middle = launch[group] if e == 0 else own[e - 1, group]
            u = jnp.concatenate([halo[e, 0, group], middle, halo[e, 1, group]], axis=1)
            if e == 0:
                channel = me * LOC + lax.broadcasted_iota(jnp.int32, (16, 1, 128), 0) // 2
                u = jnp.where(channel < lit[f], u, 0.0)
            return u

        def turned(rule, part, f, q):
            gain = nonlin[span, f] * (1.0 / CH)
            return rule(part.reshape(8, 2, *part.shape[1:]), q, gain).reshape(part.shape)

        def fetch_turned():
            middle = []
            for f in range(FIB):
                middle.append(turned(rotate_apart, own[e - 1, pl.ds(f * 16, 16)], f, total[e - 1, f]))
            side_copy(e - 1, 0).wait_recv()
            side_copy(e - 1, 1).wait_recv()
            if e == 1:
                pl.semaphore_wait(column.at[0], 2)
                for target in second_round:
                    pl.semaphore_signal(column.at[1], inc=1, device_id=target, device_id_type=MESH)
            low = low_rows()
            parts = []
            for f in range(FIB):
                group = pl.ds(f * 16, 16)
                before, after = q_side[e - 1, 0, f], q_side[e - 1, 1, f]
                halo_copy(e, 0, f).wait_recv()
                halo_copy(e, 1, f).wait_recv()
                parts.append(
                    jnp.concatenate(
                        [
                            turned(rotate_edge, halo[e, 0, group], f, jnp.where(low, turn(before, 4), before)),
                            middle[f],
                            turned(rotate_edge, halo[e, 1, group], f, jnp.where(low, after, turn(after, 4))),
                        ],
                        axis=1,
                    )
                )
            return jnp.concatenate(parts, axis=0)

        def keep(f, result):
            own[e, pl.ds(f * 16, 16)] = result
            if send_halo:
                keep_edges(e, f, result)
            both = jnp.sum(result * result, axis=0)
            return both[:8] + both[8:] if e < 3 else both + swap(both)

        fwd = "fwd_native" if e == 0 else "fwd_apart"
        inv = "inv_native" if e == 3 else "inv_apart"
        if e in (1, 3):
            result = disperse(fetch_turned(), t, fwd, inv, filt_c[span], filt_s[span])
            powers = [keep(f, result[f * 16 : f * 16 + 16]) for f in range(FIB)]
            for f in range(FIB):
                if e == 1:
                    pack[e, f] = powers[f]
                else:
                    j, h = f // 2 * 2, f % 2
                    rows = slice(h * 8, h * 8 + 8)
                    pack[e, f] = jnp.where(even_rows(), powers[j][rows], powers[j + 1][rows])
        else:

            def body(f, carry):
                table = pl.ds(f * LOC, LOC)
                pack[e, f] = keep(f, disperse(fetch(f), t, fwd, inv, filt_c[span, table], filt_s[span, table]))
                return carry

            lax.fori_loop(0, FIB, body, 0)
        for k in range(1, 8):
            near_copy(e, k).start()

    def finish_near(e):
        acc = pack[e]
        for k in range(1, 8):
            near_copy(e, k).wait_recv()
            acc = acc + near[e, k]
        half_sum[e] = acc
        far_copy(e).start()

    def finish_far(e, sides):
        far_copy(e).wait_recv()
        total[e] = half_sum[e] + far[e]
        if e == 0:
            for target in first_round:
                pl.semaphore_signal(column.at[0], inc=1, device_id=target, device_id_type=MESH)
        if sides:
            side_copy(e, 0).start()
            side_copy(e, 1).start()

    def start_halo(f, carry):
        halo_copy(0, 0, f).start()
        halo_copy(0, 1, f).start()
        return carry

    lax.fori_loop(0, FIB, start_halo, 0)
    fill_tables(1)
    plan_switch()
    pl.semaphore_wait(vouch.at[0], 1)
    pl.semaphore_signal(vouch.at[1], inc=1, device_id=z_up, device_id_type=MESH)
    run_step(0, True)
    pl.semaphore_wait(vouch.at[1], 1)
    finish_near(0)
    finish_far(0, True)
    run_step(1, False)

    def gather(s, carry):
        send_items[s] = own[1, pl.ds(slot_item[s] * 4, 4)]
        return carry

    lax.fori_loop(WAVE, 2 * WAVE, gather, 0)
    pl.semaphore_wait(column.at[1], 5)
    for k in (14, 12, 10, 8, 15, 13, 11, 9):
        item_copy(k).start()
    lax.fori_loop(0, WAVE, gather, 0)
    for k in (1, 2, 3, 4, 5, 6, 7):
        item_copy(k).start()
    recv_items[0:2] = send_items[0:2]
    finish_near(1)
    finish_far(1, False)
    for k in range(1, 16):
        item_copy(k).wait_recv()

    def place(i, carry):
        fibre = take_fibre[i]
        u = recv_items[take[i]].reshape(2, 2, 16, 128)
        u = rotate_apart(u, total[1, fibre], nonlin[0, fibre] * (1.0 / CH))
        own[1, pl.ds(i * 4, 4)] = u.reshape(4, 16, 128)
        return carry

    def place_fibre(f, carry):
        for i in range(4):
            place(f * 4 + i, carry)
        keep_edges(1, f, own[1, pl.ds(f * 16, 16)])
        return carry

    lax.fori_loop(0, FIB, place_fibre, 0)

    run_step(2, True)
    finish_near(2)
    finish_far(2, True)
    run_step(3, False)
    finish_near(3)

    def drain_halo(f, carry):
        for e in range(4):
            halo_copy(e, 0, f).wait_send()
            halo_copy(e, 1, f).wait_send()
        return carry

    lax.fori_loop(0, FIB, drain_halo, 0)
    for e in range(3):
        for k in range(1, 8):
            near_copy(e, k).wait_send()
        far_copy(e).wait_send()
    for e in (0, 2):
        side_copy(e, 0).wait_send()
        side_copy(e, 1).wait_send()
    for k in range(1, 16):
        item_copy(k).wait_send()
    finish_far(3, False)

    def store(f):
        group = pl.ds(f * 16, 16)
        return pltpu.make_async_copy(result_buf.at[group], out_hbm.at[group], out_s.at[f])

    def last(f, carry):
        group = pl.ds(f * 16, 16)
        u = own[3, group].reshape(8, 2, 16, 128)
        first, second = unpack_pair(total[3, pl.ds(f // 2 * 2, 2)].reshape(16, 128))
        q = jnp.where(lax.rem(f, 2) == 0, first, second)
        u = rotate_native(u, q, nonlin[1, f] * (1.0 / CH))
        result_buf[group] = u.reshape(16, 16, 128)
        store(f).start()
        return carry

    lax.fori_loop(0, FIB, last, 0)

    for k in range(1, 8):
        near_copy(3, k).wait_send()
    far_copy(3).wait_send()
    for f in range(FIB):
        store(f).wait()


def local(field, lit_count, route_fibre, route_slot, dispersion, nonlinearity):
    rows = field.reshape(FIB, LOC, 2, 2, 8, 128).transpose(0, 1, 2, 4, 3, 5).reshape(SEQ, 16, 128)
    wide, twist = tables()
    smem = pl.BlockSpec(memory_space=pltpu.SMEM)
    hbm = pl.BlockSpec(memory_space=pltpu.HBM)
    dma = pltpu.SemaphoreType.DMA
    result = pl.pallas_call(
        kernel,
        out_shape=jax.ShapeDtypeStruct((SEQ, 16, 128), F32),
        in_specs=[smem] * 3 + [hbm] * 5,
        out_specs=hbm,
        scratch_shapes=[
            pltpu.VMEM((10, 256, 256), BF16),
            pltpu.VMEM((2, 16, 128), F32),
            pltpu.VMEM((FIB, 64), jnp.int32),
            pltpu.VMEM((FIB, 64), jnp.int32),
            pltpu.VMEM((SEQ, 16, 128), F32),
            pltpu.VMEM((SEQ, 16, 128), F32),
            pltpu.VMEM((2, FIB * LOC, 16, 128), F32),
            pltpu.VMEM((2, FIB * LOC, 16, 128), F32),
            pltpu.VMEM((4, 2, SEQ, 8, 128), F32),
            pltpu.VMEM((4, SEQ, 16, 128), F32),
            pltpu.VMEM((3, 2, SEQ, 8, 128), F32),
            pltpu.VMEM((4, FIB, 8, 128), F32),
            pltpu.VMEM((4, 8, FIB, 8, 128), F32),
            pltpu.VMEM((4, FIB, 8, 128), F32),
            pltpu.VMEM((4, FIB, 8, 128), F32),
            pltpu.VMEM((4, FIB, 8, 128), F32),
            pltpu.VMEM((4, 2, FIB, 8, 128), F32),
            pltpu.VMEM((2 * WAVE, 4, 16, 128), F32),
            pltpu.VMEM((2 * WAVE, 4, 16, 128), F32),
            pltpu.SMEM((2 * WAVE,), jnp.int32),
            pltpu.SMEM((WAVE,), jnp.int32),
            pltpu.SMEM((WAVE,), jnp.int32),
            dma((5,)), dma((FIB,)),
            dma((4, 2, FIB)), dma((4, 2, FIB)),
            dma((4, 8)), dma((4, 8)),
            dma((4,)), dma((4,)),
            dma((4, 2)), dma((4, 2)),
            dma((WAVE,)), dma((WAVE,)), pltpu.SemaphoreType.REGULAR((2,)),
            pltpu.SemaphoreType.REGULAR((2,)),
        ],
        compiler_params=pltpu.CompilerParams(
            collective_id=0, has_side_effects=True, vmem_limit_bytes=67043328
        ),
        name="propagate",
    )(lit_count, dispersion, nonlinearity, route_fibre, route_slot, rows, wide, twist)
    back = result.reshape(FIB, LOC, 2, 8, 2, 128).transpose(0, 1, 2, 4, 3, 5)
    return back.reshape(FIB, LOC, 2, 2, 1024)


def solution(mesh):
    return jax.shard_map(
        local,
        mesh=mesh,
        in_specs=(P(None, "wave", None, None, "tm"), P(), P(), P(), P(), P()),
        out_specs=P(None, "wave", None, None, "tm"),
        check_vma=False,
    )
```
